32 devices in a mesh: dp: 8 (over z, x), fsdp: 4 (over y, core).
Axes of the slice: x: 2, y: 2, z: 4, core: 2. Of those that a mesh axis runs over, the one named last changes fastest.
Arguments:
- frames: bfloat16 [32768, 512], P(('dp', 'fsdp')), may hold values from -6 to 6
- cotangent: bfloat16 [32768, 512], P(('dp', 'fsdp')), may hold values from -6 to 6
- lengths: int32 [32, 5], P(('dp', 'fsdp')), may hold values from 1 to 512, 1024 in all within a row
- expand: float32 [2, 512, 2048], P(None, 'fsdp'), may hold values from -0.25 to 0.25
- expand_first: float32 [2, 512, 2048], P(None, 'fsdp'), may hold values from -12 to 12
- expand_second: float32 [2, 512, 2048], P(None, 'fsdp'), may hold values from 6.5536 to 26.2144
- shrink: float32 [2, 2048, 512], P(None, 'fsdp'), may hold values from -0.125 to 0.125
- shrink_first: float32 [2, 2048, 512], P(None, 'fsdp'), may hold values from -32 to 32
- shrink_second: float32 [2, 2048, 512], P(None, 'fsdp'), may hold values from 40.96 to 163.84
- attend: float32 [512, 1536], P('fsdp'), may hold values from -0.25 to 0.25
- attend_first: float32 [512, 1536], P('fsdp'), may hold values from -12 to 12
- attend_second: float32 [512, 1536], P('fsdp'), may hold values from 6.5536 to 26.2144
- heads_out: float32 [512, 512], P('fsdp'), may hold values from -0.75 to 0.75
- heads_out_first: float32 [512, 512], P('fsdp'), may hold values from -24 to 24
- heads_out_second: float32 [512, 512], P('fsdp'), may hold values from 26.2144 to 104.8576
- pointwise: float32 [512, 1024], P('fsdp'), may hold values from -0.25 to 0.25
- pointwise_first: float32 [512, 1024], P('fsdp'), may hold values from -12 to 12
- pointwise_second: float32 [512, 1024], P('fsdp'), may hold values from 6.5536 to 26.2144
- pointwise_out: float32 [512, 512], P('fsdp'), may hold values from -0.375 to 0.375
- pointwise_out_first: float32 [512, 512], P('fsdp'), may hold values from -32 to 32
- pointwise_out_second: float32 [512, 512], P('fsdp'), may hold values from 58.9824 to 235.9296
- depthwise: float32 [32, 512], P(None, 'fsdp'), may hold values from -1 to 1
- depthwise_first: float32 [32, 512], P(None, 'fsdp'), may hold values from -32 to 32
- depthwise_second: float32 [32, 512], P(None, 'fsdp'), may hold values from 58.9824 to 235.9296
- norm_table: float32 [12, 512], P(None, 'fsdp'), may hold values from -0.8 to 1.6
- norm_table_first: float32 [12, 512], P(None, 'fsdp'), may hold values from -64 to 64
- norm_table_second: float32 [12, 512], P(None, 'fsdp'), may hold values from 163.84 to 655.36
Outputs:
- layer_output: bfloat16 [32768, 512], P(('dp', 'fsdp'))
- frames_grad: float32 [32768, 512], P(('dp', 'fsdp'))
- expand_updated: float32 [2, 512, 2048], P(None, 'fsdp')
- expand_first_updated: float32 [2, 512, 2048], P(None, 'fsdp')
- expand_second_updated: float32 [2, 512, 2048], P(None, 'fsdp')
- shrink_updated: float32 [2, 2048, 512], P(None, 'fsdp')
- shrink_first_updated: float32 [2, 2048, 512], P(None, 'fsdp')
- shrink_second_updated: float32 [2, 2048, 512], P(None, 'fsdp')
- attend_updated: float32 [512, 1536], P('fsdp')
- attend_first_updated: float32 [512, 1536], P('fsdp')
- attend_second_updated: float32 [512, 1536], P('fsdp')
- heads_out_updated: float32 [512, 512], P('fsdp')
- heads_out_first_updated: float32 [512, 512], P('fsdp')
- heads_out_second_updated: float32 [512, 512], P('fsdp')
- pointwise_updated: float32 [512, 1024], P('fsdp')
- pointwise_first_updated: float32 [512, 1024], P('fsdp')
- pointwise_second_updated: float32 [512, 1024], P('fsdp')
- pointwise_out_updated: float32 [512, 512], P('fsdp')
- pointwise_out_first_updated: float32 [512, 512], P('fsdp')
- pointwise_out_second_updated: float32 [512, 512], P('fsdp')
- depthwise_updated: float32 [32, 512], P(None, 'fsdp')
- depthwise_first_updated: float32 [32, 512], P(None, 'fsdp')
- depthwise_second_updated: float32 [32, 512], P(None, 'fsdp')
- norm_table_grad: float32 [12, 512], P(None, 'fsdp')
- norm_table_first_updated: float32 [12, 512], P(None, 'fsdp')
- norm_table_second_updated: float32 [12, 512], P(None, 'fsdp')
The draws below stay inside these ranges and needn't reach their ends.
Inputs may be any that keep to these rules, and one draw needn't show every extreme that they name: Each row: four utterance lengths of one pack, then its padding frames; the row sums to 1024, its largest entry is exactly 512.
All inputs are finite; a program needn't handle non-finite values.
Results may differ from the reference program's by a relative error of at most 0.018.
Values may be sent and summed in bfloat16 or wider, within the bound.
No kernel may reach another device: no remote copies, remote signals or barrier semaphores. Data moves between devices by JAX's collectives and lax.ppermute only.
A program may use at most 320 MiB of HBM per device.

```python
import math
import jax
import jax.numpy as jnp
import numpy as np
from jax import lax

D = 512
FF = 2048
HEADS = 8
KERNEL = 32
FRAMES_DEV = 1024
MAXLEN = 512
STEP = 10
PACKS = 32
TOKENS = 32768


def draw_norm_table(key, part):
    noise = jnp.clip(jax.random.normal(key, (12, D), jnp.float32), -4.0, 4.0)
    rows = jnp.arange(12)[:, None]
    return jnp.where(rows % 2 == 0, 1.0 + 0.15 * noise, 0.2 * noise)


def steps_of(stream_key, shape, split, least, largest):
    loudness, own = 1.0, jax.random.fold_in(stream_key, 6)
    for dim, blocks in split:
        steps = jnp.exp(jax.random.uniform(jax.random.fold_in(own, dim), (blocks,), jnp.float32, least / len(split), largest / len(split)))
        loudness = loudness * jnp.repeat(steps, shape[dim] // blocks).reshape([-1 if axis == dim else 1 for axis in range(len(shape))])
    return loudness


def profile(amount, total, bound, slope):
    weights = [(1 << 20) // math.isqrt(grade ** slope) + 1 for grade in range(2, amount + 1)]
    rest, counts = total - bound - (amount - 1), [1] * (amount - 1)
    while rest > 0:
        candidates = [i for i in range(amount - 1) if counts[i] < bound]
        mass, remaining = sum([weights[i] for i in candidates]), rest
        for i in candidates:
            addition = min(bound - counts[i], max(1, remaining * weights[i] // mass), rest)
            counts[i] = counts[i] + addition
            rest = rest - addition
    return np.array([bound] + counts)


def uneven_parts(stream_key, amount, total, most, skew):
    if amount == 2:
        one = jax.random.randint(stream_key, (), max(1, total - most), min(most, total - 1) + 1)
        return jnp.stack([one, total - one])
    sizes = jnp.asarray(profile(amount, total, most, skew), jnp.int32)
    twos = (amount - 1) // 2
    giver, receiver = sizes[1:1 + 2 * twos:2], sizes[2:2 + 2 * twos:2]
    slack = jnp.minimum(giver - 1, most - receiver)
    passed = jax.random.randint(jax.random.fold_in(stream_key, 1), (twos,), 0, 1 << 20) % (slack + 1)
    sizes = sizes.at[1:1 + 2 * twos:2].set(giver - passed).at[2:2 + 2 * twos:2].set(receiver + passed)
    return sizes[jax.random.permutation(jax.random.fold_in(stream_key, 2), amount)]


def scatter_about(key, extent, scale, limit, cuts=(), held_as=jnp.bfloat16):
    factor_of = steps_of(key, extent, cuts, -0.22, 0.18) if cuts else 1.0
    array = jax.random.normal(key, extent, jnp.float32) * scale * factor_of
    return jnp.minimum(jnp.maximum(array, -limit), limit).astype(held_as)


def setup_inputs(seed: int = 0) -> dict:
    keys = jax.random.split(jax.random.key(seed), 28)
    frames = scatter_about(keys[0], (TOKENS, D), 1.0, 6.0, ((0, 32),))
    cotangent = scatter_about(keys[1], (TOKENS, D), 1.0, 6.0, ((0, 32),))
    lengths = jax.vmap(lambda own: uneven_parts(own, 5, FRAMES_DEV, MAXLEN, 2))(jax.random.split(keys[2], PACKS)).reshape((PACKS, 5)).astype(jnp.int32)
    expand = scatter_about(keys[3], (2, D, FF), D ** -0.5, 0.25, ((1, 4),), jnp.float32)
    expand_first = scatter_about(keys[4], (2, D, FF), (0.011 * TOKENS ** 0.5), 12.0, ((1, 4),), jnp.float32)
    expand_second = jnp.clip(jnp.exp(math.log(26.2144) - 1.3862944 * jax.random.uniform(keys[5], (2, D, FF), jnp.float32) ** steps_of(keys[5], (2, D, FF), ((1, 4),), -0.2, 0.2)), 6.5536, 26.2144)
    shrink = scatter_about(keys[6], (2, FF, D), FF ** -0.5, 0.125, ((1, 4),), jnp.float32)
    shrink_first = scatter_about(keys[7], (2, FF, D), (0.0275 * TOKENS ** 0.5), 32.0, ((1, 4),), jnp.float32)
    shrink_second = jnp.clip(jnp.exp(math.log(163.84) - 1.3862944 * jax.random.uniform(keys[8], (2, FF, D), jnp.float32) ** steps_of(keys[8], (2, FF, D), ((1, 4),), -0.2, 0.2)), 40.96, 163.84)
    attend = scatter_about(keys[9], (D, 3 * D), D ** -0.5, 0.25, ((0, 4),), jnp.float32)
    attend_first = scatter_about(keys[10], (D, 3 * D), (0.011 * TOKENS ** 0.5), 12.0, ((0, 4),), jnp.float32)
    attend_second = jnp.clip(jnp.exp(math.log(26.2144) - 1.3862944 * jax.random.uniform(keys[11], (D, 3 * D), jnp.float32) ** steps_of(keys[11], (D, 3 * D), ((0, 4),), -0.2, 0.2)), 6.5536, 26.2144)
    heads_out = scatter_about(keys[12], (D, D), (D // 8) ** -0.5, 0.75, ((0, 4),), jnp.float32)
    heads_out_first = scatter_about(keys[13], (D, D), (0.022 * TOKENS ** 0.5), 24.0, ((0, 4),), jnp.float32)
    heads_out_second = jnp.clip(jnp.exp(math.log(104.8576) - 1.3862944 * jax.random.uniform(keys[14], (D, D), jnp.float32) ** steps_of(keys[14], (D, D), ((0, 4),), -0.2, 0.2)), 26.2144, 104.8576)
    pointwise = scatter_about(keys[15], (D, 2 * D), D ** -0.5, 0.25, ((0, 4),), jnp.float32)
    pointwise_first = scatter_about(keys[16], (D, 2 * D), (0.011 * TOKENS ** 0.5), 12.0, ((0, 4),), jnp.float32)
    pointwise_second = jnp.clip(jnp.exp(math.log(26.2144) - 1.3862944 * jax.random.uniform(keys[17], (D, 2 * D), jnp.float32) ** steps_of(keys[17], (D, 2 * D), ((0, 4),), -0.2, 0.2)), 6.5536, 26.2144)
    pointwise_out = scatter_about(keys[18], (D, D), (D // 2) ** -0.5, 0.375, ((0, 4),), jnp.float32)
    pointwise_out_first = scatter_about(keys[19], (D, D), (0.033 * TOKENS ** 0.5), 32.0, ((0, 4),), jnp.float32)
    pointwise_out_second = jnp.clip(jnp.exp(math.log(235.9296) - 1.3862944 * jax.random.uniform(keys[20], (D, D), jnp.float32) ** steps_of(keys[20], (D, D), ((0, 4),), -0.2, 0.2)), 58.9824, 235.9296)
    depthwise = scatter_about(keys[21], (KERNEL, D), KERNEL ** -0.5, 1.0, ((1, 4),), jnp.float32)
    depthwise_first = scatter_about(keys[22], (KERNEL, D), (0.033 * TOKENS ** 0.5), 32.0, ((1, 4),), jnp.float32)
    depthwise_second = jnp.clip(jnp.exp(math.log(235.9296) - 1.3862944 * jax.random.uniform(keys[23], (KERNEL, D), jnp.float32) ** steps_of(keys[23], (KERNEL, D), ((1, 4),), -0.2, 0.2)), 58.9824, 235.9296)
    norm_table = draw_norm_table(jax.random.fold_in(keys[27], 71), 0)
    norm_table_first = scatter_about(keys[25], (12, D), (0.055 * TOKENS ** 0.5), 64.0, ((1, 4),), jnp.float32)
    norm_table_second = jnp.clip(jnp.exp(math.log(655.36) - 1.3862944 * jax.random.uniform(keys[26], (12, D), jnp.float32) ** steps_of(keys[26], (12, D), ((1, 4),), -0.2, 0.2)), 163.84, 655.36)
    return dict(frames=frames, cotangent=cotangent, lengths=lengths, expand=expand, expand_first=expand_first, expand_second=expand_second, shrink=shrink, shrink_first=shrink_first, shrink_second=shrink_second, attend=attend, attend_first=attend_first, attend_second=attend_second, heads_out=heads_out, heads_out_first=heads_out_first, heads_out_second=heads_out_second, pointwise=pointwise, pointwise_first=pointwise_first, pointwise_second=pointwise_second, pointwise_out=pointwise_out, pointwise_out_first=pointwise_out_first, pointwise_out_second=pointwise_out_second, depthwise=depthwise, depthwise_first=depthwise_first, depthwise_second=depthwise_second, norm_table=norm_table, norm_table_first=norm_table_first, norm_table_second=norm_table_second)


HIGHEST = lax.Precision.HIGHEST
norm_epsilon = 1e-05
batch_epsilon = 1e-05
masked_score = -1000000000.0
learn_rate = 0.1
beta_first = 0.9
beta_second = 0.98
adam_epsilon = 1e-08
decay_rate = 0.01

@jax.custom_vjp
def low(v):
    return lax.optimization_barrier(v.astype(jnp.bfloat16)).astype(jnp.float32)

@jax.custom_vjp
def low_back(v):
    return v

def low_keep(v):
    return (low(v), None)

def low_pass(kept, grad):
    return (grad,)

def back_keep(v):
    return (v, None)

def back_low(kept, grad):
    return (low(grad),)
low.defvjp(low_keep, low_pass)
low_back.defvjp(back_keep, back_low)

def product(left, right):
    return jnp.dot(left, right, precision=HIGHEST, preferred_element_type=jnp.float32)

def layer_normalize(value, gain, bias):
    center = value - lax.optimization_barrier(jnp.mean(value, axis=-1, keepdims=True))
    scale = lax.rsqrt(lax.optimization_barrier(jnp.mean(center * center, axis=-1, keepdims=True)) + norm_epsilon)
    return center * scale * gain + bias

def swish(value):
    return value * jax.nn.sigmoid(value)

def layout(row, frames):
    bounds = jnp.cumsum(row[:4]).astype(jnp.int32)
    places = jnp.arange(frames, dtype=jnp.int32)
    segment = lax.optimization_barrier(jnp.sum((places[:, None] >= bounds[None, :]).astype(jnp.int32), axis=1)).astype(jnp.int32)
    starts = jnp.concatenate([jnp.zeros((1,), jnp.int32), bounds])
    pick = (segment[:, None] == jnp.arange(5, dtype=jnp.int32)[None, :]).astype(jnp.int32)
    position = (places - lax.optimization_barrier(jnp.sum(pick * starts[None, :], axis=1))).astype(jnp.int32)
    return (segment, position, segment < 4)

def rotary_tables(position, half):
    freq = jnp.exp(jnp.arange(half, dtype=jnp.float32) * (-math.log(10000.0) / half))
    angle = position.astype(jnp.float32)[:, None] * freq[None, :]
    return (jnp.cos(angle)[:, None, :], jnp.sin(angle)[:, None, :])

def rotate(value, cosine, sine):
    half = value.shape[-1] // 2
    first, second_block = (value[..., :half], value[..., half:])
    return jnp.concatenate([first * cosine - second_block * sine, first * sine + second_block * cosine], axis=-1)

def depth_conv(glu, kernel, segment):
    size = kernel.shape[0]
    left = size // 2
    frames = glu.shape[0]
    padded = jnp.pad(glu, ((left, size - 1 - left), (0, 0)))
    padded_seg = jnp.pad(segment, (left, size - 1 - left), constant_values=-1)
    total = jnp.zeros_like(glu)
    for offset in range(size):
        keep = (padded_seg[offset:offset + frames] == segment).astype(jnp.float32)[:, None]
        total = total + kernel[offset] * padded[offset:offset + frames] * keep
    return total

def front(params, single_item):
    expand, shrink, attend, heads_out, pointwise, pointwise_out, depthwise, norm_entries = params
    value, segment, position = single_item
    frames = value.shape[0]
    head_dim = D // HEADS
    hidden = low(layer_normalize(value, norm_entries[0], norm_entries[1]))
    pre = low_back(product(hidden, expand[0]))
    out = low_back(product(low(swish(pre)), shrink[0]))
    first = value + 0.5 * out
    hidden = low(layer_normalize(first, norm_entries[2], norm_entries[3]))
    packed = low_back(product(hidden, attend)).reshape(frames, 3, HEADS, head_dim)
    cosine, sine = rotary_tables(position, head_dim // 2)
    query = low(rotate(packed[:, 0], cosine, sine))
    keyset = low(rotate(packed[:, 1], cosine, sine))
    values = low(packed[:, 2])
    scores = low_back(jnp.einsum('qhd,khd->hqk', query, keyset, precision=HIGHEST) * head_dim ** (-0.5))
    same = segment[:, None] == segment[None, :]
    scores = jnp.where(same[None], scores, masked_score)
    top = lax.optimization_barrier(jnp.max(scores, axis=-1, keepdims=True))
    expo = jnp.exp(scores - top)
    prob = expo / lax.optimization_barrier(jnp.sum(expo, axis=-1, keepdims=True))
    mixed = low(low_back(jnp.einsum('hqk,khd->qhd', low(prob), values, precision=HIGHEST))).reshape(frames, D)
    second_block = first + low_back(product(mixed, heads_out))
    hidden = low(layer_normalize(second_block, norm_entries[4], norm_entries[5]))
    gates = low_back(product(hidden, pointwise))
    glu = gates[:, :D] * jax.nn.sigmoid(gates[:, D:])
    return (second_block, depth_conv(glu, depthwise, segment))

def rear(params, stats, single_item):
    expand, shrink, attend, heads_out, pointwise, pointwise_out, depthwise, norm_entries = params
    second_block, convolution_module, valid_mask = single_item
    masked_mean, batch_norm_scale = stats
    zhat = (convolution_module - masked_mean) * batch_norm_scale
    zed = zhat * norm_entries[6] + norm_entries[7]
    third = second_block + low_back(product(low(swish(zed)), pointwise_out))
    hidden = low(layer_normalize(third, norm_entries[8], norm_entries[9]))
    pre = low_back(product(hidden, expand[1]))
    out = low_back(product(low(swish(pre)), shrink[1]))
    fourth_block = third + 0.5 * out
    return layer_normalize(fourth_block, norm_entries[10], norm_entries[11]) * valid_mask

def adam_update(master, first, second_block, grad, decay):
    first_new = beta_first * first + (1.0 - beta_first) * grad
    second_new = beta_second * second_block + (1.0 - beta_second) * grad * grad
    first_hat = first_new / (1.0 - beta_first ** STEP)
    second_hat = second_new / (1.0 - beta_second ** STEP)
    master_new = master - learn_rate * (first_hat / (jnp.sqrt(second_hat) + adam_epsilon) + decay * master)
    return (master_new, first_new, second_new)

def moments_only(first, second_block, grad):
    first_new = beta_first * first + (1.0 - beta_first) * grad
    second_new = beta_second * second_block + (1.0 - beta_second) * grad * grad
    return (first_new, second_new)

def reference(frames, cotangent, lengths, expand, expand_first, expand_second, shrink, shrink_first, shrink_second, attend, attend_first, attend_second, heads_out, heads_out_first, heads_out_second, pointwise, pointwise_first, pointwise_second, pointwise_out, pointwise_out_first, pointwise_out_second, depthwise, depthwise_first, depthwise_second, norm_table, norm_table_first, norm_table_second):
    packs = lengths.shape[0]
    segment, position, valid_frames = jax.vmap(lambda row: layout(row, FRAMES_DEV))(lengths)
    valid_mask = valid_frames.astype(jnp.float32)[..., None]
    value = frames.astype(jnp.float32).reshape(packs, FRAMES_DEV, D)
    masters = (expand, shrink, attend, heads_out, pointwise, pointwise_out, depthwise, norm_table)
    front_saved = jax.checkpoint(front)
    rear_residuals = jax.checkpoint(rear)

    def forward(inputs, weights):
        rounded_value = tuple((low(weight) for weight in weights))
        second_block, convolution_module = lax.map(lambda single_item: front_saved(rounded_value, single_item), (inputs, segment, position))
        valid_count = jnp.sum(valid_mask)
        masked_mean = lax.optimization_barrier(jnp.sum(valid_mask * convolution_module, axis=(0, 1))) / valid_count
        masked_variance = lax.optimization_barrier(jnp.sum(valid_mask * convolution_module * convolution_module, axis=(0, 1))) / valid_count - masked_mean * masked_mean
        batch_norm_scale = lax.rsqrt(masked_variance + batch_epsilon)
        return lax.map(lambda single_item: rear_residuals(rounded_value, (masked_mean, batch_norm_scale), single_item), (second_block, convolution_module, valid_mask))
    result, pull = jax.vjp(forward, value, masters)
    grad_in, grads = pull(cotangent.astype(jnp.float32).reshape(packs, FRAMES_DEV, D))
    firsts = (expand_first, shrink_first, attend_first, heads_out_first, pointwise_first, pointwise_out_first, depthwise_first, norm_table_first)
    seconds = (expand_second, shrink_second, attend_second, heads_out_second, pointwise_second, pointwise_out_second, depthwise_second, norm_table_second)
    updates = []
    for index in range(7):
        updates.extend(adam_update(masters[index], firsts[index], seconds[index], grads[index], decay_rate))
    norm_first_new, norm_second_new = moments_only(firsts[7], seconds[7], grads[7])
    updates.extend((grads[7], norm_first_new, norm_second_new))
    return (result.reshape(TOKENS, D).astype(jnp.bfloat16), grad_in.reshape(TOKENS, D), updates[0], updates[1], updates[2], updates[3], updates[4], updates[5], updates[6], updates[7], updates[8], updates[9], updates[10], updates[11], updates[12], updates[13], updates[14], updates[15], updates[16], updates[17], updates[18], updates[19], updates[20], updates[21], updates[22], updates[23])
```

```python
import math

import jax
import jax.numpy as jnp
from jax import lax
from jax.sharding import PartitionSpec as P

HEADS = 8
STEP = 10


norm_epsilon = 1e-05
batch_epsilon = 1e-05
masked_score = -1000000000.0
learn_rate = 0.1
beta_first = 0.9
beta_second = 0.98
adam_epsilon = 1e-08
decay_rate = 0.01


def product(left, right):
    return jnp.dot(left, right, preferred_element_type=jnp.float32)


def times_transposed(left, right):
    return lax.dot_general(
        left, right, (((1,), (1,)), ((), ())), preferred_element_type=jnp.float32
    )


def transposed_times(left, right):
    return lax.dot_general(
        left, right, (((0,), (0,)), ((), ())), preferred_element_type=jnp.float32
    )


def layer_normalize(value, gain, bias):
    center = value - jnp.mean(value, axis=-1, keepdims=True)
    scale = lax.rsqrt(jnp.mean(center * center, axis=-1, keepdims=True) + norm_epsilon)
    normed = center * scale
    return (normed * gain + bias, normed, scale)


def norm_back(grad_out, gain, normed, scale):
    grad_norm = grad_out * gain
    grad_in = scale * (
        grad_norm
        - jnp.mean(grad_norm, axis=-1, keepdims=True)
        - normed * jnp.mean(grad_norm * normed, axis=-1, keepdims=True)
    )
    return (grad_in, jnp.sum(grad_out * normed, axis=0), jnp.sum(grad_out, axis=0))


def swish(value):
    return value * jax.nn.sigmoid(value)


def swish_slope(value):
    sigma = jax.nn.sigmoid(value)
    return sigma * (1.0 + value * (1.0 - sigma))


def layout(row, frames):
    bounds = jnp.cumsum(row[:4])
    places = jnp.arange(frames, dtype=jnp.int32)
    segment = jnp.sum((places[:, None] >= bounds[None, :]).astype(jnp.int32), axis=1)
    starts = jnp.concatenate([jnp.zeros((1,), jnp.int32), bounds])
    pick = (segment[:, None] == jnp.arange(5, dtype=jnp.int32)[None, :]).astype(jnp.int32)
    position = places - jnp.sum(pick * starts[None, :], axis=1)
    return (segment, position, segment < 4)


def rotary_tables(position, half):
    freq = jnp.exp(jnp.arange(half, dtype=jnp.float32) * (-math.log(10000.0) / half))
    angle = position.astype(jnp.float32)[:, None] * freq[None, :]
    return (jnp.cos(angle)[:, None, :], jnp.sin(angle)[:, None, :])


def rotate(value, cosine, sine):
    half = value.shape[-1] // 2
    first, second_block = (value[..., :half], value[..., half:])
    return jnp.concatenate(
        [first * cosine - second_block * sine, first * sine + second_block * cosine], axis=-1
    )


def unrotate(grad, cosine, sine):
    half = grad.shape[-1] // 2
    first, second_block = (grad[..., :half], grad[..., half:])
    return jnp.concatenate(
        [first * cosine + second_block * sine, second_block * cosine - first * sine], axis=-1
    )


def neighbour_masks(segment, size):
    left = size // 2
    frames = segment.shape[0]
    padded = jnp.pad(segment, (left, size - 1 - left), constant_values=-1)
    return [
        (padded[offset : offset + frames] == segment).astype(jnp.float32)[:, None]
        for offset in range(size)
    ]


def depth_forward(glu, kernel, masks):
    size = kernel.shape[0]
    left = size // 2
    frames = glu.shape[0]
    padded = jnp.pad(glu, ((left, size - 1 - left), (0, 0)))
    total = jnp.zeros_like(glu)
    for offset in range(size):
        total = total + kernel[offset] * padded[offset : offset + frames] * masks[offset]
    return (total, padded)


def depth_backward(grad, kernel, masks, padded):
    size = kernel.shape[0]
    left = size // 2
    frames = grad.shape[0]
    grad_wide = jnp.pad(grad, ((size - 1 - left, left), (0, 0)))
    grad_glu = jnp.zeros_like(grad)
    taps = []
    for offset in range(size):
        taps.append(jnp.sum(grad * masks[offset] * padded[offset : offset + frames], axis=0))
        mask_wide = jnp.pad(masks[offset], ((size - 1 - left, left), (0, 0)))
        begin = size - 1 - offset
        grad_glu = (
            grad_glu
            + kernel[offset] * grad_wide[begin : begin + frames] * mask_wide[begin : begin + frames]
        )
    return (grad_glu, jnp.stack(taps))


def feed_forward(value, w_in, w_out, gain, bias):
    normed_out, normed, scale = layer_normalize(value, gain, bias)
    hidden = normed_out.astype(jnp.bfloat16)
    before = product(hidden, w_in)
    active = swish(before).astype(jnp.bfloat16)
    return (value + 0.5 * product(active, w_out), (normed, scale, hidden, before, active))


def feed_back(grad, w_in, w_out, gain, saved):
    normed, scale, hidden, before, active = saved
    grad_out = (0.5 * grad).astype(jnp.bfloat16)
    grad_w_out = transposed_times(active, grad_out)
    grad_before = (times_transposed(grad_out, w_out) * swish_slope(before)).astype(jnp.bfloat16)
    grad_w_in = transposed_times(hidden, grad_before)
    grad_hidden = times_transposed(grad_before, w_in)
    grad_in, grad_gain, grad_bias = norm_back(grad_hidden, gain, normed, scale)
    return (grad + grad_in, grad_w_in, grad_w_out, grad_gain, grad_bias)


def masked_scores(query, keyset, same, score_scale):
    scores = (
        jnp.einsum("qhd,khd->hqk", query, keyset, preferred_element_type=jnp.float32) * score_scale
    )
    return jnp.where(same[None], scores, masked_score)


def adam_update(master, first, second_block, grad, decay):
    first_new = beta_first * first + (1.0 - beta_first) * grad
    second_new = beta_second * second_block + (1.0 - beta_second) * grad * grad
    first_hat = first_new / (1.0 - beta_first**STEP)
    second_hat = second_new / (1.0 - beta_second**STEP)
    master_new = master - learn_rate * (
        first_hat / (jnp.sqrt(second_hat) + adam_epsilon) + decay * master
    )
    return (master_new, first_new, second_new)


def moments_only(first, second_block, grad):
    first_new = beta_first * first + (1.0 - beta_first) * grad
    second_new = beta_second * second_block + (1.0 - beta_second) * grad * grad
    return (first_new, second_new)


def bits_of(size):
    return int(size).bit_length() - 1


def swap(value, axis, size, bit):
    pairs = [(k, k ^ (1 << bit)) for k in range(size)]
    return lax.ppermute(value, axis, pairs)


def gather_shards(own, fs):
    me = lax.axis_index("fsdp")
    pieces, rel = own[None], [0]
    for bit in reversed(range(bits_of(fs))):
        other = swap(pieces, "fsdp", fs, bit)
        pieces = jnp.concatenate([pieces, other], axis=0)
        rel = rel + [r ^ (1 << bit) for r in rel]
    full = jnp.zeros((fs,) + own.shape, own.dtype)
    for k, r in enumerate(rel):
        full = lax.dynamic_update_slice_in_dim(full, pieces[k : k + 1], me ^ r, 0)
    return full


def halve(value, axis, size, bit, side):
    send = lax.dynamic_index_in_dim(value, 1 - side, 0, keepdims=False)
    keep = lax.dynamic_index_in_dim(value, side, 0, keepdims=False)
    got = swap(send, axis, size, bit)
    return (keep.astype(jnp.float32) + got.astype(jnp.float32)).astype(value.dtype)


def reduce_all(grad, fs, dp):
    me = lax.axis_index("fsdp")
    pack = lax.axis_index("dp")
    part = grad
    for bit in range(bits_of(fs)):
        shape = part.shape
        pairs = part.reshape((shape[0] // 2, 2) + shape[1:]).swapaxes(0, 1)
        part = halve(pairs, "fsdp", fs, bit, (me >> bit) & 1)
    part = part[0]
    for bit in range(bits_of(dp)):
        rows = part.shape[0]
        part = halve(part.reshape((2, rows // 2) + part.shape[1:]), "dp", dp, bit, (pack >> bit) & 1)
    for bit in reversed(range(bits_of(dp))):
        other = swap(part, "dp", dp, bit)
        side = (pack >> bit) & 1
        both = jnp.zeros((2,) + part.shape, part.dtype)
        both = lax.dynamic_update_slice_in_dim(both, part[None], side, 0)
        both = lax.dynamic_update_slice_in_dim(both, other[None], 1 - side, 0)
        part = both.reshape((2 * part.shape[0],) + part.shape[1:])
    return part


def total_over_all(rows):
    axes = ("dp", "fsdp")
    count = lax.axis_size(axes)
    spread = jnp.broadcast_to(rows[None], (count,) + rows.shape)
    got = lax.all_to_all(spread, axes, 0, 0, tiled=True)
    return jnp.sum(got, axis=0)


def to_rows(block):
    r, c = block.shape
    k = c // 512
    return block.reshape(r, k, 512).swapaxes(0, 1).reshape(k * r, 512)


def from_rows(rows, r, c):
    k = c // 512
    return rows.reshape(k, r, 512).swapaxes(0, 1).reshape(r, c)


def owners_rows(grad, fs):
    r = grad.shape[0] // fs
    k = grad.shape[1] // 512
    return grad.astype(jnp.bfloat16).reshape(fs, r, k, 512).swapaxes(1, 2).reshape(fs, k * r, 512)


def full_of(rows, r, c):
    fs = rows.shape[0]
    k = c // 512
    return rows.reshape(fs, k, r, 512).swapaxes(1, 2).reshape(fs * r, c)


def per_device(
    frames,
    cotangent,
    lengths,
    expand,
    expand_first,
    expand_second,
    shrink,
    shrink_first,
    shrink_second,
    attend,
    attend_first,
    attend_second,
    heads_out,
    heads_out_first,
    heads_out_second,
    pointwise,
    pointwise_first,
    pointwise_second,
    pointwise_out,
    pointwise_out_first,
    pointwise_out_second,
    depthwise,
    depthwise_first,
    depthwise_second,
    norm_table,
    norm_table_first,
    norm_table_second,
):
    masters = (expand, shrink, attend, heads_out, pointwise, pointwise_out, depthwise, norm_table)
    rounded_value = [master.astype(jnp.bfloat16) for master in masters]
    fs, dp = (lax.axis_size("fsdp"), lax.axis_size("dp"))
    er, sr, ar = expand.shape[1], shrink.shape[1], attend.shape[0]
    dr = depthwise.shape[1]
    small = jnp.concatenate([rounded_value[6], rounded_value[7]], axis=0)
    tiny_rows = small.shape[0]
    in_zero = gather_shards(to_rows(rounded_value[0][0]), fs)
    small_full = gather_shards(small, fs)
    out_zero = gather_shards(rounded_value[1][0], fs)
    attn_full = gather_shards(
        jnp.concatenate([to_rows(rounded_value[2]), rounded_value[3]], axis=0), fs
    )
    conv_full = gather_shards(
        jnp.concatenate([to_rows(rounded_value[4]), rounded_value[5]], axis=0), fs
    )
    ff_one = gather_shards(
        jnp.concatenate([to_rows(rounded_value[0][1]), rounded_value[1][1]], axis=0), fs
    )
    full_expand = (full_of(in_zero, er, 2048), full_of(ff_one[:, : 4 * er], er, 2048))
    full_shrink = (out_zero.reshape(fs * sr, 512), ff_one[:, 4 * er :].reshape(fs * sr, 512))
    full_attend = full_of(attn_full[:, : 3 * ar], ar, 1536)
    full_heads = attn_full[:, 3 * ar :].reshape(fs * ar, 512)
    full_point = full_of(conv_full[:, : 2 * ar], ar, 1024)
    full_point_out = conv_full[:, 2 * ar :].reshape(fs * ar, 512)
    small_cols = small_full.swapaxes(0, 1).reshape(tiny_rows, fs * dr)
    full_depth, full_norms = (small_cols[:32], small_cols[32:])
    norm_entries = full_norms.astype(jnp.float32)
    kernel = full_depth.astype(jnp.float32)
    value = frames.astype(jnp.float32)
    frame_count, width = value.shape
    heads = HEADS
    head_dim = width // heads
    score_scale = head_dim ** (-0.5)
    segment, position, valid_frames = layout(lengths[0], frame_count)
    valid_col = valid_frames.astype(jnp.float32)[:, None]
    cosine, sine = rotary_tables(position, head_dim // 2)
    same = segment[:, None] == segment[None, :]
    masks = neighbour_masks(segment, kernel.shape[0])
    first, saved_one = feed_forward(
        value, full_expand[0], full_shrink[0], norm_entries[0], norm_entries[1]
    )
    attn_out, attn_normed, attn_scale = layer_normalize(first, norm_entries[2], norm_entries[3])
    attn_hidden = attn_out.astype(jnp.bfloat16)
    packed = product(attn_hidden, full_attend).reshape(frame_count, 3, heads, head_dim)
    query = rotate(packed[:, 0], cosine, sine).astype(jnp.bfloat16)
    keyset = rotate(packed[:, 1], cosine, sine).astype(jnp.bfloat16)
    values = packed[:, 2].astype(jnp.bfloat16)
    scores = masked_scores(query, keyset, same, score_scale)
    top = jnp.max(scores, axis=-1, keepdims=True)
    expo = jnp.exp(scores - top)
    total = jnp.sum(expo, axis=-1, keepdims=True)
    prob = expo / total
    log_total = top + jnp.log(total)
    mixed = jnp.einsum(
        "hqk,khd->qhd", prob.astype(jnp.bfloat16), values, preferred_element_type=jnp.float32
    )
    mixed = mixed.astype(jnp.bfloat16).reshape(frame_count, width)
    second_block = first + product(mixed, full_heads)
    conv_out, conv_normed, conv_scale = layer_normalize(
        second_block, norm_entries[4], norm_entries[5]
    )
    conv_hidden = conv_out.astype(jnp.bfloat16)
    gates = product(conv_hidden, full_point)
    half_value = gates[:, :width]
    sigma = jax.nn.sigmoid(gates[:, width:])
    glu = half_value * sigma
    convolution_module, padded_glu = depth_forward(glu, kernel, masks)
    masked = valid_col * convolution_module
    stats = total_over_all(
        jnp.stack(
            [
                jnp.sum(masked, axis=0),
                jnp.sum(masked * convolution_module, axis=0),
                jnp.broadcast_to(jnp.sum(valid_col), (width,)),
            ]
        )
    )
    valid_count = stats[2]
    masked_mean = stats[0] / valid_count
    batch_norm_scale = lax.rsqrt(stats[1] / valid_count - masked_mean * masked_mean + batch_epsilon)
    zhat = (convolution_module - masked_mean) * batch_norm_scale
    zed = zhat * norm_entries[6] + norm_entries[7]
    conv_active = swish(zed).astype(jnp.bfloat16)
    third = second_block + product(conv_active, full_point_out)
    fourth_block, saved_two = feed_forward(
        third, full_expand[1], full_shrink[1], norm_entries[8], norm_entries[9]
    )
    last_out, last_normed, last_scale = layer_normalize(
        fourth_block, norm_entries[10], norm_entries[11]
    )
    layer_output = (last_out * valid_col).astype(jnp.bfloat16)
    back_expand, back_shrink, back_attend, back_heads = (
        full_expand,
        full_shrink,
        full_attend,
        full_heads,
    )
    back_point, back_point_out, back_depth, back_norms = (
        full_point,
        full_point_out,
        full_depth,
        full_norms,
    )
    norms_back = back_norms.astype(jnp.float32)
    kernel_back = back_depth.astype(jnp.float32)
    grad_y = cotangent.astype(jnp.float32) * valid_col
    grad_fourth, gain_last, bias_last = norm_back(grad_y, norms_back[10], last_normed, last_scale)
    grad_third, grad_in_two, grad_out_two, gain_four, bias_four = feed_back(
        grad_fourth, back_expand[1], back_shrink[1], norms_back[8], saved_two
    )
    grad_branch = grad_third.astype(jnp.bfloat16)
    grad_point_out = transposed_times(conv_active, grad_branch)
    grad_zed = times_transposed(grad_branch, back_point_out) * swish_slope(zed)
    local_bias = jnp.sum(grad_zed, axis=0)
    local_gain = jnp.sum(grad_zed * zhat, axis=0)
    totals = total_over_all(jnp.stack([local_bias, local_gain]))
    grad_conv = (
        batch_norm_scale
        * norms_back[6]
        * (grad_zed - valid_col * (totals[0] + zhat * totals[1]) / valid_count)
    )
    grad_glu, grad_kernel = depth_backward(grad_conv, kernel_back, masks, padded_glu)
    grad_gates = jnp.concatenate(
        [grad_glu * sigma, grad_glu * half_value * sigma * (1.0 - sigma)], axis=1
    ).astype(jnp.bfloat16)
    grad_point = transposed_times(conv_hidden, grad_gates)
    grad_conv_in, gain_conv, bias_conv = norm_back(
        times_transposed(grad_gates, back_point), norms_back[4], conv_normed, conv_scale
    )
    grad_second = grad_third + grad_conv_in
    grad_attn = grad_second.astype(jnp.bfloat16)
    grad_heads = transposed_times(mixed, grad_attn)
    grad_mixed = (
        times_transposed(grad_attn, back_heads)
        .astype(jnp.bfloat16)
        .reshape(frame_count, heads, head_dim)
    )
    scores = masked_scores(query, keyset, same, score_scale)
    prob = jnp.exp(scores - log_total)
    grad_values = jnp.einsum(
        "hqk,qhd->khd", prob.astype(jnp.bfloat16), grad_mixed, preferred_element_type=jnp.float32
    )
    grad_prob = jnp.einsum("qhd,khd->hqk", grad_mixed, values, preferred_element_type=jnp.float32)
    grad_scores = (prob * (grad_prob - jnp.sum(prob * grad_prob, axis=-1, keepdims=True))).astype(
        jnp.bfloat16
    )
    grad_query = (
        jnp.einsum("hqk,khd->qhd", grad_scores, keyset, preferred_element_type=jnp.float32)
        * score_scale
    )
    grad_key = (
        jnp.einsum("hqk,qhd->khd", grad_scores, query, preferred_element_type=jnp.float32)
        * score_scale
    )
    grad_packed = jnp.stack(
        [unrotate(grad_query, cosine, sine), unrotate(grad_key, cosine, sine), grad_values], axis=1
    )
    grad_packed = grad_packed.reshape(frame_count, 3 * width).astype(jnp.bfloat16)
    grad_attend = transposed_times(attn_hidden, grad_packed)
    grad_attn_in, gain_attn, bias_attn = norm_back(
        times_transposed(grad_packed, back_attend), norms_back[2], attn_normed, attn_scale
    )
    grad_first = grad_second + grad_attn_in
    frames_grad, grad_in_one, grad_out_one, gain_one, bias_one = feed_back(
        grad_first, back_expand[0], back_shrink[0], norms_back[0], saved_one
    )
    grad_norms = jnp.stack(
        [
            gain_one,
            bias_one,
            gain_attn,
            bias_attn,
            gain_conv,
            bias_conv,
            local_gain,
            local_bias,
            gain_four,
            bias_four,
            gain_last,
            bias_last,
        ]
    )
    small_grad = jnp.concatenate([grad_kernel, grad_norms], axis=0).astype(jnp.bfloat16)
    small_grad = small_grad.reshape(tiny_rows, fs, dr).swapaxes(0, 1)
    small_size = tiny_rows * dr
    small_pad = -small_size % (512 * dp)
    small_grad = jnp.pad(small_grad.reshape(fs, small_size), ((0, 0), (0, small_pad)))
    small_grad = small_grad.reshape(fs, -1, 512)
    red_ff_one = reduce_all(
        jnp.concatenate([owners_rows(grad_in_two, fs), owners_rows(grad_out_two, fs)], axis=1),
        fs,
        dp,
    )
    red_conv = reduce_all(
        jnp.concatenate([owners_rows(grad_point, fs), owners_rows(grad_point_out, fs)], axis=1),
        fs,
        dp,
    )
    red_attn = reduce_all(
        jnp.concatenate([owners_rows(grad_attend, fs), owners_rows(grad_heads, fs)], axis=1),
        fs,
        dp,
    )
    red_out_zero = reduce_all(owners_rows(grad_out_one, fs), fs, dp)
    red_in_zero = reduce_all(
        jnp.concatenate([owners_rows(grad_in_one, fs), small_grad], axis=1), fs, dp
    )
    red_small = red_in_zero[4 * er :].reshape(-1)[:small_size].reshape(tiny_rows, dr)
    reduced = (
        jnp.stack([from_rows(red_in_zero[: 4 * er], er, 2048), from_rows(red_ff_one[: 4 * er], er, 2048)]),
        jnp.stack([red_out_zero, red_ff_one[4 * er :]]),
        from_rows(red_attn[: 3 * ar], ar, 1536),
        red_attn[3 * ar :],
        from_rows(red_conv[: 2 * ar], ar, 1024),
        red_conv[2 * ar :],
        red_small[:32],
        red_small[32:],
    )
    reduced = tuple(value.astype(jnp.float32) for value in reduced)
    firsts = (
        expand_first,
        shrink_first,
        attend_first,
        heads_out_first,
        pointwise_first,
        pointwise_out_first,
        depthwise_first,
        norm_table_first,
    )
    seconds = (
        expand_second,
        shrink_second,
        attend_second,
        heads_out_second,
        pointwise_second,
        pointwise_out_second,
        depthwise_second,
        norm_table_second,
    )
    updates = []
    for index in range(7):
        updates.extend(
            adam_update(masters[index], firsts[index], seconds[index], reduced[index], decay_rate)
        )
    norm_first_new, norm_second_new = moments_only(firsts[7], seconds[7], reduced[7])
    updates.extend((reduced[7], norm_first_new, norm_second_new))
    return (
        layer_output,
        frames_grad,
        updates[0],
        updates[1],
        updates[2],
        updates[3],
        updates[4],
        updates[5],
        updates[6],
        updates[7],
        updates[8],
        updates[9],
        updates[10],
        updates[11],
        updates[12],
        updates[13],
        updates[14],
        updates[15],
        updates[16],
        updates[17],
        updates[18],
        updates[19],
        updates[20],
        updates[21],
        updates[22],
        updates[23],
    )


def solution(mesh):
    return jax.shard_map(
        per_device,
        mesh=mesh,
        in_specs=(
            P(("dp", "fsdp"), None),
            P(("dp", "fsdp"), None),
            P(("dp", "fsdp"), None),
            P(None, "fsdp", None),
            P(None, "fsdp", None),
            P(None, "fsdp", None),
            P(None, "fsdp", None),
            P(None, "fsdp", None),
            P(None, "fsdp", None),
            P("fsdp", None),
            P("fsdp", None),
            P("fsdp", None),
            P("fsdp", None),
            P("fsdp", None),
            P("fsdp", None),
            P("fsdp", None),
            P("fsdp", None),
            P("fsdp", None),
            P("fsdp", None),
            P("fsdp", None),
            P("fsdp", None),
            P(None, "fsdp"),
            P(None, "fsdp"),
            P(None, "fsdp"),
            P(None, "fsdp"),
            P(None, "fsdp"),
            P(None, "fsdp"),
        ),
        out_specs=(
            P(("dp", "fsdp"), None),
            P(("dp", "fsdp"), None),
            P(None, "fsdp", None),
            P(None, "fsdp", None),
            P(None, "fsdp", None),
            P(None, "fsdp", None),
            P(None, "fsdp", None),
            P(None, "fsdp", None),
            P("fsdp", None),
            P("fsdp", None),
            P("fsdp", None),
            P("fsdp", None),
            P("fsdp", None),
            P("fsdp", None),
            P("fsdp", None),
            P("fsdp", None),
            P("fsdp", None),
            P("fsdp", None),
            P("fsdp", None),
            P("fsdp", None),
            P(None, "fsdp"),
            P(None, "fsdp"),
            P(None, "fsdp"),
            P(None, "fsdp"),
            P(None, "fsdp"),
            P(None, "fsdp"),
        ),
        check_vma=False,
    )
```

```python
import functools
import math

import jax
import jax.numpy as jnp
from jax import lax
from jax.experimental import pallas as pl
from jax.experimental.pallas import tpu as pltpu
from jax.sharding import PartitionSpec as P

HEADS = 8
STEP = 10
TAPS = 32
GAP = 16
LIMIT = 50 * 1024 * 1024
TILE = 256
WINDOWS = (512, 768)

norm_epsilon = 1e-05
batch_epsilon = 1e-05
masked_score = -1000000000.0
learn_rate = 0.1
beta_first = 0.9
beta_second = 0.98
adam_epsilon = 1e-08
decay_rate = 0.01

f32, bf16 = jnp.float32, jnp.bfloat16


def mm(a, b):
    return jnp.dot(a, b, preferred_element_type=f32)


def mm_nt(a, b):
    return lax.dot_general(a, b, (((1,), (1,)), ((), ())), preferred_element_type=f32)


def mm_tn(a, b):
    return lax.dot_general(a, b, (((0,), (0,)), ((), ())), preferred_element_type=f32)


def normalize(value):
    center = value - jnp.mean(value, axis=-1, keepdims=True)
    scale = lax.rsqrt(jnp.mean(center * center, axis=-1, keepdims=True) + norm_epsilon)
    return center * scale, scale


def norm_back(grad_out, gain, normed, scale):
    grad_norm = grad_out * gain
    return scale * (
        grad_norm
        - jnp.mean(grad_norm, axis=-1, keepdims=True)
        - normed * jnp.mean(grad_norm * normed, axis=-1, keepdims=True)
    )


def col_sum(value):
    return jnp.sum(value, axis=0, keepdims=True)


def sigmoid(value):
    return 0.5 * jnp.tanh(0.5 * value) + 0.5


def slope_of(value, sigma):
    return sigma * (1.0 + value * (1.0 - sigma))


def seg_of(places, ends):
    s = (places >= ends[0]).astype(jnp.int32)
    for j in range(1, 4):
        s = s + (places >= ends[j]).astype(jnp.int32)
    return s


def pick_last(values, count):
    out = values[0]
    for j in range(1, len(values)):
        out = jnp.where(count >= j, values[j], out)
    return out


def key_range(first, last, ends, rows):
    starts = [jnp.int32(0)] + ends
    stops = ends + [jnp.int32(rows)]
    return pick_last(starts, seg_of(first, ends)), pick_last(stops, seg_of(last, ends))


def in_window(lo, hi, rows, body):
    begin = (lo // 128) * 128
    done = jnp.bool_(False)
    for w in sorted({w for w in WINDOWS if w < rows} | {rows}):
        start = jnp.minimum(begin, rows - w)
        fits = jnp.logical_and(hi <= start + w, jnp.logical_not(done))

        @pl.when(fits)
        def _(start=start, w=w):
            body(pl.multiple_of(start, 128), w)

        done = jnp.logical_or(done, fits)


def partner(x):
    lane = lax.broadcasted_iota(jnp.int32, (1, 128), 1)
    return jnp.where((lane & 32) == 0, pltpu.roll(x, 96, 1), pltpu.roll(x, 32, 1))


def load_once(t, copies, sems):
    @pl.when(t == 0)
    def _():
        made = [pltpu.make_async_copy(s, d, sems.at[k]) for k, (s, d) in enumerate(copies)]
        for copy in made:
            copy.start()
        for copy in made:
            copy.wait()


def column_blocks(piece, owner, dst, rows, base=0):
    return [
        (
            piece.at[base + rows * j : base + rows * (j + 1), :],
            dst.at[pl.ds(owner * rows, rows), 512 * j : 512 * (j + 1)],
        )
        for j in range(dst.shape[1] // 512)
    ]


def row_block(piece, owner, dst, rows, base=0):
    return [(piece.at[base : base + rows, :], dst.at[pl.ds(owner * rows, rows), :])]


def row_spec(width):
    return "row"


def whole(*shape):
    return "whole"


def anywhere(count):
    return ["any"] * count


def out_shape(*shape, dtype=f32):
    return jax.ShapeDtypeStruct(shape, dtype)


def view(ref, kind, t):
    if kind == "row":
        return ref.at[pl.ds(pl.multiple_of(t * TILE, TILE), TILE), :]
    if kind == "col":
        return ref.at[:, pl.ds(pl.multiple_of(t * TILE, TILE), TILE)]
    if isinstance(kind, tuple):
        width = kind[1]
        return ref.at[:, pl.ds(pl.multiple_of(t * width, width), width)]
    return ref


def block_of(kind, shape, index=None):
    if kind == "any":
        return pl.BlockSpec(memory_space=pl.ANY)
    if kind == "row":
        return pl.BlockSpec((TILE, shape[1]), lambda i, *_: (i, 0))
    if kind == "col":
        return pl.BlockSpec((shape[0], TILE), lambda i, *_: (0, i))
    if isinstance(kind, tuple) and kind[0] == "lane":
        return pl.BlockSpec((shape[0], kind[1]), lambda i, *_: (0, i))
    if isinstance(kind, tuple):
        return pl.BlockSpec((None,) + shape[1:], lambda i, *_: (kind[1],) + (0,) * (len(shape) - 1))
    return pl.BlockSpec(shape, lambda i, *_: (0,) * len(shape))


def run(
    body, name, scalars, inputs, in_specs, out_specs, outs, scratch, grid, flops, count=0, piped=False
):
    size = sum(math.prod(o.shape) * o.dtype.itemsize for o in outs)
    size += sum(math.prod(o.shape) * o.dtype.itemsize for o in inputs)
    lead = len(scalars)
    cost = pl.CostEstimate(flops=int(flops), bytes_accessed=int(size), transcendentals=int(count))
    params = pltpu.CompilerParams(vmem_limit_bytes=LIMIT)
    if piped:
        return pl.pallas_call(
            lambda *refs: body(pl.program_id(0), *refs),
            grid_spec=pltpu.PrefetchScalarGridSpec(
                num_scalar_prefetch=lead,
                grid=grid,
                in_specs=[block_of(k, v.shape) for k, v in zip(in_specs, inputs)],
                out_specs=[block_of(k, v.shape) for k, v in zip(out_specs, outs)],
                scratch_shapes=scratch,
            ),
            out_shape=outs,
            cost_estimate=cost,
            compiler_params=params,
            name=name,
        )(*scalars, *inputs)
    kinds = list(in_specs) + list(out_specs)

    def kernel(*refs):
        held = refs[lead : lead + len(kinds)]
        rest = refs[lead + len(kinds) :]

        def step(t, carry):
            views = [view(ref, kind, t) for ref, kind in zip(held, kinds)]
            body(t, *refs[:lead], *views, *rest)
            return carry

        if grid[0] == 1:
            step(0, 0)
        else:
            lax.fori_loop(0, grid[0], step, 0)

    vmem = pl.BlockSpec(memory_space=pltpu.VMEM)
    place = lambda kind: pl.BlockSpec(memory_space=pl.ANY) if kind == "any" else vmem
    return pl.pallas_call(
        kernel,
        in_specs=[pl.BlockSpec(memory_space=pltpu.SMEM)] * lead + [place(k) for k in in_specs],
        out_specs=[vmem] * len(outs),
        out_shape=outs,
        scratch_shapes=scratch,
        cost_estimate=cost,
        compiler_params=params,
        name=name,
    )(*scalars, *inputs)


def ff_forward_body(t, me, x, norms, *refs, rel, er, sr):
    n = len(rel)
    parts = refs[:n]
    x1, hidden, before, active, w_in, w_out, sems = refs[n:]
    copies = []
    for k, r in enumerate(rel):
        copies += column_blocks(parts[k], me[0] ^ r, w_in, er)
        copies += row_block(parts[k], me[0] ^ r, w_out, sr, 4 * er)
    load_once(t, copies, sems)
    value = x[...].astype(f32)
    normed, _ = normalize(value)
    h = (normed * norms[0:1, :] + norms[1:2, :]).astype(bf16)
    hidden[...] = h
    total = None
    for j in range(w_in.shape[1] // 512):
        cols = slice(512 * j, 512 * (j + 1))
        a = mm(h, w_in[:, cols])
        s = (a * sigmoid(a)).astype(bf16)
        before[:, cols] = a.astype(bf16)
        active[:, cols] = s
        part = mm(s, w_out[cols, :])
        total = part if total is None else total + part
    x1[...] = value + 0.5 * total


def ff_forward(me, x, norms, parts, rel):
    rows, d = x.shape
    er, sr = d // len(rel), 4 * d // len(rel)
    ff = sr * len(rel)
    return run(
        functools.partial(ff_forward_body, rel=rel, er=er, sr=sr),
        "ff_forward",
        (me,),
        (x, norms, *parts),
        [row_spec(d), whole(*norms.shape)] + anywhere(len(rel)),
        [row_spec(d), row_spec(d), row_spec(ff), row_spec(ff)],
        [
            out_shape(rows, d),
            out_shape(rows, d, dtype=bf16),
            out_shape(rows, ff, dtype=bf16),
            out_shape(rows, ff, dtype=bf16),
        ],
        [pltpu.VMEM((d, ff), bf16), pltpu.VMEM((ff, d), bf16), pltpu.SemaphoreType.DMA((5 * len(rel),))],
        (rows // TILE,),
        4 * rows * d * ff,
        rows * ff,
        True,
    )


def qkv_body(t, me, x1, norms, cs, sn, *refs, rel, ar):
    n = len(rel)
    parts = refs[:n]
    hidden, q, k, v, kt, w, sems = refs[n:]
    copies = []
    for j, r in enumerate(rel):
        copies += column_blocks(parts[j], me[0] ^ r, w, ar)
    load_once(t, copies, sems)
    normed, _ = normalize(x1[...])
    h = (normed * norms[2:3, :] + norms[3:4, :]).astype(bf16)
    hidden[...] = h
    c, s = cs[...], sn[...]
    for p in range(4):
        cols = slice(128 * p, 128 * (p + 1))
        a = mm(h, w[:, 128 * p : 128 * (p + 1)])
        q[:, cols] = ((a * c + partner(a) * s).astype(bf16) * 0.125).astype(bf16)
        a = mm(h, w[:, 512 + 128 * p : 512 + 128 * (p + 1)])
        turned = (a * c + partner(a) * s).astype(bf16)
        k[:, cols] = turned
        kt[cols, :] = turned.T
    v[...] = mm(h, w[:, 1024:1536]).astype(bf16)


def qkv(me, x1, norms, cs, sn, parts, rel):
    rows, d = x1.shape
    ar = parts[0].shape[0] // 4
    half = lambda: out_shape(rows, d, dtype=bf16)
    return run(
        functools.partial(qkv_body, rel=rel, ar=ar),
        "query_key_value",
        (me,),
        (x1, norms, cs, sn, *parts),
        [row_spec(d), whole(*norms.shape), row_spec(128), row_spec(128)] + anywhere(len(rel)),
        [row_spec(d)] * 4 + ["col"],
        [half(), half(), half(), half(), out_shape(d, rows, dtype=bf16)],
        [pltpu.VMEM((d, 3 * d), bf16), pltpu.SemaphoreType.DMA((3 * len(rel),))],
        (rows // TILE,),
        6 * rows * d * d,
    )


def attention_body(t, ends, me, q, k, v, x1, *refs, rel, ar, rows):
    n = len(rel)
    parts = refs[:n]
    x2, mixed, lse, w, sems = refs[n:]
    copies = []
    for j, r in enumerate(rel):
        copies += row_block(parts[j], me[0] ^ r, w, ar, 3 * ar)
    load_once(t, copies, sems)
    e = [ends[j] for j in range(4)]
    first = t * TILE
    lo, hi = key_range(first, first + TILE - 1, e, rows)
    sq = seg_of(first + lax.broadcasted_iota(jnp.int32, (1, TILE), 1), e)
    low = lax.broadcasted_iota(jnp.int32, (1, 128), 1) < 64
    zero = jnp.zeros((), bf16)

    def body(start, w_keys):
        keys = pl.ds(start, w_keys)
        same = seg_of(start + lax.broadcasted_iota(jnp.int32, (w_keys, 1), 0), e) == sq
        for p in range(4):
            cols = slice(128 * p, 128 * (p + 1))
            qp, kp, vp = q[:, cols], k[keys, cols], v[keys, cols]
            both = None
            for h in range(2):
                head = 2 * p + h
                pick = low if h == 0 else jnp.logical_not(low)
                s = jnp.where(same, mm_nt(kp, jnp.where(pick, qp, zero)), masked_score)
                top = jnp.max(s, axis=0, keepdims=True)
                expo = jnp.exp(s - top)
                total = col_sum(expo)
                lse[head : head + 1, :] = top + jnp.log(total)
                prob = (expo * (1.0 / total)).astype(bf16)
                part = mm_tn(prob, jnp.where(pick, vp, zero))
                both = part if both is None else both + part
            mixed[:, cols] = both.astype(bf16)

    in_window(lo, hi, rows, body)
    x2[...] = x1[...] + mm(mixed[...], w[...])


def attention(ends, me, q, k, v, x1, parts, rel):
    rows, d = q.shape
    ar = parts[0].shape[0] // 4
    return run(
        functools.partial(attention_body, rel=rel, ar=ar, rows=rows),
        "attention_forward",
        (ends, me),
        (q, k, v, x1, *parts),
        [row_spec(d), whole(rows, d), whole(rows, d), row_spec(d)] + anywhere(len(rel)),
        [row_spec(d), row_spec(d), "col"],
        [out_shape(rows, d), out_shape(rows, d, dtype=bf16), out_shape(HEADS, rows)],
        [pltpu.VMEM((d, d), bf16), pltpu.SemaphoreType.DMA((len(rel),))],
        (rows // TILE,),
        16 * rows * rows * d // 4,
        HEADS * rows * rows,
    )


def attention_back_body(t, ends, q, k, kt, v, do, lse, delta, cs, sn, gp, dqt, *, rows, pairs, base):
    e = [ends[j] for j in range(4)]
    first = pl.multiple_of(t * TILE, TILE)
    lo, hi = key_range(first, first + TILE - 1, e, rows)
    sk = seg_of(first + lax.broadcasted_iota(jnp.int32, (TILE, 1), 0), e)
    low = lax.broadcasted_iota(jnp.int32, (1, 128), 1) < 64
    here = pl.ds(first, TILE)
    zero = jnp.zeros((), bf16)

    @pl.when(t == 0)
    def _():
        dqt[...] = jnp.zeros_like(dqt)

    def body(start, w):
        qs = pl.ds(start, w)
        same = sk == seg_of(start + lax.broadcasted_iota(jnp.int32, (1, w), 1), e)
        for p in range(pairs):
            cols = slice(128 * p, 128 * (p + 1))
            held = slice(128 * (base + p), 128 * (base + p + 1))
            qp, dop = q[qs, held], do[qs, held]
            kp, vp = k[here, held], v[here, held]
            gk, gv = None, None
            for h in range(2):
                head = 2 * p + h
                full = 2 * base + head
                pick = low if h == 0 else jnp.logical_not(low)
                qm, dom = jnp.where(pick, qp, zero), jnp.where(pick, dop, zero)
                hr = slice(64 * head, 64 * (head + 1))
                hk = slice(64 * full, 64 * (full + 1))
                expo = jnp.exp(mm_nt(kp, qm) - lse[full : full + 1, qs])
                prob = jnp.where(same, expo, 0.0)
                ds = (prob * (mm_nt(vp, dom) - delta[full : full + 1, qs])).astype(bf16)
                v_part = mm(prob.astype(bf16), dom)
                k_part = mm(ds, qm)
                dqt[hr, qs] += mm(kt[hk, here], ds)
                gv = v_part if gv is None else gv + v_part
                gk = k_part if gk is None else gk + k_part
            c, s = cs[here, :], sn[here, :]
            gp[here, 128 * (2 * pairs + p) : 128 * (2 * pairs + p + 1)] = gv.astype(bf16)
            turned = gk * c - partner(gk) * s
            gp[here, 128 * (pairs + p) : 128 * (pairs + p + 1)] = turned.astype(bf16)

    in_window(lo, hi, rows, body)

    @pl.when(t == rows // TILE - 1)
    def _():
        c, s = cs[...] * 0.125, sn[...] * 0.125
        for p in range(pairs):
            cols = slice(128 * p, 128 * (p + 1))
            g = dqt[cols, :].T
            gp[:, cols] = (g * c - partner(g) * s).astype(bf16)


def attention_back(ends, q, k, kt, v, do, lse, delta, cs, sn, base, pairs):
    rows, d = q.shape
    wide = 128 * pairs
    return run(
        functools.partial(attention_back_body, rows=rows, pairs=pairs, base=base),
        "attention_backward",
        (ends,),
        (q, k, kt, v, do, lse, delta, cs, sn),
        [whole(rows, d)] * 5
        + [whole(HEADS, rows)] * 2
        + [whole(rows, 128)] * 2,
        [whole(rows, 3 * wide)],
        [out_shape(rows, 3 * wide, dtype=bf16)],
        [pltpu.VMEM((wide, rows), f32)],
        (rows // TILE,),
        10 * rows * rows * d * pairs // 4,
        HEADS * rows * rows * pairs // 4,
    )[0]


def spaced_rows(rows):
    return rows + 6 * GAP


def group_segments(row, ends):
    return seg_of(row + lax.broadcasted_iota(jnp.int32, (8, 128), 0), ends)


def spread_all(groups, first, spans, ends, read, buf):
    def put(s, row, seg, values):
        at = pl.ds(pl.multiple_of(GAP + GAP * s + row, 8), 8)
        keep = seg == s
        for c in range(4):
            buf[c, at, :] = jnp.where(keep, values[c], 0.0)

    def one(g, carry):
        row = 8 * (first + g)
        seg = group_segments(row, ends)
        values = read(g)
        put(spans[0, first + g], row, seg, values)
        put(spans[1, first + g], row, seg, values)
        return carry

    lax.fori_loop(0, groups, one, 0, unroll=4)

    @pl.when(spans[2, 0] > 1)
    def _():
        def rest(g, carry):
            row = 8 * (first + g)
            seg = group_segments(row, ends)
            values = read(g)

            def fix(s, inner):
                put(s, row, seg, values)
                return inner

            return lax.fori_loop(spans[0, first + g] + 1, spans[1, first + g], fix, carry)

        lax.fori_loop(0, groups, rest, 0)


def collect_all(groups, first, spans, ends, buf, out):
    def one(g, carry):
        row = 8 * (first + g)
        seg = group_segments(row, ends)
        lo, hi = spans[0, first + g], spans[1, first + g]
        keep = seg == lo
        a = pl.ds(pl.multiple_of(GAP + GAP * lo + row, 8), 8)
        b = pl.ds(pl.multiple_of(GAP + GAP * hi + row, 8), 8)
        to = pl.ds(pl.multiple_of(8 * g, 8), 8)
        for c in range(4):
            out[to, 128 * c : 128 * (c + 1)] = jnp.where(keep, buf[c, a, :], buf[c, b, :])
        return carry

    lax.fori_loop(0, groups, one, 0, unroll=4)

    @pl.when(spans[2, 0] > 1)
    def _():
        def rest(g, carry):
            row = 8 * (first + g)
            seg = group_segments(row, ends)
            to = pl.ds(pl.multiple_of(8 * g, 8), 8)

            def fix(s, inner):
                a = pl.ds(pl.multiple_of(GAP + GAP * s + row, 8), 8)
                for c in range(4):
                    cols = slice(128 * c, 128 * (c + 1))
                    out[to, cols] = jnp.where(seg == s, buf[c, a, :], out[to, cols])
                return inner

            return lax.fori_loop(spans[0, first + g] + 1, spans[1, first + g], fix, carry)

        lax.fori_loop(0, groups, rest, 0)


CHUNK = 8


def slide(src, taps, dst, rows, shift, reverse):
    span = 8 * CHUNK

    def step(i, carry):
        c = i // ((rows + 4 * GAP) // span)
        base = pl.multiple_of((i - c * ((rows + 4 * GAP) // span)) * span, 8)
        acc = [jnp.zeros((8, 128), f32) for _ in range(CHUNK)]
        for b in range(8):
            loads = [
                src[c, pl.ds(base + (shift + b + 8 * m), 8), :] for m in range(CHUNK + 3)
            ]
            for a in range(4):
                j = 8 * a + b
                j = TAPS - 1 - j if reverse else j
                w = jnp.broadcast_to(taps[c, j : j + 1, :], (8, 128))
                for m in range(CHUNK):
                    acc[m] = acc[m] + w * loads[m + a]
        for m in range(CHUNK):
            dst[c, pl.ds(base + GAP + 8 * m, 8), :] = acc[m]
        return carry

    lax.fori_loop(0, 4 * ((rows + 4 * GAP) // span), step, 0)


def tap_sums(grad, src, out, rows):
    span = 8 * CHUNK

    def lanes(c, carry):
        def step(i, acc):
            acc = list(acc)
            base = pl.multiple_of(i * span, 8)
            g = [grad[c, pl.ds(base + GAP + 8 * m, 8), :] for m in range(CHUNK)]
            for b in range(8):
                loads = [src[c, pl.ds(base + (b + 8 * m), 8), :] for m in range(CHUNK + 3)]
                for a in range(4):
                    j = 8 * a + b
                    for m in range(CHUNK):
                        acc[j] = acc[j] + g[m] * loads[m + a]
            return tuple(acc)

        zeros = tuple(jnp.zeros((8, 128), f32) for _ in range(TAPS))
        acc = lax.fori_loop(0, (rows + 4 * GAP) // span, step, zeros)
        for j in range(TAPS):
            out[c, j : j + 1, :] = col_sum(acc[j])
        return carry

    lax.fori_loop(0, 4, lanes, 0)


def conv_front_body(t, ends, me, spans, x2, norms, taps, *refs, rel, ar, rows):
    n = len(rel)
    parts = refs[:n]
    hidden, gates_out, conv, spaced, stats, glu, answer, w, sems = refs[n:]
    copies = []
    for j, r in enumerate(rel):
        copies += column_blocks(parts[j], me[0] ^ r, w, ar)
    load_once(t, copies, sems)
    e = [ends[j] for j in range(4)]

    @pl.when(t == 0)
    def _():
        spaced[...] = jnp.zeros_like(spaced)

    normed, _ = normalize(x2[...])
    h = (normed * norms[4:5, :] + norms[5:6, :]).astype(bf16)
    hidden[...] = h
    half = mm(h, w[:, :512])
    gate = mm(h, w[:, 512:])
    gates_out[:, :512] = half.astype(bf16)
    gates_out[:, 512:] = gate.astype(bf16)
    glu[...] = half * sigmoid(gate)

    def read(g):
        at = pl.ds(pl.multiple_of(8 * g, 8), 8)
        return [glu[at, 128 * c : 128 * (c + 1)] for c in range(4)]

    spread_all(TILE // 8, t * (TILE // 8), spans, e, read, spaced)

    @pl.when(t == rows // TILE - 1)
    def _():
        slide(spaced, taps, answer, rows, 0, False)
        collect_all(rows // 8, 0, spans, e, answer, conv)
        keep = lax.broadcasted_iota(jnp.int32, (rows, 1), 0) < e[3]
        kept = jnp.where(keep, conv[...], 0.0)
        stats[0:1, :] = col_sum(kept)
        stats[1:2, :] = col_sum(kept * kept)
        stats[2:3, :] = jnp.full((1, 512), e[3], jnp.int32).astype(f32)


def conv_front(ends, me, spans, x2, norms, taps, parts, rel):
    rows, d = x2.shape
    ar = parts[0].shape[0] // 3
    far = spaced_rows(rows)
    return run(
        functools.partial(conv_front_body, rel=rel, ar=ar, rows=rows),
        "gated_convolution",
        (ends, me, spans),
        (x2, norms, taps, *parts),
        [row_spec(d), whole(*norms.shape), whole(4, TAPS, 128)] + anywhere(len(rel)),
        [row_spec(d), row_spec(2 * d), whole(rows, d), whole(4, far, 128), whole(3, d)],
        [
            out_shape(rows, d, dtype=bf16),
            out_shape(rows, 2 * d, dtype=bf16),
            out_shape(rows, d),
            out_shape(4, far, 128),
            out_shape(3, d),
        ],
        [
            pltpu.VMEM((TILE, d), f32),
            pltpu.VMEM((4, far, 128), f32),
            pltpu.VMEM((d, 2 * d), bf16),
            pltpu.SemaphoreType.DMA((2 * len(rel),)),
        ],
        (rows // TILE,),
        8 * rows * d * d,
        rows * d,
    )


def conv_back_body(t, ends, spans, gz, conv, batch, totals, norms, taps, spaced, g_glu, tap_grad, grad, *, rows):
    e = [ends[j] for j in range(4)]
    grad[...] = jnp.zeros_like(grad)
    mean, scale, count = batch[0:1, :], batch[1:2, :], batch[2:3, :]
    bias_all = jnp.sum(totals[:, 0, :], axis=0, keepdims=True) / count
    gain_all = jnp.sum(totals[:, 1, :], axis=0, keepdims=True) / count
    factor = scale * norms[6:7, :]
    per = []
    for c in range(4):
        cols = slice(128 * c, 128 * (c + 1))
        per.append(
            [
                jnp.broadcast_to(v[:, cols], (8, 128))
                for v in (mean, scale, bias_all, gain_all, factor)
            ]
        )

    def read(g):
        row = pl.multiple_of(8 * g, 8)
        keep = row + lax.broadcasted_iota(jnp.int32, (8, 128), 0) < e[3]
        values = []
        for c in range(4):
            cols = slice(128 * c, 128 * (c + 1))
            m, s, b, k, f = per[c]
            zhat = (conv[pl.ds(row, 8), cols] - m) * s
            away = jnp.where(keep, b + zhat * k, 0.0)
            values.append(f * (gz[pl.ds(row, 8), cols] - away))
        return values

    spread_all(rows // 8, 0, spans, e, read, grad)
    slide(grad, taps, g_glu, rows, 1, True)
    tap_sums(grad, spaced, tap_grad, rows)


def conv_back(ends, spans, gz, conv, batch, totals, norms, taps, spaced):
    rows, d = conv.shape
    far = spaced_rows(rows)
    return run(
        functools.partial(conv_back_body, rows=rows),
        "convolution_backward",
        (ends, spans),
        (gz, conv, batch, totals, norms, taps, spaced),
        [whole(rows, d), whole(rows, d), whole(3, d), whole(*totals.shape), whole(*norms.shape)]
        + [whole(4, TAPS, 128), whole(4, far, 128)],
        [whole(4, far, 128), whole(4, TAPS, 128)],
        [out_shape(4, far, 128), out_shape(4, TAPS, 128)],
        [pltpu.VMEM((4, far, 128), f32)],
        (1,),
        12 * rows * d * TAPS * 40,
        rows * d,
    )


def gates_back_body(t, ends, me, spans, g_glu, norms, gates, x2, g3, mixed, *refs, rel, ar, rows):
    n = len(rel)
    parts, heads = refs[:n], refs[n : 2 * n]
    (g_gates, g2, g_attn, g_mixed, delta, sums) = refs[2 * n : 2 * n + 6]
    glu_rows, w, w_heads, sems = refs[2 * n + 6 :]
    copies = []
    for j, r in enumerate(rel):
        copies += column_blocks(parts[j], me[0] ^ r, w, ar)
        copies += row_block(heads[j], me[0] ^ r, w_heads, ar, 3 * ar)
    load_once(t, copies, sems)
    e = [ends[j] for j in range(4)]

    @pl.when(t == 0)
    def _():
        sums[...] = jnp.zeros_like(sums)

    collect_all(TILE // 8, t * (TILE // 8), spans, e, g_glu, glu_rows)
    gg = glu_rows[...]
    sigma = sigmoid(gates[:, 512:].astype(f32))
    first = (gg * sigma).astype(bf16)
    second = (gg * gates[:, :512].astype(f32) * sigma * (1.0 - sigma)).astype(bf16)
    g_gates[:, :512] = first
    g_gates[:, 512:] = second
    g_hidden = mm_nt(first, w[:, :512]) + mm_nt(second, w[:, 512:])
    normed, scale = normalize(x2[...])
    sums[0:1, :] += col_sum(g_hidden * normed)
    sums[1:2, :] += col_sum(g_hidden)
    out = g3[...] + norm_back(g_hidden, norms[4:5, :], normed, scale)
    g2[...] = out
    branch = out.astype(bf16)
    g_attn[...] = branch
    gm = mm_nt(branch, w_heads[...]).astype(bf16)
    g_mixed[...] = gm
    dots = gm.astype(f32) * mixed[...].astype(f32)
    upper = dots.astype(bf16)
    lower = (dots - upper.astype(f32)).astype(bf16)
    head = lax.broadcasted_iota(jnp.int32, (HEADS, 512), 0)
    ones = (lax.broadcasted_iota(jnp.int32, (HEADS, 512), 1) // 64 == head).astype(bf16)
    delta[...] = mm_nt(ones, upper) + mm_nt(ones, lower)


def gates_back(ends, me, spans, g_glu, norms, gates, x2, g3, mixed, parts, heads, rel):
    rows, d = x2.shape
    ar = parts[0].shape[0] // 3
    return run(
        functools.partial(gates_back_body, rel=rel, ar=ar, rows=rows),
        "gates_backward",
        (ends, me, spans),
        (g_glu, norms, gates, x2, g3, mixed, *parts, *heads),
        [whole(*g_glu.shape), whole(*norms.shape), row_spec(2 * d)]
        + [row_spec(d)] * 3
        + anywhere(2 * len(rel)),
        [row_spec(2 * d), row_spec(d), row_spec(d), row_spec(d)]
        + ["col", whole(2, d)],
        [
            out_shape(rows, 2 * d, dtype=bf16),
            out_shape(rows, d),
            out_shape(rows, d, dtype=bf16),
            out_shape(rows, d, dtype=bf16),
            out_shape(HEADS, rows),
            out_shape(2, d),
        ],
        [
            pltpu.VMEM((TILE, d), f32),
            pltpu.VMEM((d, 2 * d), bf16),
            pltpu.VMEM((d, d), bf16),
            pltpu.SemaphoreType.DMA((3 * len(rel),)),
        ],
        (rows // TILE,),
        6 * rows * d * d,
        rows * d,
    )


def rear_body(t, ends, me, conv, totals, x2, cot, norms, *refs, rel, ar, er, sr):
    n = len(rel)
    points, ffs = refs[:n], refs[n : 2 * n]
    (y, g_third, g_zed, wact, branch_out, hidden, active, g_before, g_out, sums, batch) = refs[2 * n : 2 * n + 11]
    w_point, w_in, w_out, slope, sems = refs[2 * n + 11 :]
    copies = []
    for j, r in enumerate(rel):
        copies += row_block(points[j], me[0] ^ r, w_point, ar, 2 * ar)
        copies += column_blocks(ffs[j], me[0] ^ r, w_in, er)
        copies += row_block(ffs[j], me[0] ^ r, w_out, sr, 4 * er)
    load_once(t, copies, sems)

    @pl.when(t == 0)
    def _():
        sums[...] = jnp.zeros_like(sums)
        total = jnp.sum(totals[...], axis=0)
        count = total[2:3, :]
        mean = total[0:1, :] / count
        batch[0:1, :] = mean
        batch[1:2, :] = lax.rsqrt(total[1:2, :] / count - mean * mean + batch_epsilon)
        batch[2:3, :] = count

    zhat = (conv[...] - batch[0:1, :]) * batch[1:2, :]
    zed = zhat * norms[6:7, :] + norms[7:8, :]
    sigma = sigmoid(zed)
    wa = (zed * sigma).astype(bf16)
    wact[...] = wa
    zed_slope = slope_of(zed, sigma)
    third = x2[...] + mm(wa, w_point[...])
    normed, scale = normalize(third)
    h = (normed * norms[8:9, :] + norms[9:10, :]).astype(bf16)
    hidden[...] = h
    total = None
    for j in range(w_in.shape[1] // 512):
        cols = slice(512 * j, 512 * (j + 1))
        a = mm(h, w_in[:, cols])
        sg = sigmoid(a)
        s = (a * sg).astype(bf16)
        active[:, cols] = s
        slope[:, cols] = slope_of(a, sg)
        part = mm(s, w_out[cols, :])
        total = part if total is None else total + part
    fourth = third + 0.5 * total
    last, last_scale = normalize(fourth)
    keep = t * TILE + lax.broadcasted_iota(jnp.int32, (TILE, 1), 0) < ends[3]
    y[...] = jnp.where(keep, last * norms[10:11, :] + norms[11:12, :], 0.0).astype(bf16)
    g_y = jnp.where(keep, cot[...].astype(f32), 0.0)
    sums[0:1, :] += col_sum(g_y * last)
    sums[1:2, :] += col_sum(g_y)
    g_fourth = norm_back(g_y, norms[10:11, :], last, last_scale)
    go = (0.5 * g_fourth).astype(bf16)
    g_out[...] = go
    g_hidden = None
    for j in range(w_in.shape[1] // 512):
        cols = slice(512 * j, 512 * (j + 1))
        gb = (mm_nt(go, w_out[cols, :]) * slope[:, cols]).astype(bf16)
        g_before[:, cols] = gb
        part = mm_nt(gb, w_in[:, cols])
        g_hidden = part if g_hidden is None else g_hidden + part
    sums[2:3, :] += col_sum(g_hidden * normed)
    sums[3:4, :] += col_sum(g_hidden)
    g3 = g_fourth + norm_back(g_hidden, norms[8:9, :], normed, scale)
    g_third[...] = g3
    branch = g3.astype(bf16)
    branch_out[...] = branch
    gz = mm_nt(branch, w_point[...]) * zed_slope
    g_zed[...] = gz
    sums[4:5, :] += col_sum(gz)
    sums[5:6, :] += col_sum(gz * zhat)


def rear(ends, me, conv, totals, x2, cot, norms, points, ffs, rel):
    rows, d = x2.shape
    ar = points[0].shape[0] // 3
    ff = 4 * d
    er, sr = d // len(rel), ff // len(rel)
    return run(
        functools.partial(rear_body, rel=rel, ar=ar, er=er, sr=sr),
        "norm_feed_forward_and_back",
        (ends, me),
        (conv, totals, x2, cot, norms, *points, *ffs),
        [row_spec(d), whole(*totals.shape), row_spec(d), row_spec(d), whole(*norms.shape)]
        + anywhere(2 * len(rel)),
        [row_spec(d)] * 6 + [row_spec(ff), row_spec(ff), row_spec(d), whole(6, d), whole(3, d)],
        [
            out_shape(rows, d, dtype=bf16),
            out_shape(rows, d),
            out_shape(rows, d),
            out_shape(rows, d, dtype=bf16),
            out_shape(rows, d, dtype=bf16),
            out_shape(rows, d, dtype=bf16),
            out_shape(rows, ff, dtype=bf16),
            out_shape(rows, ff, dtype=bf16),
            out_shape(rows, d, dtype=bf16),
            out_shape(6, d),
            out_shape(3, d),
        ],
        [
            pltpu.VMEM((d, d), bf16),
            pltpu.VMEM((d, ff), bf16),
            pltpu.VMEM((ff, d), bf16),
            pltpu.VMEM((TILE, ff), f32),
            pltpu.SemaphoreType.DMA((6 * len(rel),)),
        ],
        (rows // TILE,),
        rows * d * (8 * ff + 4 * d),
        rows * ff,
        True,
    )


def qkv_back_body(t, me, ga, gb, x1, g2, norms, *refs, rel, ar):
    n = len(rel)
    attn = refs[:n]
    g1, g_out, sums, w, sems = refs[n:]
    copies = []
    for j, r in enumerate(rel):
        copies += column_blocks(attn[j], me[0] ^ r, w, ar)
    load_once(t, copies, sems)

    @pl.when(t == 0)
    def _():
        sums[...] = jnp.zeros_like(sums)

    g_hidden = None
    for z in range(3):
        for half, g in enumerate((ga, gb)):
            cols = slice(512 * z + 256 * half, 512 * z + 256 * (half + 1))
            part = mm_nt(g[:, 256 * z : 256 * (z + 1)], w[:, cols])
            g_hidden = part if g_hidden is None else g_hidden + part
    normed, scale = normalize(x1[...])
    sums[0:1, :] += col_sum(g_hidden * normed)
    sums[1:2, :] += col_sum(g_hidden)
    out = g2[...] + norm_back(g_hidden, norms[2:3, :], normed, scale)
    g1[...] = out
    g_out[...] = (0.5 * out).astype(bf16)


def qkv_back(me, ga, gb, x1, g2, norms, attn, rel):
    rows, d = x1.shape
    ar = d // len(rel)
    return run(
        functools.partial(qkv_back_body, rel=rel, ar=ar),
        "query_key_value_backward",
        (me,),
        (ga, gb, x1, g2, norms, *attn),
        [row_spec(3 * d // 2)] * 2 + [row_spec(d)] * 2 + [whole(*norms.shape)] + anywhere(len(rel)),
        [row_spec(d), row_spec(d), whole(2, d)],
        [out_shape(rows, d), out_shape(rows, d, dtype=bf16), out_shape(2, d)],
        [pltpu.VMEM((d, 3 * d), bf16), pltpu.SemaphoreType.DMA((3 * len(rel),))],
        (rows // TILE,),
        6 * rows * d * d,
    )


def ff_back_body(t, me, g1, go, x, before, norms, *refs, rel, er, sr):
    n = len(rel)
    parts = refs[:n]
    g_frames, g_before, sums, w_in, w_out, sems = refs[n:]
    copies = []
    for j, r in enumerate(rel):
        copies += column_blocks(parts[j], me[0] ^ r, w_in, er)
        copies += row_block(parts[j], me[0] ^ r, w_out, sr, 4 * er)
    load_once(t, copies, sems)

    @pl.when(t == 0)
    def _():
        sums[...] = jnp.zeros_like(sums)

    out = go[...]
    g_hidden = None
    for j in range(w_in.shape[1] // 512):
        cols = slice(512 * j, 512 * (j + 1))
        a = before[:, cols].astype(f32)
        gb = (mm_nt(out, w_out[cols, :]) * slope_of(a, sigmoid(a))).astype(bf16)
        g_before[:, cols] = gb
        part = mm_nt(gb, w_in[:, cols])
        g_hidden = part if g_hidden is None else g_hidden + part
    normed, scale = normalize(x[...].astype(f32))
    sums[0:1, :] += col_sum(g_hidden * normed)
    sums[1:2, :] += col_sum(g_hidden)
    g_frames[...] = g1[...] + norm_back(g_hidden, norms[0:1, :], normed, scale)


def ff_back(me, g1, go, x, before, norms, parts, rel):
    rows, d = x.shape
    ff = 4 * d
    er, sr = d // len(rel), ff // len(rel)
    return run(
        functools.partial(ff_back_body, rel=rel, er=er, sr=sr),
        "feed_forward_backward",
        (me,),
        (g1, go, x, before, norms, *parts),
        [row_spec(d), row_spec(d), row_spec(d), row_spec(ff), whole(*norms.shape)] + anywhere(len(rel)),
        [row_spec(d), row_spec(ff), whole(2, d)],
        [out_shape(rows, d), out_shape(rows, ff, dtype=bf16), out_shape(2, d)],
        [
            pltpu.VMEM((d, ff), bf16),
            pltpu.VMEM((ff, d), bf16),
            pltpu.SemaphoreType.DMA((5 * len(rel),)),
        ],
        (rows // TILE,),
        4 * rows * d * ff,
        rows * ff,
        True,
    )


def place_owners(me, tile, keep, send, base, height, owners, first):
    for k in range(owners):
        owner = first + k
        rows = tile[k * height : (k + 1) * height, :]
        mine = ((owner ^ me[0]) & 1) == 0

        @pl.when(mine)
        def _(rows=rows, owner=owner):
            keep[owner >> 1, pl.ds(base, height), :] = rows

        @pl.when(jnp.logical_not(mine))
        def _(rows=rows, owner=owner):
            send[owner >> 1, pl.ds(base, height), :] = rows


def weight_grad_body(t, me, *refs, fs, parts, n1, n2):
    refs = list(refs)
    first = [refs.pop(0) for _ in range(1 + parts)] if n1 else None
    second = [refs.pop(0) for _ in range(2)] if n2 else None
    keep, send = refs.pop(0), refs.pop(0)
    er = 512 // fs
    if n1:
        base = pl.multiple_of(t * er, er)
        tiles = [mm_tn(first[0][...], ref[...]).astype(bf16) for ref in first[1:]]
        tile = tiles[0] if parts == 1 else jnp.concatenate(tiles, axis=1)
        place_owners(me, tile, keep, send, base, er, fs, 0)
    if n2:
        sr = 512 * n2 // fs
        per = max(1, 512 // sr)

        def one(block):
            tile = mm_tn(second[0][...], second[1][...]).astype(bf16)
            place_owners(me, tile, keep, send, n1 * er, sr, per, block * per)

        if n1 in (0, n2):
            one(t)
        else:
            pl.when(t == 0)(lambda: one(0))


def weight_grad(name, me, fs, first=None, second=None):
    inputs, specs = [], []
    n1 = n2 = parts = 0
    if first:
        h, gs = first
        rows, parts = h.shape[0], len(gs)
        wide = 512 // parts
        n1 = gs[0].shape[1] // wide
        inputs += [h, *gs]
        specs += [whole(rows, 512)] + [("lane", wide)] * parts
    if second:
        s, o = second
        rows = s.shape[0]
        n2 = s.shape[1] // 512
        inputs += [s, o]
        stepped = n1 in (0, n2)
        specs += [("lane", 512) if stepped else "whole", whole(rows, 512)]
    height = (n1 + n2) * 512 // fs
    return run(
        functools.partial(weight_grad_body, fs=fs, parts=parts, n1=n1, n2=n2),
        name,
        (me,),
        inputs,
        specs,
        [whole(fs // 2, height, 512)] * 2,
        [out_shape(fs // 2, height, 512, dtype=bf16)] * 2,
        [],
        (n1 or n2,),
        2 * rows * 512 * 512 * (n1 + n2),
        0,
        n1 == n2,
    )


def join(*pairs):
    return tuple(jnp.concatenate(list(side), axis=1) for side in zip(*pairs))


def bits_of(size):
    return int(size).bit_length() - 1


def swap(value, axis, size, mask):
    return lax.ppermute(value, axis, [(k, k ^ mask) for k in range(size)])


def relative(fs):
    rel = [0]
    for bit in reversed(range(bits_of(fs))):
        rel = rel + [r ^ (1 << bit) for r in rel]
    return tuple(rel)


def first_part(own, fs):
    parts = [own]
    for bit in reversed(range(1, bits_of(fs))):
        parts = parts + [swap(part, "fsdp", fs, 1 << bit) for part in parts]
    return parts


def second_part(parts, fs):
    return parts + [swap(part, "fsdp", fs, 1) for part in parts]


def sum_of(parts):
    total = parts[0].astype(f32)
    for part in parts[1:]:
        total = total + part.astype(f32)
    return total.astype(bf16)


class Chain:
    def __init__(self, pair, fs, dp):
        keep, send = pair
        self.fs, self.dp = fs, dp
        self.me, self.pack = lax.axis_index("fsdp"), lax.axis_index("dp")
        zero = jnp.int32(0)
        self.at, self.size = [zero, zero], list(keep.shape[:2])
        self.parts = [(keep, zero, zero)]
        self.stages = [("fsdp", bit, "halve") for bit in reversed(range(1, bits_of(fs)))]
        self.stages += [("dp", bit, "add" if bit else "halve") for bit in range(bits_of(dp))]
        self.stages.append(("dp", 0, "join"))
        self.flight = swap(send, "fsdp", fs, 1)
        self.whole = None

    def take(self, y, r):
        shape = (self.size[0], self.size[1], 512)
        return sum_of(
            [lax.dynamic_slice(part, (y - y0, r - r0, 0), shape) for part, y0, r0 in self.parts]
        )

    def hold(self, *tokens):
        self.flight = after(self.flight, *tokens)

    def advance(self):
        if not self.stages:
            return None
        self.parts.append((self.flight, *self.at))
        axis, bit, kind = self.stages.pop(0)
        size, index = (self.fs, self.me) if axis == "fsdp" else (self.dp, self.pack)
        side = (index >> bit) & 1
        if kind == "halve":
            dim = 0 if axis == "fsdp" else 1
            base = self.at[dim]
            self.size[dim] //= 2
            self.at[dim] = base + (1 - side) * self.size[dim]
            send = self.take(*self.at)
            self.at[dim] = base + side * self.size[dim]
        else:
            send = self.take(*self.at)
            self.parts = [(send, *self.at)]
        self.flight = swap(send, axis, size, 1 << bit)
        return send

    def result(self):
        while self.stages:
            self.advance()
        mine, other = self.parts[0][0].reshape(-1, 512), self.flight.reshape(-1, 512)
        pair = [jnp.concatenate([mine, other], axis=0), jnp.concatenate([other, mine], axis=0)]
        return jnp.where((self.pack & 1) == 0, *pair)


def after(value, *tokens):
    tokens = [token for token in tokens if token is not None]
    return lax.optimization_barrier((value, *tokens))[0]


def from_everyone(rows):
    axes = ("dp", "fsdp")
    count = lax.axis_size(axes)
    spread = jnp.broadcast_to(rows[None], (count,) + rows.shape)
    return lax.all_to_all(spread, axes, 0, 0, tiled=True)


def to_rows(block):
    r, c = block.shape
    k = c // 512
    return block.reshape(r, k, 512).swapaxes(0, 1).reshape(k * r, 512)


def from_rows(rows, r, c):
    k = c // 512
    return rows.reshape(k, r, 512).swapaxes(0, 1).reshape(r, c)


def pack_body(t, a, b, out, *, n, er):
    for j in range(n):
        out[er * j : er * (j + 1), :] = a[:, 512 * j : 512 * (j + 1)].astype(bf16)
    out[er * n :, :] = b[...].astype(bf16)


def pack(name, a, b, index=None):
    er, n = a.shape[-2], a.shape[-1] // 512
    sr = b.shape[-2]
    return run(
        functools.partial(pack_body, n=n, er=er),
        name,
        (),
        (a, b),
        ["whole" if index is None else ("stack", index)] * 2,
        ["whole"],
        [out_shape(n * er + sr, 512, dtype=bf16)],
        [],
        (1,),
        er * n * 1024,
        0,
        True,
    )[0]


def adam_body(*refs):
    ga, gb = refs[0][...], refs[1][...]
    outs = refs[-6:]
    for ref, grad, to in ((refs[2:5], ga, outs[:3]), (refs[5:8], gb, outs[3:])):
        new = adam_update(ref[0][...], ref[1][...], ref[2][...], grad.astype(f32), decay_rate)
        for place, value in zip(to, new):
            place[...] = value


def adam_single_body(*refs):
    outs = refs[-3:]
    new = adam_update(refs[1][...], refs[2][...], refs[3][...], refs[0][...].astype(f32), decay_rate)
    for place, value in zip(outs, new):
        place[...] = value


def adam_single(name, grad, state, by_row, index, into):
    height, width = state[0].shape[-2:]
    n = 4
    block = (height // n, width) if by_row else (height, width // n)
    spec = pl.BlockSpec((None,) + block, lambda i: (index, i, 0) if by_row else (index, 0, i))
    return pl.pallas_call(
        adam_single_body,
        grid=(n,),
        in_specs=[pl.BlockSpec(block, lambda i: (i, 0))] + [spec] * 3 + [pl.BlockSpec(memory_space=pl.ANY)] * 3,
        out_specs=[spec] * 3,
        out_shape=[out_shape(*v.shape) for v in state],
        input_output_aliases={4 + j: j for j in range(3)},
        cost_estimate=pl.CostEstimate(
            flops=20 * height * width, bytes_accessed=26 * height * width, transcendentals=height * width
        ),
        name=name,
    )(grad, *state, *into)


def adam_pair(name, grad, first, second, steps, index=None, into=None):
    er, n = first[0].shape[-2], first[0].shape[-1] // 512
    sr = second[0].shape[-2]
    part = sr // n if steps else sr
    lead = () if index is None else (None,)
    at = () if index is None else (index,)
    spec_a = pl.BlockSpec(lead + (er, 512), lambda i: at + (0, i))
    spec_b = pl.BlockSpec(lead + (part, 512), lambda i: at + ((i, 0) if steps else (0, 0)))
    grad_a = pl.BlockSpec((er, 512), lambda i: (i, 0))
    grad_b = pl.BlockSpec((part, 512), lambda i: (n * er // part + (i if steps else 0), 0))
    inputs = [grad, grad, *first, *second]
    specs = [grad_a, grad_b] + [spec_a] * 3 + [spec_b] * 3
    alias = {}
    if into is not None:
        alias = {len(inputs) + j: j for j in range(6)}
        inputs += list(into)
        specs += [pl.BlockSpec(memory_space=pl.ANY)] * 6
    return pl.pallas_call(
        adam_body,
        grid=(n,),
        in_specs=specs,
        out_specs=[spec_a] * 3 + [spec_b] * 3,
        out_shape=[out_shape(*v.shape) for v in (*first, *second)],
        input_output_aliases=alias,
        cost_estimate=pl.CostEstimate(
            flops=20 * er * 512 * n, bytes_accessed=26 * (er * n + sr) * 512, transcendentals=er * 512 * n
        ),
        name=name,
    )(*inputs)


def adam_update(master, first, second_block, grad, decay):
    first_new = beta_first * first + (1.0 - beta_first) * grad
    second_new = beta_second * second_block + (1.0 - beta_second) * grad * grad
    first_hat = first_new / (1.0 - beta_first**STEP)
    second_hat = second_new / (1.0 - beta_second**STEP)
    master_new = master - learn_rate * (
        first_hat / (jnp.sqrt(second_hat) + adam_epsilon) + decay * master
    )
    return (master_new, first_new, second_new)


def moments_only(first, second_block, grad):
    first_new = beta_first * first + (1.0 - beta_first) * grad
    second_new = beta_second * second_block + (1.0 - beta_second) * grad * grad
    return (first_new, second_new)


def rotary_tables(position, half):
    freq = jnp.exp(jnp.arange(half, dtype=f32) * (-math.log(10000.0) / half))
    angle = position.astype(f32)[:, None] * freq[None, :]
    cosine, sine = jnp.cos(angle), jnp.sin(angle)
    return (
        jnp.concatenate([cosine] * 4, axis=1),
        jnp.concatenate([-sine, sine, -sine, sine], axis=1),
    )


def per_device(
    frames,
    cotangent,
    lengths,
    expand,
    expand_first,
    expand_second,
    shrink,
    shrink_first,
    shrink_second,
    attend,
    attend_first,
    attend_second,
    heads_out,
    heads_out_first,
    heads_out_second,
    pointwise,
    pointwise_first,
    pointwise_second,
    pointwise_out,
    pointwise_out_first,
    pointwise_out_second,
    depthwise,
    depthwise_first,
    depthwise_second,
    norm_table,
    norm_table_first,
    norm_table_second,
):
    fs, dp = (lax.axis_size("fsdp"), lax.axis_size("dp"))
    rel = relative(fs)
    er, sr, ar = expand.shape[1], shrink.shape[1], attend.shape[0]
    dr = depthwise.shape[1]
    device = lax.axis_index("fsdp")
    me = device.astype(jnp.int32).reshape(1)
    ends = jnp.cumsum(lengths[0, :4]).astype(jnp.int32)
    rows, width = frames.shape

    early_own = pack("pack_early", expand, shrink, 0)
    ff_zero = first_part(early_own, fs)
    small = jnp.concatenate([after(depthwise, early_own), norm_table], axis=0).astype(bf16)
    tiny_rows = small.shape[0]
    small_parts = second_part(first_part(small, fs), fs)
    places = jnp.arange(rows, dtype=jnp.int32)
    segment = jnp.sum((places[:, None] >= ends[None, :]).astype(jnp.int32), axis=1)
    starts = jnp.concatenate([jnp.zeros((1,), jnp.int32), ends])
    pick = (segment[:, None] == jnp.arange(5, dtype=jnp.int32)[None, :]).astype(jnp.int32)
    position = places - jnp.sum(pick * starts[None, :], axis=1)
    lo, hi = segment[::8], segment[7::8]
    spans = jnp.stack([lo, hi, jnp.broadcast_to(jnp.max(hi - lo), lo.shape)])
    cs, sn = rotary_tables(position, width // HEADS // 2)

    attn_own = pack("pack_attn", attend, heads_out)
    conv_own = pack("pack_conv", pointwise, pointwise_out)
    late_own = pack("pack_late", expand, shrink, 1)
    small_full = jnp.zeros((fs, tiny_rows, dr), bf16)
    for k, r in enumerate(rel):
        small_full = lax.dynamic_update_slice_in_dim(small_full, small_parts[k][None], device ^ r, 0)
    small_full = small_full.swapaxes(0, 1).reshape(tiny_rows, fs * dr).astype(f32)
    norms = small_full[TAPS:]
    taps = small_full[:TAPS].reshape(TAPS, width // 128, 128).swapaxes(0, 1)
    ff_zero = [ff_zero[0]] + [after(part, attn_own, conv_own, late_own, cs, sn, norms, taps) for part in ff_zero[1:]]
    attn_parts = first_part(after(attn_own, *ff_zero), fs)
    ff_zero = second_part(ff_zero, fs)


    x1, hidden_zero, before_zero, active_zero = ff_forward(
        me, frames, norms, ff_zero, rel
    )
    attn_parts = [after(part, x1) for part in attn_parts]
    conv_parts = first_part(after(conv_own, *attn_parts), fs)
    attn_parts = second_part(attn_parts, fs)
    hidden_attn, q, k, v, kt = qkv(me, x1, norms, cs, sn, attn_parts, rel)
    conv_parts = [after(part, q) for part in conv_parts]
    ff_one = first_part(after(late_own, *conv_parts), fs)
    conv_parts = second_part(conv_parts, fs)
    x2, mixed, lse = attention(ends, me, after(q, *conv_parts), k, v, x1, attn_parts, rel)
    hidden_conv, gates, conv, spaced, stats = conv_front(ends, me, spans, x2, norms, taps, conv_parts, rel)
    ff_one = second_part([after(part, stats) for part in ff_one], fs)
    totals = from_everyone(stats)
    (
        layer_output,
        g_third,
        g_zed,
        wact,
        g_branch,
        hidden_one,
        active_one,
        g_before_one,
        g_out_one,
        rear_sums,
        batch,
    ) = rear(ends, me, conv, totals, x2, cotangent, norms, conv_parts, ff_one, rel)
    back_totals = from_everyone(rear_sums[4:6])
    late_pair = weight_grad(
        "weight_grad_late", me, fs, (hidden_one, (g_before_one,)), (active_one, g_out_one)
    )
    late = Chain((late_pair[0], after(late_pair[1], back_totals)), fs, dp)
    g_glu, tap_grad = conv_back(ends, spans, after(g_zed, late_pair[1]), conv, batch, back_totals, norms, taps, spaced)
    g_glu = after(g_glu, late.advance())
    g_gates, g_second, g_attn, g_mixed, delta, conv_sums = gates_back(
        ends, me, spans, g_glu, norms, gates, x2, g_third, mixed, conv_parts, attn_parts, rel
    )
    conv_pair = weight_grad("weight_grad_conv", me, fs, (hidden_conv, (g_gates,)), (wact, g_branch))
    middle = Chain(conv_pair, fs, dp)
    first_half = attention_back(
        ends, q, k, kt, v, after(g_mixed, conv_pair[1]), lse, delta, cs, sn, 0, 2
    )
    late.hold(first_half)
    middle.hold(first_half)
    tokens = (late.advance(), middle.advance(), first_half)
    second_half = attention_back(ends, q, k, kt, v, after(g_mixed, *tokens), lse, delta, cs, sn, 2, 2)
    late.hold(second_half)
    middle.hold(second_half)
    first_half = after(first_half, late.advance(), middle.advance())
    attn_pair = weight_grad(
        "weight_grad_attn", me, fs, (hidden_attn, (first_half, second_half)), (mixed, g_attn)
    )
    attn = Chain(attn_pair, fs, dp)
    g_first, g_out_zero, qkv_sums = qkv_back(
        me, after(first_half, attn_pair[1]), second_half, x1, g_second, norms, attn_parts, rel
    )
    for chain in (late, middle, attn):
        chain.hold(g_first)
    tokens = (late.advance(), middle.advance(), attn.advance())
    out_pair = weight_grad(
        "weight_grad_shrink", me, fs, None, (active_zero, after(g_out_zero, *tokens))
    )
    early_out = Chain(out_pair, fs, dp)
    middle.hold(out_pair[1])
    frames_grad, g_before_zero, ff_sums = ff_back(
        me, g_first, after(g_out_zero, out_pair[1], middle.advance()), frames, before_zero, norms, ff_zero, rel
    )
    for chain in (late, middle, attn, early_out):
        chain.hold(g_before_zero)
    tokens = (late.advance(), attn.advance(), early_out.advance(), middle.advance())
    early_in = weight_grad(
        "weight_grad_expand", me, fs, (hidden_zero, (after(g_before_zero, *tokens),))
    )
    grad_norms = jnp.concatenate(
        [
            ff_sums,
            qkv_sums,
            conv_sums,
            rear_sums[5:6],
            rear_sums[4:5],
            rear_sums[2:4],
            rear_sums[0:2],
        ]
    )
    grad_kernel = tap_grad.swapaxes(0, 1).reshape(TAPS, width)
    small_grad = jnp.concatenate([grad_kernel, grad_norms], axis=0).astype(bf16)
    small_grad = small_grad.reshape(tiny_rows, fs, dr).swapaxes(0, 1)
    small_size = tiny_rows * dr
    small_pad = -small_size % (512 * dp)
    small_grad = jnp.pad(small_grad.reshape(fs, small_size), ((0, 0), (0, small_pad)))
    small_grad = small_grad.reshape(fs // 2, 2, -1, 512).swapaxes(0, 1)
    core = device & 1
    small_pair = (
        lax.dynamic_index_in_dim(small_grad, core, 0, False),
        lax.dynamic_index_in_dim(small_grad, 1 - core, 0, False),
    )
    tail_pair = join(early_in, small_pair)
    tail = Chain(tail_pair, fs, dp)
    for chain in (late, middle, attn, early_out):
        chain.hold(tail_pair[1])
    sent = tail.advance()
    for chain in (late, middle, attn, early_out):
        chain.hold(sent)
    attn.advance()
    early_out.advance()
    red_late, red_conv = late.result(), middle.result()
    expands = (expand, expand_first, expand_second)
    shrinks = (shrink, shrink_first, shrink_second)
    new_late = adam_pair("adam_late", red_late, expands, shrinks, True, 1)
    new_conv = adam_pair(
        "adam_conv",
        red_conv,
        (pointwise, pointwise_first, pointwise_second),
        (pointwise_out, pointwise_out_first, pointwise_out_second),
        False,
    )
    tail.hold(new_late[0])
    sent = tail.advance()
    attn.hold(sent)
    early_out.hold(sent)
    tail.hold(attn.advance(), early_out.advance(), new_conv[0])
    sent = tail.advance()
    attn.hold(sent)
    early_out.hold(sent)
    tail.hold(attn.advance(), early_out.advance())
    sent = tail.advance()
    early_out.hold(sent)
    tail.hold(early_out.advance())
    new_attn = adam_pair(
        "adam_attn",
        after(attn.result(), sent),
        (attend, attend_first, attend_second),
        (heads_out, heads_out_first, heads_out_second),
        False,
    )
    tail.hold(new_attn[0])
    sent = tail.advance()
    red_out = after(early_out.result(), sent)
    new_shrink = adam_single("adam_shrink", red_out, shrinks, True, 0, new_late[3:])
    tail.hold(new_shrink[0])
    red_in = tail.result()
    new_expand = adam_single("adam_expand", red_in, expands, False, 0, new_late[:3])
    red_small = red_in[4 * er :].reshape(-1)[:small_size].reshape(tiny_rows, dr).astype(f32)
    new_taps = adam_update(depthwise, depthwise_first, depthwise_second, red_small[:TAPS], decay_rate)
    red_norms = red_small[TAPS:]
    new_norms = moments_only(norm_table_first, norm_table_second, red_norms)
    return (
        layer_output,
        frames_grad,
        *new_expand,
        *new_shrink,
        *new_attn,
        *new_conv,
        *new_taps,
        red_norms,
        *new_norms,
    )


def solution(mesh):
    return jax.shard_map(
        per_device,
        mesh=mesh,
        in_specs=(
            P(("dp", "fsdp"), None),
            P(("dp", "fsdp"), None),
            P(("dp", "fsdp"), None),
            P(None, "fsdp", None),
            P(None, "fsdp", None),
            P(None, "fsdp", None),
            P(None, "fsdp", None),
            P(None, "fsdp", None),
            P(None, "fsdp", None),
            P("fsdp", None),
            P("fsdp", None),
            P("fsdp", None),
            P("fsdp", None),
            P("fsdp", None),
            P("fsdp", None),
            P("fsdp", None),
            P("fsdp", None),
            P("fsdp", None),
            P("fsdp", None),
            P("fsdp", None),
            P("fsdp", None),
            P(None, "fsdp"),
            P(None, "fsdp"),
            P(None, "fsdp"),
            P(None, "fsdp"),
            P(None, "fsdp"),
            P(None, "fsdp"),
        ),
        out_specs=(
            P(("dp", "fsdp"), None),
            P(("dp", "fsdp"), None),
            P(None, "fsdp", None),
            P(None, "fsdp", None),
            P(None, "fsdp", None),
            P(None, "fsdp", None),
            P(None, "fsdp", None),
            P(None, "fsdp", None),
            P("fsdp", None),
            P("fsdp", None),
            P("fsdp", None),
            P("fsdp", None),
            P("fsdp", None),
            P("fsdp", None),
            P("fsdp", None),
            P("fsdp", None),
            P("fsdp", None),
            P("fsdp", None),
            P("fsdp", None),
            P("fsdp", None),
            P(None, "fsdp"),
            P(None, "fsdp"),
            P(None, "fsdp"),
            P(None, "fsdp"),
            P(None, "fsdp"),
            P(None, "fsdp"),
        ),
        check_vma=False,
    )
```

```python
import functools
import math

import jax
import jax.numpy as jnp
from jax import lax
from jax.experimental import pallas as pl
from jax.experimental.pallas import tpu as pltpu
from jax.sharding import PartitionSpec as P

HEADS = 8
STEP = 10
TAPS = 32
GAP = 16
LIMIT = 48 * 1024 * 1024
TILE = 256
WINDOWS = (512, 768)
BIG_TILE = 512
BIG = ("ff_forward", "norm_feed_forward_and_back")

norm_epsilon = 1e-05
batch_epsilon = 1e-05
masked_score = -1000000000.0
learn_rate = 0.1
beta_first = 0.9
beta_second = 0.98
adam_epsilon = 1e-08
decay_rate = 0.01

f32, bf16 = jnp.float32, jnp.bfloat16


def mm(a, b):
    return jnp.dot(a, b, preferred_element_type=f32)


def mm_nt(a, b):
    return lax.dot_general(a, b, (((1,), (1,)), ((), ())), preferred_element_type=f32)


def mm_tn(a, b):
    return lax.dot_general(a, b, (((0,), (0,)), ((), ())), preferred_element_type=f32)


def normalize(value):
    center = value - jnp.mean(value, axis=-1, keepdims=True)
    scale = lax.rsqrt(jnp.mean(center * center, axis=-1, keepdims=True) + norm_epsilon)
    return center * scale, scale


def norm_back(grad_out, gain, normed, scale):
    grad_norm = grad_out * gain
    return scale * (
        grad_norm
        - jnp.mean(grad_norm, axis=-1, keepdims=True)
        - normed * jnp.mean(grad_norm * normed, axis=-1, keepdims=True)
    )


def col_sum(value):
    return jnp.sum(value, axis=0, keepdims=True)


def sigmoid(value):
    return 0.5 * jnp.tanh(0.5 * value) + 0.5


def slope_of(value, sigma):
    return sigma * (1.0 + value * (1.0 - sigma))


def seg_of(places, ends):
    s = (places >= ends[0]).astype(jnp.int32)
    for j in range(1, 4):
        s = s + (places >= ends[j]).astype(jnp.int32)
    return s


def pick_last(values, count):
    out = values[0]
    for j in range(1, len(values)):
        out = jnp.where(count >= j, values[j], out)
    return out


def key_range(first, last, ends, rows):
    starts = [jnp.int32(0)] + ends
    stops = ends + [jnp.int32(rows)]
    return pick_last(starts, seg_of(first, ends)), pick_last(stops, seg_of(last, ends))


def in_window(lo, hi, rows, body):
    begin = (lo // 128) * 128
    done = jnp.bool_(False)
    for w in sorted({w for w in WINDOWS if w < rows} | {rows}):
        start = jnp.minimum(begin, rows - w)
        fits = jnp.logical_and(hi <= start + w, jnp.logical_not(done))

        @pl.when(fits)
        def _(start=start, w=w):
            body(pl.multiple_of(start, 128), w)

        done = jnp.logical_or(done, fits)


def partner(x):
    lane = lax.broadcasted_iota(jnp.int32, (1, 128), 1)
    return jnp.where((lane & 32) == 0, pltpu.roll(x, 96, 1), pltpu.roll(x, 32, 1))


def load_once(t, copies, sems):
    @pl.when(t == 0)
    def _():
        made = [pltpu.make_async_copy(s, d, sems.at[k]) for k, (s, d) in enumerate(copies)]
        for copy in made:
            copy.start()
        for copy in made:
            copy.wait()


def column_blocks(piece, owner, dst, rows, base=0):
    return [
        (
            piece.at[base + rows * j : base + rows * (j + 1), :],
            dst.at[pl.ds(owner * rows, rows), 512 * j : 512 * (j + 1)],
        )
        for j in range(dst.shape[1] // 512)
    ]


def row_block(piece, owner, dst, rows, base=0):
    return [(piece.at[base : base + rows, :], dst.at[pl.ds(owner * rows, rows), :])]


def row_spec(width):
    return "row"


def whole(*shape):
    return "whole"


def anywhere(count):
    return ["any"] * count


def out_shape(*shape, dtype=f32):
    return jax.ShapeDtypeStruct(shape, dtype)


def view(ref, kind, t):
    if kind == "row":
        return ref.at[pl.ds(pl.multiple_of(t * TILE, TILE), TILE), :]
    if kind == "col":
        return ref.at[:, pl.ds(pl.multiple_of(t * TILE, TILE), TILE)]
    if isinstance(kind, tuple):
        width = kind[1]
        return ref.at[:, pl.ds(pl.multiple_of(t * width, width), width)]
    return ref


def block_of(kind, shape, tile):
    if kind == "any":
        return pl.BlockSpec(memory_space=pl.ANY)
    if kind == "row":
        return pl.BlockSpec((tile, shape[1]), lambda i, *_: (i, 0))
    if kind == "col":
        return pl.BlockSpec((shape[0], tile), lambda i, *_: (0, i))
    if isinstance(kind, tuple) and kind[0] == "lane":
        return pl.BlockSpec((shape[0], kind[1]), lambda i, *_: (0, i))
    if isinstance(kind, tuple) and kind[0] == "cut":
        _, dim, width, at = kind
        block = (shape[0], width) if dim else (width, shape[1])
        return pl.BlockSpec(block, lambda i, *_: (0, at) if dim else (at, 0))
    if isinstance(kind, tuple):
        return pl.BlockSpec((None,) + shape[1:], lambda i, *_: (kind[1],) + (0,) * (len(shape) - 1))
    return pl.BlockSpec(shape, lambda i, *_: (0,) * len(shape))


def run(
    body, name, scalars, inputs, in_specs, out_specs, outs, scratch, grid, flops, count=0, piped=False
):
    tile = BIG_TILE if name in BIG else TILE
    size = sum(math.prod(o.shape) * o.dtype.itemsize for o in outs)
    size += sum(math.prod(o.shape) * o.dtype.itemsize for o in inputs)
    lead = len(scalars)
    cost = pl.CostEstimate(flops=int(flops), bytes_accessed=int(size), transcendentals=int(count))
    params = pltpu.CompilerParams(vmem_limit_bytes=LIMIT)
    if piped or grid[0] > 1:
        inputs = [pltpu.with_memory_space_constraint(v, pltpu.HBM) for v in inputs]
        outs = [pltpu.HBM(v.shape, v.dtype) for v in outs]
        return pl.pallas_call(
            lambda *refs: body(pl.program_id(0), *refs),
            grid_spec=pltpu.PrefetchScalarGridSpec(
                num_scalar_prefetch=lead,
                grid=grid,
                in_specs=[block_of(k, v.shape, tile) for k, v in zip(in_specs, inputs)],
                out_specs=[block_of(k, v.shape, tile) for k, v in zip(out_specs, outs)],
                scratch_shapes=scratch,
            ),
            out_shape=outs,
            cost_estimate=cost,
            compiler_params=params,
            name=name,
        )(*scalars, *inputs)
    kinds = list(in_specs) + list(out_specs)

    def kernel(*refs):
        held = refs[lead : lead + len(kinds)]
        rest = refs[lead + len(kinds) :]

        def step(t, carry):
            views = [view(ref, kind, t) for ref, kind in zip(held, kinds)]
            body(t, *refs[:lead], *views, *rest)
            return carry

        if grid[0] == 1:
            step(0, 0)
        else:
            lax.fori_loop(0, grid[0], step, 0)

    vmem = pl.BlockSpec(memory_space=pltpu.VMEM)
    place = lambda kind: pl.BlockSpec(memory_space=pl.ANY) if kind == "any" else vmem
    return pl.pallas_call(
        kernel,
        in_specs=[pl.BlockSpec(memory_space=pltpu.SMEM)] * lead + [place(k) for k in in_specs],
        out_specs=[vmem] * len(outs),
        out_shape=outs,
        scratch_shapes=scratch,
        cost_estimate=cost,
        compiler_params=params,
        name=name,
    )(*scalars, *inputs)


def ff_forward_body(t, me, x, norms, *refs, rel, er, sr):
    n = len(rel)
    parts = refs[:n]
    x1, hidden, before, active, w_in, w_out, sems = refs[n:]
    copies = []
    for k, r in enumerate(rel):
        copies += column_blocks(parts[k], me[0] ^ r, w_in, er)
        copies += row_block(parts[k], me[0] ^ r, w_out, sr, 4 * er)
    load_once(t, copies, sems)
    value = x[...].astype(f32)
    normed, _ = normalize(value)
    h = (normed * norms[0:1, :] + norms[1:2, :]).astype(bf16)
    hidden[...] = h
    total = None
    for j in range(w_in.shape[1] // 512):
        cols = slice(512 * j, 512 * (j + 1))
        a = mm(h, w_in[:, cols])
        s = (a * sigmoid(a)).astype(bf16)
        before[:, cols] = a.astype(bf16)
        active[:, cols] = s
        part = mm(s, w_out[cols, :])
        total = part if total is None else total + part
    x1[...] = value + 0.5 * total


def ff_forward(me, x, norms, parts, rel):
    rows, d = x.shape
    er, sr = d // len(rel), 4 * d // len(rel)
    ff = sr * len(rel)
    return run(
        functools.partial(ff_forward_body, rel=rel, er=er, sr=sr),
        "ff_forward",
        (me,),
        (x, norms, *parts),
        [row_spec(d), whole(*norms.shape)] + anywhere(len(rel)),
        [row_spec(d), row_spec(d), row_spec(ff), row_spec(ff)],
        [
            out_shape(rows, d),
            out_shape(rows, d, dtype=bf16),
            out_shape(rows, ff, dtype=bf16),
            out_shape(rows, ff, dtype=bf16),
        ],
        [pltpu.VMEM((d, ff), bf16), pltpu.VMEM((ff, d), bf16), pltpu.SemaphoreType.DMA((5 * len(rel),))],
        (rows // BIG_TILE,),
        4 * rows * d * ff,
        rows * ff,
        True,
    )


def qkv_body(t, me, x1, norms, cs, sn, *refs, rel, ar):
    n = len(rel)
    parts = refs[:n]
    hidden, q, k, v, kt, w, sems = refs[n:]
    copies = []
    for j, r in enumerate(rel):
        copies += column_blocks(parts[j], me[0] ^ r, w, ar)
    load_once(t, copies, sems)
    normed, _ = normalize(x1[...])
    h = (normed * norms[2:3, :] + norms[3:4, :]).astype(bf16)
    hidden[...] = h
    c, s = cs[...], sn[...]
    for p in range(4):
        cols = slice(128 * p, 128 * (p + 1))
        a = mm(h, w[:, 128 * p : 128 * (p + 1)])
        q[:, cols] = ((a * c + partner(a) * s).astype(bf16) * 0.125).astype(bf16)
        a = mm(h, w[:, 512 + 128 * p : 512 + 128 * (p + 1)])
        turned = (a * c + partner(a) * s).astype(bf16)
        k[:, cols] = turned
        kt[cols, :] = turned.T
    v[...] = mm(h, w[:, 1024:1536]).astype(bf16)


def qkv(me, x1, norms, cs, sn, parts, rel):
    rows, d = x1.shape
    ar = parts[0].shape[0] // 4
    half = lambda: out_shape(rows, d, dtype=bf16)
    return run(
        functools.partial(qkv_body, rel=rel, ar=ar),
        "query_key_value",
        (me,),
        (x1, norms, cs, sn, *parts),
        [row_spec(d), whole(*norms.shape), row_spec(128), row_spec(128)] + anywhere(len(rel)),
        [row_spec(d)] * 4 + ["col"],
        [half(), half(), half(), half(), out_shape(d, rows, dtype=bf16)],
        [pltpu.VMEM((d, 3 * d), bf16), pltpu.SemaphoreType.DMA((3 * len(rel),))],
        (rows // TILE,),
        6 * rows * d * d,
    )


def attention_body(t, ends, me, q, k, v, x1, *refs, rel, ar, rows):
    n = len(rel)
    parts = refs[:n]
    x2, mixed, lse, w, sems = refs[n:]
    copies = []
    for j, r in enumerate(rel):
        copies += row_block(parts[j], me[0] ^ r, w, ar, 3 * ar)
    load_once(t, copies, sems)
    e = [ends[j] for j in range(4)]
    first = t * TILE
    lo, hi = key_range(first, first + TILE - 1, e, rows)
    sq = seg_of(first + lax.broadcasted_iota(jnp.int32, (1, TILE), 1), e)
    low = lax.broadcasted_iota(jnp.int32, (1, 128), 1) < 64
    zero = jnp.zeros((), bf16)

    def body(start, w_keys):
        keys = pl.ds(start, w_keys)
        same = seg_of(start + lax.broadcasted_iota(jnp.int32, (w_keys, 1), 0), e) == sq

        def pair(p, carry):
            cols = pl.ds(pl.multiple_of(128 * p, 128), 128)
            qp, kp, vp = q[:, cols], k[keys, cols], v[keys, cols]
            both = None
            for h in range(2):
                head = 2 * p + h
                pick = low if h == 0 else jnp.logical_not(low)
                s = jnp.where(same, mm_nt(kp, jnp.where(pick, qp, zero)), masked_score)
                top = jnp.max(s, axis=0, keepdims=True)
                expo = jnp.exp(s - top)
                total = col_sum(expo)
                lse[pl.ds(head, 1), :] = top + jnp.log(total)
                prob = (expo * (1.0 / total)).astype(bf16)
                part = mm_tn(prob, jnp.where(pick, vp, zero))
                both = part if both is None else both + part
            mixed[:, cols] = both.astype(bf16)
            return carry

        lax.fori_loop(0, 4, pair, 0, unroll=2)

    in_window(lo, hi, rows, body)
    x2[...] = x1[...] + mm(mixed[...], w[...])


def attention(ends, me, q, k, v, x1, parts, rel):
    rows, d = q.shape
    ar = parts[0].shape[0] // 4
    return run(
        functools.partial(attention_body, rel=rel, ar=ar, rows=rows),
        "attention_forward",
        (ends, me),
        (q, k, v, x1, *parts),
        [row_spec(d), whole(rows, d), whole(rows, d), row_spec(d)] + anywhere(len(rel)),
        [row_spec(d), row_spec(d), "col"],
        [out_shape(rows, d), out_shape(rows, d, dtype=bf16), out_shape(HEADS, rows)],
        [pltpu.VMEM((d, d), bf16), pltpu.SemaphoreType.DMA((len(rel),))],
        (rows // TILE,),
        16 * rows * rows * d // 4,
        HEADS * rows * rows,
    )


def attention_back_body(t, ends, q, k, kt, v, do, lse, delta, cs, sn, gp, dqt, *, rows, pairs, base):
    e = [ends[j] for j in range(4)]
    first = pl.multiple_of(t * TILE, TILE)
    lo, hi = key_range(first, first + TILE - 1, e, rows)
    sk = seg_of(first + lax.broadcasted_iota(jnp.int32, (TILE, 1), 0), e)
    low = lax.broadcasted_iota(jnp.int32, (1, 128), 1) < 64
    here = pl.ds(first, TILE)
    zero = jnp.zeros((), bf16)

    @pl.when(t == 0)
    def _():
        dqt[...] = jnp.zeros_like(dqt)

    def body(start, w):
        qs = pl.ds(start, w)
        same = sk == seg_of(start + lax.broadcasted_iota(jnp.int32, (1, w), 1), e)

        def pair(p, carry):
            held = pl.ds(pl.multiple_of(128 * p, 128), 128)
            qp, dop = q[qs, held], do[qs, held]
            kp, vp = k[here, held], v[here, held]
            gk, gv = None, None
            for h in range(2):
                head = 2 * p + h
                full = 2 * base + head
                pick = low if h == 0 else jnp.logical_not(low)
                qm, dom = jnp.where(pick, qp, zero), jnp.where(pick, dop, zero)
                hr = pl.ds(pl.multiple_of(64 * head, 64), 64)
                expo = jnp.exp(mm_nt(kp, qm) - lse[pl.ds(full, 1), qs])
                prob = jnp.where(same, expo, 0.0)
                ds = (prob * (mm_nt(vp, dom) - delta[pl.ds(full, 1), qs])).astype(bf16)
                v_part = mm(prob.astype(bf16), dom)
                k_part = mm(ds, qm)
                dqt[hr, qs] += mm(kt[hr, here], ds)
                gv = v_part if gv is None else gv + v_part
                gk = k_part if gk is None else gk + k_part
            c, s = cs[here, :], sn[here, :]
            gp[here, pl.ds(pl.multiple_of(128 * (2 * pairs + p), 128), 128)] = gv.astype(bf16)
            turned = gk * c - partner(gk) * s
            gp[here, pl.ds(pl.multiple_of(128 * (pairs + p), 128), 128)] = turned.astype(bf16)
            return carry

        lax.fori_loop(0, pairs, pair, 0)

    in_window(lo, hi, rows, body)

    @pl.when(t == rows // TILE - 1)
    def _():
        c, s = cs[...] * 0.125, sn[...] * 0.125
        for p in range(pairs):
            cols = slice(128 * p, 128 * (p + 1))
            g = dqt[cols, :].T
            gp[:, cols] = (g * c - partner(g) * s).astype(bf16)


def attention_back(ends, q, k, kt, v, do, lse, delta, cs, sn, base, pairs):
    rows, d = q.shape
    wide, at = 128 * pairs, base // pairs
    return run(
        functools.partial(attention_back_body, rows=rows, pairs=pairs, base=base),
        "attention_backward",
        (ends,),
        (q, k, kt, v, do, lse, delta, cs, sn),
        [("cut", 1, wide, at)] * 2
        + [("cut", 0, wide, at)]
        + [("cut", 1, wide, at)] * 2
        + [whole(HEADS, rows)] * 2
        + [whole(rows, 128)] * 2,
        [whole(rows, 3 * wide)],
        [out_shape(rows, 3 * wide, dtype=bf16)],
        [pltpu.VMEM((wide, rows), f32)],
        (rows // TILE,),
        10 * rows * rows * d * pairs // 4,
        HEADS * rows * rows * pairs // 4,
    )[0]


def spaced_rows(rows):
    return rows + 6 * GAP


def group_segments(row, ends):
    return seg_of(row + lax.broadcasted_iota(jnp.int32, (8, 128), 0), ends)


def spread_all(groups, first, spans, ends, read, buf):
    def put(s, row, seg, values):
        at = pl.ds(pl.multiple_of(GAP + GAP * s + row, 8), 8)
        keep = seg == s
        for c in range(4):
            buf[c, at, :] = jnp.where(keep, values[c], 0.0)

    def one(g, carry):
        row = 8 * (first + g)
        seg = group_segments(row, ends)
        values = read(g)
        put(spans[0, first + g], row, seg, values)
        put(spans[1, first + g], row, seg, values)
        return carry

    lax.fori_loop(0, groups, one, 0, unroll=4)

    @pl.when(spans[2, 0] > 1)
    def _():
        def rest(g, carry):
            row = 8 * (first + g)
            seg = group_segments(row, ends)
            values = read(g)

            def fix(s, inner):
                put(s, row, seg, values)
                return inner

            return lax.fori_loop(spans[0, first + g] + 1, spans[1, first + g], fix, carry)

        lax.fori_loop(0, groups, rest, 0)


def collect_all(groups, first, spans, ends, buf, out):
    def one(g, carry):
        row = 8 * (first + g)
        seg = group_segments(row, ends)
        lo, hi = spans[0, first + g], spans[1, first + g]
        keep = seg == lo
        a = pl.ds(pl.multiple_of(GAP + GAP * lo + row, 8), 8)
        b = pl.ds(pl.multiple_of(GAP + GAP * hi + row, 8), 8)
        to = pl.ds(pl.multiple_of(8 * g, 8), 8)
        for c in range(4):
            out[to, 128 * c : 128 * (c + 1)] = jnp.where(keep, buf[c, a, :], buf[c, b, :])
        return carry

    lax.fori_loop(0, groups, one, 0, unroll=4)

    @pl.when(spans[2, 0] > 1)
    def _():
        def rest(g, carry):
            row = 8 * (first + g)
            seg = group_segments(row, ends)
            to = pl.ds(pl.multiple_of(8 * g, 8), 8)

            def fix(s, inner):
                a = pl.ds(pl.multiple_of(GAP + GAP * s + row, 8), 8)
                for c in range(4):
                    cols = slice(128 * c, 128 * (c + 1))
                    out[to, cols] = jnp.where(seg == s, buf[c, a, :], out[to, cols])
                return inner

            return lax.fori_loop(spans[0, first + g] + 1, spans[1, first + g], fix, carry)

        lax.fori_loop(0, groups, rest, 0)


CHUNK = 8


def slide(src, taps, dst, rows, shift, reverse):
    span = 8 * CHUNK

    def step(i, carry):
        c = i // ((rows + 4 * GAP) // span)
        base = pl.multiple_of((i - c * ((rows + 4 * GAP) // span)) * span, 8)
        acc = [jnp.zeros((8, 128), f32) for _ in range(CHUNK)]
        for b in range(8):
            loads = [
                src[c, pl.ds(base + (shift + b + 8 * m), 8), :] for m in range(CHUNK + 3)
            ]
            for a in range(4):
                j = 8 * a + b
                j = TAPS - 1 - j if reverse else j
                w = jnp.broadcast_to(taps[c, j : j + 1, :], (8, 128))
                for m in range(CHUNK):
                    acc[m] = acc[m] + w * loads[m + a]
        for m in range(CHUNK):
            dst[c, pl.ds(base + GAP + 8 * m, 8), :] = acc[m]
        return carry

    lax.fori_loop(0, 4 * ((rows + 4 * GAP) // span), step, 0)


def tap_sums(grad, src, out, rows):
    span = 8 * CHUNK

    def lanes(c, carry):
        def step(i, acc):
            acc = list(acc)
            base = pl.multiple_of(i * span, 8)
            g = [grad[c, pl.ds(base + GAP + 8 * m, 8), :] for m in range(CHUNK)]
            for b in range(8):
                loads = [src[c, pl.ds(base + (b + 8 * m), 8), :] for m in range(CHUNK + 3)]
                for a in range(4):
                    j = 8 * a + b
                    for m in range(CHUNK):
                        acc[j] = acc[j] + g[m] * loads[m + a]
            return tuple(acc)

        zeros = tuple(jnp.zeros((8, 128), f32) for _ in range(TAPS))
        acc = lax.fori_loop(0, (rows + 4 * GAP) // span, step, zeros)
        for j in range(TAPS):
            out[c, j : j + 1, :] = col_sum(acc[j])
        return carry

    lax.fori_loop(0, 4, lanes, 0)


def conv_front_body(t, ends, me, spans, x2, norms, taps, *refs, rel, ar, rows):
    n = len(rel)
    parts = refs[:n]
    hidden, gates_out, conv, spaced, stats, glu, answer, w, sems = refs[n:]
    copies = []
    for j, r in enumerate(rel):
        copies += column_blocks(parts[j], me[0] ^ r, w, ar)
    load_once(t, copies, sems)
    e = [ends[j] for j in range(4)]

    @pl.when(t == 0)
    def _():
        spaced[...] = jnp.zeros_like(spaced)

    normed, _ = normalize(x2[...])
    h = (normed * norms[4:5, :] + norms[5:6, :]).astype(bf16)
    hidden[...] = h
    half = mm(h, w[:, :512])
    gate = mm(h, w[:, 512:])
    gates_out[:, :512] = half.astype(bf16)
    gates_out[:, 512:] = gate.astype(bf16)
    glu[...] = half * sigmoid(gate)

    def read(g):
        at = pl.ds(pl.multiple_of(8 * g, 8), 8)
        return [glu[at, 128 * c : 128 * (c + 1)] for c in range(4)]

    spread_all(TILE // 8, t * (TILE // 8), spans, e, read, spaced)

    @pl.when(t == rows // TILE - 1)
    def _():
        slide(spaced, taps, answer, rows, 0, False)
        collect_all(rows // 8, 0, spans, e, answer, conv)
        keep = lax.broadcasted_iota(jnp.int32, (rows, 1), 0) < e[3]
        kept = jnp.where(keep, conv[...], 0.0)
        stats[0:1, :] = col_sum(kept)
        stats[1:2, :] = col_sum(kept * kept)
        stats[2:3, :] = jnp.full((1, 512), e[3], jnp.int32).astype(f32)


def conv_front(ends, me, spans, x2, norms, taps, parts, rel):
    rows, d = x2.shape
    ar = parts[0].shape[0] // 3
    far = spaced_rows(rows)
    return run(
        functools.partial(conv_front_body, rel=rel, ar=ar, rows=rows),
        "gated_convolution",
        (ends, me, spans),
        (x2, norms, taps, *parts),
        [row_spec(d), whole(*norms.shape), whole(4, TAPS, 128)] + anywhere(len(rel)),
        [row_spec(d), row_spec(2 * d), whole(rows, d), whole(4, far, 128), whole(3, d)],
        [
            out_shape(rows, d, dtype=bf16),
            out_shape(rows, 2 * d, dtype=bf16),
            out_shape(rows, d),
            out_shape(4, far, 128),
            out_shape(3, d),
        ],
        [
            pltpu.VMEM((TILE, d), f32),
            pltpu.VMEM((4, far, 128), f32),
            pltpu.VMEM((d, 2 * d), bf16),
            pltpu.SemaphoreType.DMA((2 * len(rel),)),
        ],
        (rows // TILE,),
        8 * rows * d * d,
        rows * d,
    )


def conv_back_body(t, ends, spans, gz, conv, batch, totals, norms, taps, far, g_glu, tap_grad, grad, spaced, sem, *, rows):
    arriving = pltpu.make_async_copy(far, spaced, sem.at[0])
    arriving.start()
    e = [ends[j] for j in range(4)]
    grad[...] = jnp.zeros_like(grad)
    mean, scale, count = batch[0:1, :], batch[1:2, :], batch[2:3, :]
    bias_all = jnp.sum(totals[:, 0, :], axis=0, keepdims=True) / count
    gain_all = jnp.sum(totals[:, 1, :], axis=0, keepdims=True) / count
    factor = scale * norms[6:7, :]
    per = []
    for c in range(4):
        cols = slice(128 * c, 128 * (c + 1))
        per.append(
            [
                jnp.broadcast_to(v[:, cols], (8, 128))
                for v in (mean, scale, bias_all, gain_all, factor)
            ]
        )

    def read(g):
        row = pl.multiple_of(8 * g, 8)
        keep = row + lax.broadcasted_iota(jnp.int32, (8, 128), 0) < e[3]
        values = []
        for c in range(4):
            cols = slice(128 * c, 128 * (c + 1))
            m, s, b, k, f = per[c]
            zhat = (conv[pl.ds(row, 8), cols] - m) * s
            away = jnp.where(keep, b + zhat * k, 0.0)
            values.append(f * (gz[pl.ds(row, 8), cols] - away))
        return values

    spread_all(rows // 8, 0, spans, e, read, grad)
    slide(grad, taps, g_glu, rows, 1, True)
    arriving.wait()
    tap_sums(grad, spaced, tap_grad, rows)


def conv_back(ends, spans, gz, conv, batch, totals, norms, taps, spaced):
    rows, d = conv.shape
    far = spaced_rows(rows)
    return run(
        functools.partial(conv_back_body, rows=rows),
        "convolution_backward",
        (ends, spans),
        (gz, conv, batch, totals, norms, taps, spaced),
        [whole(rows, d), whole(rows, d), whole(3, d), whole(*totals.shape), whole(*norms.shape)]
        + [whole(4, TAPS, 128), "any"],
        [whole(4, far, 128), whole(4, TAPS, 128)],
        [out_shape(4, far, 128), out_shape(4, TAPS, 128)],
        [
            pltpu.VMEM((4, far, 128), f32),
            pltpu.VMEM((4, far, 128), f32),
            pltpu.SemaphoreType.DMA((1,)),
        ],
        (1,),
        12 * rows * d * TAPS * 40,
        rows * d,
    )


def gates_back_body(t, ends, me, spans, g_glu, norms, gates, x2, g3, mixed, *refs, rel, ar, rows):
    n = len(rel)
    parts, heads = refs[:n], refs[n : 2 * n]
    (g_gates, g2, g_attn, g_mixed, delta, sums) = refs[2 * n : 2 * n + 6]
    glu_rows, w, w_heads, sems = refs[2 * n + 6 :]
    copies = []
    for j, r in enumerate(rel):
        copies += column_blocks(parts[j], me[0] ^ r, w, ar)
        copies += row_block(heads[j], me[0] ^ r, w_heads, ar, 3 * ar)
    load_once(t, copies, sems)
    e = [ends[j] for j in range(4)]

    @pl.when(t == 0)
    def _():
        sums[...] = jnp.zeros_like(sums)

    collect_all(TILE // 8, t * (TILE // 8), spans, e, g_glu, glu_rows)
    gg = glu_rows[...]
    sigma = sigmoid(gates[:, 512:].astype(f32))
    first = (gg * sigma).astype(bf16)
    second = (gg * gates[:, :512].astype(f32) * sigma * (1.0 - sigma)).astype(bf16)
    g_gates[:, :512] = first
    g_gates[:, 512:] = second
    g_hidden = mm_nt(first, w[:, :512]) + mm_nt(second, w[:, 512:])
    normed, scale = normalize(x2[...])
    sums[0:1, :] += col_sum(g_hidden * normed)
    sums[1:2, :] += col_sum(g_hidden)
    out = g3[...] + norm_back(g_hidden, norms[4:5, :], normed, scale)
    g2[...] = out
    branch = out.astype(bf16)
    g_attn[...] = branch
    gm = mm_nt(branch, w_heads[...]).astype(bf16)
    g_mixed[...] = gm
    dots = gm.astype(f32) * mixed[...].astype(f32)
    upper = dots.astype(bf16)
    lower = (dots - upper.astype(f32)).astype(bf16)
    head = lax.broadcasted_iota(jnp.int32, (HEADS, 512), 0)
    ones = (lax.broadcasted_iota(jnp.int32, (HEADS, 512), 1) // 64 == head).astype(bf16)
    delta[...] = mm_nt(ones, upper) + mm_nt(ones, lower)


def gates_back(ends, me, spans, g_glu, norms, gates, x2, g3, mixed, parts, heads, rel):
    rows, d = x2.shape
    ar = parts[0].shape[0] // 3
    return run(
        functools.partial(gates_back_body, rel=rel, ar=ar, rows=rows),
        "gates_backward",
        (ends, me, spans),
        (g_glu, norms, gates, x2, g3, mixed, *parts, *heads),
        [whole(*g_glu.shape), whole(*norms.shape), row_spec(2 * d)]
        + [row_spec(d)] * 3
        + anywhere(2 * len(rel)),
        [row_spec(2 * d), row_spec(d), row_spec(d), row_spec(d)]
        + ["col", whole(2, d)],
        [
            out_shape(rows, 2 * d, dtype=bf16),
            out_shape(rows, d),
            out_shape(rows, d, dtype=bf16),
            out_shape(rows, d, dtype=bf16),
            out_shape(HEADS, rows),
            out_shape(2, d),
        ],
        [
            pltpu.VMEM((TILE, d), f32),
            pltpu.VMEM((d, 2 * d), bf16),
            pltpu.VMEM((d, d), bf16),
            pltpu.SemaphoreType.DMA((3 * len(rel),)),
        ],
        (rows // TILE,),
        6 * rows * d * d,
        rows * d,
    )


def rear_body(t, ends, me, conv, totals, x2, cot, norms, *refs, rel, ar, er, sr):
    n = len(rel)
    points, ffs = refs[:n], refs[n : 2 * n]
    (y, g_third, g_zed, wact, branch_out, hidden, active, g_before, g_out, sums, batch) = refs[2 * n : 2 * n + 11]
    w_point, w_in, w_out, slope, sems = refs[2 * n + 11 :]
    copies = []
    for j, r in enumerate(rel):
        copies += row_block(points[j], me[0] ^ r, w_point, ar, 2 * ar)
        copies += column_blocks(ffs[j], me[0] ^ r, w_in, er)
        copies += row_block(ffs[j], me[0] ^ r, w_out, sr, 4 * er)
    load_once(t, copies, sems)

    @pl.when(t == 0)
    def _():
        sums[...] = jnp.zeros_like(sums)
        total = jnp.sum(totals[...], axis=0)
        count = total[2:3, :]
        mean = total[0:1, :] / count
        batch[0:1, :] = mean
        batch[1:2, :] = lax.rsqrt(total[1:2, :] / count - mean * mean + batch_epsilon)
        batch[2:3, :] = count

    zhat = (conv[...] - batch[0:1, :]) * batch[1:2, :]
    zed = zhat * norms[6:7, :] + norms[7:8, :]
    sigma = sigmoid(zed)
    wa = (zed * sigma).astype(bf16)
    wact[...] = wa
    zed_slope = slope_of(zed, sigma)
    third = x2[...] + mm(wa, w_point[...])
    normed, scale = normalize(third)
    h = (normed * norms[8:9, :] + norms[9:10, :]).astype(bf16)
    hidden[...] = h
    total = None
    for j in range(w_in.shape[1] // 512):
        cols = slice(512 * j, 512 * (j + 1))
        a = mm(h, w_in[:, cols])
        sg = sigmoid(a)
        s = (a * sg).astype(bf16)
        active[:, cols] = s
        slope[:, cols] = slope_of(a, sg)
        part = mm(s, w_out[cols, :])
        total = part if total is None else total + part
    fourth = third + 0.5 * total
    last, last_scale = normalize(fourth)
    keep = t * BIG_TILE + lax.broadcasted_iota(jnp.int32, (BIG_TILE, 1), 0) < ends[3]
    y[...] = jnp.where(keep, last * norms[10:11, :] + norms[11:12, :], 0.0).astype(bf16)
    g_y = jnp.where(keep, cot[...].astype(f32), 0.0)
    sums[0:1, :] += col_sum(g_y * last)
    sums[1:2, :] += col_sum(g_y)
    g_fourth = norm_back(g_y, norms[10:11, :], last, last_scale)
    go = (0.5 * g_fourth).astype(bf16)
    g_out[...] = go
    g_hidden = None
    for j in range(w_in.shape[1] // 512):
        cols = slice(512 * j, 512 * (j + 1))
        gb = (mm_nt(go, w_out[cols, :]) * slope[:, cols]).astype(bf16)
        g_before[:, cols] = gb
        part = mm_nt(gb, w_in[:, cols])
        g_hidden = part if g_hidden is None else g_hidden + part
    sums[2:3, :] += col_sum(g_hidden * normed)
    sums[3:4, :] += col_sum(g_hidden)
    g3 = g_fourth + norm_back(g_hidden, norms[8:9, :], normed, scale)
    g_third[...] = g3
    branch = g3.astype(bf16)
    branch_out[...] = branch
    gz = mm_nt(branch, w_point[...]) * zed_slope
    g_zed[...] = gz
    sums[4:5, :] += col_sum(gz)
    sums[5:6, :] += col_sum(gz * zhat)


def rear(ends, me, conv, totals, x2, cot, norms, points, ffs, rel):
    rows, d = x2.shape
    ar = points[0].shape[0] // 3
    ff = 4 * d
    er, sr = d // len(rel), ff // len(rel)
    return run(
        functools.partial(rear_body, rel=rel, ar=ar, er=er, sr=sr),
        "norm_feed_forward_and_back",
        (ends, me),
        (conv, totals, x2, cot, norms, *points, *ffs),
        [row_spec(d), whole(*totals.shape), row_spec(d), row_spec(d), whole(*norms.shape)]
        + anywhere(2 * len(rel)),
        [row_spec(d)] * 6 + [row_spec(ff), row_spec(ff), row_spec(d), whole(6, d), whole(3, d)],
        [
            out_shape(rows, d, dtype=bf16),
            out_shape(rows, d),
            out_shape(rows, d),
            out_shape(rows, d, dtype=bf16),
            out_shape(rows, d, dtype=bf16),
            out_shape(rows, d, dtype=bf16),
            out_shape(rows, ff, dtype=bf16),
            out_shape(rows, ff, dtype=bf16),
            out_shape(rows, d, dtype=bf16),
            out_shape(6, d),
            out_shape(3, d),
        ],
        [
            pltpu.VMEM((d, d), bf16),
            pltpu.VMEM((d, ff), bf16),
            pltpu.VMEM((ff, d), bf16),
            pltpu.VMEM((BIG_TILE, ff), f32),
            pltpu.SemaphoreType.DMA((6 * len(rel),)),
        ],
        (rows // BIG_TILE,),
        rows * d * (8 * ff + 4 * d),
        rows * ff,
        True,
    )


def qkv_back_body(t, me, ga, gb, x1, g2, norms, *refs, rel, ar):
    n = len(rel)
    attn = refs[:n]
    g1, g_out, sums, w, sems = refs[n:]
    copies = []
    for j, r in enumerate(rel):
        copies += column_blocks(attn[j], me[0] ^ r, w, ar)
    load_once(t, copies, sems)

    @pl.when(t == 0)
    def _():
        sums[...] = jnp.zeros_like(sums)

    g_hidden = None
    for z in range(3):
        for half, g in enumerate((ga, gb)):
            cols = slice(512 * z + 256 * half, 512 * z + 256 * (half + 1))
            part = mm_nt(g[:, 256 * z : 256 * (z + 1)], w[:, cols])
            g_hidden = part if g_hidden is None else g_hidden + part
    normed, scale = normalize(x1[...])
    sums[0:1, :] += col_sum(g_hidden * normed)
    sums[1:2, :] += col_sum(g_hidden)
    out = g2[...] + norm_back(g_hidden, norms[2:3, :], normed, scale)
    g1[...] = out
    g_out[...] = (0.5 * out).astype(bf16)


def qkv_back(me, ga, gb, x1, g2, norms, attn, rel):
    rows, d = x1.shape
    ar = d // len(rel)
    return run(
        functools.partial(qkv_back_body, rel=rel, ar=ar),
        "query_key_value_backward",
        (me,),
        (ga, gb, x1, g2, norms, *attn),
        [row_spec(3 * d // 2)] * 2 + [row_spec(d)] * 2 + [whole(*norms.shape)] + anywhere(len(rel)),
        [row_spec(d), row_spec(d), whole(2, d)],
        [out_shape(rows, d), out_shape(rows, d, dtype=bf16), out_shape(2, d)],
        [pltpu.VMEM((d, 3 * d), bf16), pltpu.SemaphoreType.DMA((3 * len(rel),))],
        (rows // TILE,),
        6 * rows * d * d,
    )


def ff_back_body(t, me, g1, go, x, before, norms, qkv_sums, conv_sums, rear_sums, tap_grad, *refs, rel, er, sr, steps):
    n = len(rel)
    parts = refs[:n]
    g_frames, g_before, small, sums, w_in, w_out, sems = refs[n:]
    copies = []
    for j, r in enumerate(rel):
        copies += column_blocks(parts[j], me[0] ^ r, w_in, er)
        copies += row_block(parts[j], me[0] ^ r, w_out, sr, 4 * er)
    load_once(t, copies, sems)

    @pl.when(t == 0)
    def _():
        sums[...] = jnp.zeros_like(sums)

    out = go[...]
    g_hidden = None
    for j in range(w_in.shape[1] // 512):
        cols = slice(512 * j, 512 * (j + 1))
        a = before[:, cols].astype(f32)
        gb = (mm_nt(out, w_out[cols, :]) * slope_of(a, sigmoid(a))).astype(bf16)
        g_before[:, cols] = gb
        part = mm_nt(gb, w_in[:, cols])
        g_hidden = part if g_hidden is None else g_hidden + part
    normed, scale = normalize(x[...].astype(f32))
    sums[0:1, :] += col_sum(g_hidden * normed)
    sums[1:2, :] += col_sum(g_hidden)
    g_frames[...] = g1[...] + norm_back(g_hidden, norms[0:1, :], normed, scale)

    @pl.when(t == steps - 1)
    def _():
        for c in range(tap_grad.shape[0]):
            small[:TAPS, 128 * c : 128 * (c + 1)] = tap_grad[c, :, :]
        rows = [sums[0:1, :], sums[1:2, :], qkv_sums[...], conv_sums[...], rear_sums[5:6, :]]
        rows += [rear_sums[4:5, :], rear_sums[2:4, :], rear_sums[0:2, :]]
        at = TAPS
        for row in rows:
            small[at : at + row.shape[0], :] = row
            at += row.shape[0]


def ff_back(me, g1, go, x, before, norms, sums, parts, rel):
    rows, d = x.shape
    ff = 4 * d
    er, sr = d // len(rel), ff // len(rel)
    return run(
        functools.partial(ff_back_body, rel=rel, er=er, sr=sr, steps=rows // TILE),
        "feed_forward_backward",
        (me,),
        (g1, go, x, before, norms, *sums, *parts),
        [row_spec(d), row_spec(d), row_spec(d), row_spec(ff), whole(*norms.shape)]
        + ["whole"] * len(sums)
        + anywhere(len(rel)),
        [row_spec(d), row_spec(ff), whole(TAPS + 12, d)],
        [out_shape(rows, d), out_shape(rows, ff, dtype=bf16), out_shape(TAPS + 12, d)],
        [
            pltpu.VMEM((2, d), f32),
            pltpu.VMEM((d, ff), bf16),
            pltpu.VMEM((ff, d), bf16),
            pltpu.SemaphoreType.DMA((5 * len(rel),)),
        ],
        (rows // TILE,),
        4 * rows * d * ff,
        rows * ff,
        True,
    )


def place_owners(me, tile, keep, send, base, height, owners, first):
    for k in range(owners):
        owner = first + k
        rows = tile[k * height : (k + 1) * height, :]
        mine = ((owner ^ me[0]) & 1) == 0

        @pl.when(mine)
        def _(rows=rows, owner=owner):
            keep[owner >> 1, pl.ds(base, height), :] = rows

        @pl.when(jnp.logical_not(mine))
        def _(rows=rows, owner=owner):
            send[owner >> 1, pl.ds(base, height), :] = rows


def weight_grad_body(t, me, *refs, fs, parts, n1, n2, extra):
    refs = list(refs)
    first = [refs.pop(0) for _ in range(1 + parts)] if n1 else None
    second = [refs.pop(0) for _ in range(2)] if n2 else None
    more = refs.pop(0) if extra else None
    keep, send = refs.pop(0), refs.pop(0)
    er = 512 // fs
    if n1:
        base = pl.multiple_of(t * er, er)
        tiles = [mm_tn(first[0][...], ref[...]).astype(bf16) for ref in first[1:]]
        tile = tiles[0] if parts == 1 else jnp.concatenate(tiles, axis=1)
        place_owners(me, tile, keep, send, base, er, fs, 0)
    if n2:
        sr = 512 * n2 // fs
        per = max(1, 512 // sr)

        def one(block):
            tile = mm_tn(second[0][...], second[1][...]).astype(bf16)
            place_owners(me, tile, keep, send, n1 * er, sr, per, block * per)

        if n1 in (0, n2):
            one(t)
        else:
            pl.when(t == 0)(lambda: one(0))
    if extra:

        @pl.when(t == 0)
        def _():
            tile = more[...].reshape(fs * extra, 512)
            place_owners(me, tile, keep, send, (n1 + n2) * er, extra, fs, 0)


def weight_grad(name, me, fs, first=None, second=None, more=None):
    inputs, specs = [], []
    n1 = n2 = parts = 0
    if first:
        h, gs = first
        rows, parts = h.shape[0], len(gs)
        wide = 512 // parts
        n1 = gs[0].shape[1] // wide
        inputs += [h, *gs]
        specs += [whole(rows, 512)] + [("lane", wide)] * parts
    if second:
        s, o = second
        rows = s.shape[0]
        n2 = s.shape[1] // 512
        inputs += [s, o]
        stepped = n1 in (0, n2)
        specs += [("lane", 512) if stepped else "whole", whole(rows, 512)]
    extra = 0
    if more is not None:
        extra = more.shape[1]
        inputs.append(more)
        specs.append("whole")
    height = (n1 + n2) * 512 // fs + extra
    return run(
        functools.partial(weight_grad_body, fs=fs, parts=parts, n1=n1, n2=n2, extra=extra),
        name,
        (me,),
        inputs,
        specs,
        [whole(fs // 2, height, 512)] * 2,
        [out_shape(fs // 2, height, 512, dtype=bf16)] * 2,
        [],
        (n1 or n2,),
        2 * rows * 512 * 512 * (n1 + n2),
        0,
        n1 == n2,
    )


def join(*pairs):
    return tuple(jnp.concatenate(list(side), axis=1) for side in zip(*pairs))


def bits_of(size):
    return int(size).bit_length() - 1


def swap(value, axis, size, mask):
    return lax.ppermute(value, axis, [(k, k ^ mask) for k in range(size)])


def relative(fs):
    rel = [0]
    for bit in reversed(range(bits_of(fs))):
        rel = rel + [r ^ (1 << bit) for r in rel]
    return tuple(rel)


def first_part(own, fs):
    parts = [own]
    for bit in reversed(range(1, bits_of(fs))):
        parts = parts + [swap(part, "fsdp", fs, 1 << bit) for part in parts]
    return parts


def second_part(parts, fs):
    return parts + [swap(part, "fsdp", fs, 1) for part in parts]


def sum_of(parts):
    total = parts[0].astype(f32)
    for part in parts[1:]:
        total = total + part.astype(f32)
    return total.astype(bf16)


class Chain:
    def __init__(self, pair, fs, dp):
        keep, send = pair
        self.fs, self.dp = fs, dp
        self.me, self.pack = lax.axis_index("fsdp"), lax.axis_index("dp")
        zero = jnp.int32(0)
        self.at, self.size = [zero, zero], list(keep.shape[:2])
        self.parts = [(keep, zero, zero)]
        self.stages = [("fsdp", bit, "halve") for bit in reversed(range(1, bits_of(fs)))]
        last = bits_of(dp) - 1
        self.stages += [("dp", bit, "halve") for bit in range(last)] + [("dp", last, "add")]
        self.stages += [("dp", bit, "join") for bit in reversed(range(last))]
        self.flight = swap(send, "fsdp", fs, 1)
        self.joining = None

    def take(self, y, r):
        shape = (self.size[0], self.size[1], 512)
        return sum_of(
            [lax.dynamic_slice(part, (y - y0, r - r0, 0), shape) for part, y0, r0 in self.parts]
        )

    def hold(self, *tokens):
        self.flight = after(self.flight, *tokens)

    def advance(self):
        if not self.stages:
            return None
        self.settle()
        axis, bit, kind = self.stages.pop(0)
        size, index = (self.fs, self.me) if axis == "fsdp" else (self.dp, self.pack)
        side = (index >> bit) & 1
        if kind == "halve":
            dim = 0 if axis == "fsdp" else 1
            base = self.at[dim]
            self.size[dim] //= 2
            self.at[dim] = base + (1 - side) * self.size[dim]
            send = self.take(*self.at)
            self.at[dim] = base + side * self.size[dim]
        else:
            if self.joining is None:
                send = self.take(*self.at)
            else:
                send = self.whole
            if kind == "join":
                send = send.reshape(-1, 512)
                self.whole, self.joining = send, side
            else:
                self.parts = [(send, *self.at)]
        self.flight = swap(send, axis, size, 1 << bit)
        return send

    def settle(self):
        if self.joining is None:
            self.parts.append((self.flight, *self.at))
        else:
            pair = [self.whole, self.flight]
            self.whole = jnp.where(
                self.joining == 0, jnp.concatenate(pair, axis=0), jnp.concatenate(pair[::-1], axis=0)
            )

    def result(self):
        while self.stages:
            self.advance()
        self.settle()
        return self.whole


def after(value, *tokens):
    tokens = [token for token in tokens if token is not None]
    return lax.optimization_barrier((value, *tokens))[0]


def from_everyone(rows):
    axes = ("dp", "fsdp")
    count = lax.axis_size(axes)
    spread = jnp.broadcast_to(rows[None], (count,) + rows.shape)
    return lax.all_to_all(spread, axes, 0, 0, tiled=True)


def to_rows(block):
    r, c = block.shape
    k = c // 512
    return block.reshape(r, k, 512).swapaxes(0, 1).reshape(k * r, 512)


def from_rows(rows, r, c):
    k = c // 512
    return rows.reshape(k, r, 512).swapaxes(0, 1).reshape(r, c)


def pack_body(t, a, b, out, *, n, er):
    for j in range(n):
        out[er * j : er * (j + 1), :] = a[:, 512 * j : 512 * (j + 1)].astype(bf16)
    out[er * n :, :] = b[...].astype(bf16)


def pack(name, a, b, index=None):
    er, n = a.shape[-2], a.shape[-1] // 512
    sr = b.shape[-2]
    return run(
        functools.partial(pack_body, n=n, er=er),
        name,
        (),
        (a, b),
        ["whole" if index is None else ("stack", index)] * 2,
        ["whole"],
        [out_shape(n * er + sr, 512, dtype=bf16)],
        [],
        (1,),
        er * n * 1024,
        0,
        True,
    )[0]


def adam_body(*refs):
    ga, gb = refs[0][...], refs[1][...]
    outs = refs[-6:]
    for ref, grad, to in ((refs[2:5], ga, outs[:3]), (refs[5:8], gb, outs[3:])):
        new = adam_update(ref[0][...], ref[1][...], ref[2][...], grad.astype(f32), decay_rate)
        for place, value in zip(to, new):
            place[...] = value


def adam_single_body(*refs):
    outs = refs[-3:]
    new = adam_update(refs[1][...], refs[2][...], refs[3][...], refs[0][...].astype(f32), decay_rate)
    for place, value in zip(outs, new):
        place[...] = value


def adam_single(name, grad, state, by_row, index, into):
    height, width = state[0].shape[-2:]
    n = 4
    block = (height // n, width) if by_row else (height, width // n)
    spec = pl.BlockSpec((None,) + block, lambda i: (index, i, 0) if by_row else (index, 0, i))
    return pl.pallas_call(
        adam_single_body,
        grid=(n,),
        in_specs=[pl.BlockSpec(block, lambda i: (i, 0))] + [spec] * 3 + [pl.BlockSpec(memory_space=pl.ANY)] * 3,
        out_specs=[spec] * 3,
        out_shape=[out_shape(*v.shape) for v in state],
        input_output_aliases={4 + j: j for j in range(3)},
        cost_estimate=pl.CostEstimate(
            flops=20 * height * width, bytes_accessed=26 * height * width, transcendentals=height * width
        ),
        compiler_params=pltpu.CompilerParams(vmem_limit_bytes=(8 if by_row else 48) * 1024 * 1024),
        name=name,
    )(grad, *state, *into)


def adam_pair(name, grad, first, second, steps, index=None, into=None):
    er, n = first[0].shape[-2], first[0].shape[-1] // 512
    sr = second[0].shape[-2]
    part = sr // n if steps else sr
    lead = () if index is None else (None,)
    at = () if index is None else (index,)
    spec_a = pl.BlockSpec(lead + (er, 512), lambda i: at + (0, i))
    spec_b = pl.BlockSpec(lead + (part, 512), lambda i: at + ((i, 0) if steps else (0, 0)))
    grad_a = pl.BlockSpec((er, 512), lambda i: (i, 0))
    grad_b = pl.BlockSpec((part, 512), lambda i: (n * er // part + (i if steps else 0), 0))
    inputs = [grad, grad, *first, *second]
    specs = [grad_a, grad_b] + [spec_a] * 3 + [spec_b] * 3
    alias = {}
    if into is not None:
        alias = {len(inputs) + j: j for j in range(6)}
        inputs += list(into)
        specs += [pl.BlockSpec(memory_space=pl.ANY)] * 6
    return pl.pallas_call(
        adam_body,
        grid=(n,),
        in_specs=specs,
        out_specs=[spec_a] * 3 + [spec_b] * 3,
        out_shape=[out_shape(*v.shape) for v in (*first, *second)],
        input_output_aliases=alias,
        cost_estimate=pl.CostEstimate(
            flops=20 * er * 512 * n, bytes_accessed=26 * (er * n + sr) * 512, transcendentals=er * 512 * n
        ),
        compiler_params=pltpu.CompilerParams(vmem_limit_bytes=8 * 1024 * 1024),
        name=name,
    )(*inputs)


def adam_update(master, first, second_block, grad, decay):
    first_new = beta_first * first + (1.0 - beta_first) * grad
    second_new = beta_second * second_block + (1.0 - beta_second) * grad * grad
    first_hat = first_new / (1.0 - beta_first**STEP)
    second_hat = second_new / (1.0 - beta_second**STEP)
    master_new = master - learn_rate * (
        first_hat / (jnp.sqrt(second_hat) + adam_epsilon) + decay * master
    )
    return (master_new, first_new, second_new)


def moments_only(first, second_block, grad):
    first_new = beta_first * first + (1.0 - beta_first) * grad
    second_new = beta_second * second_block + (1.0 - beta_second) * grad * grad
    return (first_new, second_new)


def rotary_tables(position, half):
    freq = jnp.exp(jnp.arange(half, dtype=f32) * (-math.log(10000.0) / half))
    angle = position.astype(f32)[:, None] * freq[None, :]
    cosine, sine = jnp.cos(angle), jnp.sin(angle)
    return (
        jnp.concatenate([cosine] * 4, axis=1),
        jnp.concatenate([-sine, sine, -sine, sine], axis=1),
    )


def per_device(
    frames,
    cotangent,
    lengths,
    expand,
    expand_first,
    expand_second,
    shrink,
    shrink_first,
    shrink_second,
    attend,
    attend_first,
    attend_second,
    heads_out,
    heads_out_first,
    heads_out_second,
    pointwise,
    pointwise_first,
    pointwise_second,
    pointwise_out,
    pointwise_out_first,
    pointwise_out_second,
    depthwise,
    depthwise_first,
    depthwise_second,
    norm_table,
    norm_table_first,
    norm_table_second,
):
    fs, dp = (lax.axis_size("fsdp"), lax.axis_size("dp"))
    rel = relative(fs)
    er, sr, ar = expand.shape[1], shrink.shape[1], attend.shape[0]
    dr = depthwise.shape[1]
    device = lax.axis_index("fsdp")
    me = device.astype(jnp.int32).reshape(1)
    ends = jnp.cumsum(lengths[0, :4]).astype(jnp.int32)
    rows, width = frames.shape

    early_own = pack("pack_early", expand, shrink, 0)
    ff_zero = first_part(early_own, fs)
    small = jnp.concatenate([after(depthwise, early_own), norm_table], axis=0).astype(bf16)
    tiny_rows = small.shape[0]
    small_parts = second_part(first_part(small, fs), fs)
    places = jnp.arange(rows, dtype=jnp.int32)
    segment = jnp.sum((places[:, None] >= ends[None, :]).astype(jnp.int32), axis=1)
    starts = jnp.concatenate([jnp.zeros((1,), jnp.int32), ends])
    pick = (segment[:, None] == jnp.arange(5, dtype=jnp.int32)[None, :]).astype(jnp.int32)
    position = places - jnp.sum(pick * starts[None, :], axis=1)
    lo, hi = segment[::8], segment[7::8]
    spans = jnp.stack([lo, hi, jnp.broadcast_to(jnp.max(hi - lo), lo.shape)])
    cs, sn = rotary_tables(position, width // HEADS // 2)

    attn_own = pack("pack_attn", attend, heads_out)
    conv_own = pack("pack_conv", pointwise, pointwise_out)
    late_own = pack("pack_late", expand, shrink, 1)
    small_full = jnp.zeros((fs, tiny_rows, dr), bf16)
    for k, r in enumerate(rel):
        small_full = lax.dynamic_update_slice_in_dim(small_full, small_parts[k][None], device ^ r, 0)
    small_full = small_full.swapaxes(0, 1).reshape(tiny_rows, fs * dr).astype(f32)
    norms = small_full[TAPS:]
    taps = small_full[:TAPS].reshape(TAPS, width // 128, 128).swapaxes(0, 1)
    ff_zero = [ff_zero[0]] + [after(part, attn_own, conv_own, late_own, cs, sn, norms, taps) for part in ff_zero[1:]]
    attn_parts = first_part(after(attn_own, *ff_zero), fs)
    ff_zero = second_part(ff_zero, fs)


    x1, hidden_zero, before_zero, active_zero = ff_forward(
        me, frames, norms, ff_zero, rel
    )
    attn_parts = [after(part, x1) for part in attn_parts]
    conv_parts = first_part(after(conv_own, *attn_parts), fs)
    attn_parts = second_part(attn_parts, fs)
    hidden_attn, q, k, v, kt = qkv(me, x1, norms, cs, sn, attn_parts, rel)
    conv_parts = [after(part, q) for part in conv_parts]
    ff_one = first_part(after(late_own, *conv_parts), fs)
    conv_parts = second_part(conv_parts, fs)
    x2, mixed, lse = attention(ends, me, after(q, *conv_parts), k, v, x1, attn_parts, rel)
    hidden_conv, gates, conv, spaced, stats = conv_front(ends, me, spans, x2, norms, taps, conv_parts, rel)
    ff_one = second_part([after(part, stats) for part in ff_one], fs)
    totals = from_everyone(stats)
    (
        layer_output,
        g_third,
        g_zed,
        wact,
        g_branch,
        hidden_one,
        active_one,
        g_before_one,
        g_out_one,
        rear_sums,
        batch,
    ) = rear(ends, me, conv, totals, x2, cotangent, norms, conv_parts, ff_one, rel)
    back_totals = from_everyone(rear_sums[4:6])
    late_pair = weight_grad(
        "weight_grad_late", me, fs, (hidden_one, (g_before_one,)), (active_one, g_out_one)
    )
    late = Chain((late_pair[0], after(late_pair[1], back_totals)), fs, dp)
    g_glu, tap_grad = conv_back(ends, spans, after(g_zed, late_pair[1]), conv, batch, back_totals, norms, taps, spaced)
    g_glu = after(g_glu, late.advance())
    g_gates, g_second, g_attn, g_mixed, delta, conv_sums = gates_back(
        ends, me, spans, g_glu, norms, gates, x2, g_third, mixed, conv_parts, attn_parts, rel
    )
    conv_pair = weight_grad("weight_grad_conv", me, fs, (hidden_conv, (g_gates,)), (wact, g_branch))
    middle = Chain(conv_pair, fs, dp)
    first_half = attention_back(
        ends, q, k, kt, v, after(g_mixed, conv_pair[1]), lse, delta, cs, sn, 0, 2
    )
    late.hold(first_half)
    middle.hold(first_half)
    tokens = (late.advance(), middle.advance(), first_half)
    second_half = attention_back(ends, q, k, kt, v, after(g_mixed, *tokens), lse, delta, cs, sn, 2, 2)
    late.hold(second_half)
    middle.hold(second_half)
    first_half = after(first_half, late.advance(), middle.advance())
    attn_pair = weight_grad(
        "weight_grad_attn", me, fs, (hidden_attn, (first_half, second_half)), (mixed, g_attn)
    )
    attn = Chain(attn_pair, fs, dp)
    g_first, g_out_zero, qkv_sums = qkv_back(
        me, after(first_half, attn_pair[1]), second_half, x1, g_second, norms, attn_parts, rel
    )
    for chain in (late, middle, attn):
        chain.hold(g_first)
    tokens = (late.advance(), middle.advance(), attn.advance())
    out_pair = weight_grad(
        "weight_grad_shrink", me, fs, None, (active_zero, after(g_out_zero, *tokens))
    )
    early_out = Chain(out_pair, fs, dp)
    middle.hold(out_pair[1])
    sums = (qkv_sums, conv_sums, rear_sums, tap_grad)
    frames_grad, g_before_zero, small_grad = ff_back(
        me,
        g_first,
        after(g_out_zero, out_pair[1], early_out.advance()),
        frames,
        before_zero,
        norms,
        sums,
        ff_zero,
        rel,
    )
    for chain in (late, middle, attn, early_out):
        chain.hold(g_before_zero)
    tokens = (attn.flight, early_out.flight, late.flight, middle.flight)
    small_grad = small_grad.astype(bf16).reshape(tiny_rows, fs, dr).swapaxes(0, 1)
    small_size = tiny_rows * dr
    small_pad = -small_size % (512 * 16)
    small_grad = jnp.pad(small_grad.reshape(fs, small_size), ((0, 0), (0, small_pad)))
    small_grad = small_grad.reshape(fs, -1, 512)
    tail_pair = weight_grad(
        "weight_grad_expand",
        me,
        fs,
        (hidden_zero, (after(g_before_zero, *tokens),)),
        None,
        small_grad,
    )
    tail = Chain(tail_pair, fs, dp)
    attn.hold(tail_pair[1])
    early_out.hold(tail_pair[1])
    tail_sent = tail.advance()
    expands = (expand, expand_first, expand_second)
    shrinks = (shrink, shrink_first, shrink_second)

    def hold(*chains):
        for chain in chains:
            chain.hold(tail_sent)

    hold(late, middle, attn, early_out)
    red_late, red_conv = late.result(), middle.result()
    new_late = adam_pair("adam_late", red_late, expands, shrinks, True, 1)
    new_conv = adam_pair(
        "adam_conv",
        red_conv,
        (pointwise, pointwise_first, pointwise_second),
        (pointwise_out, pointwise_out_first, pointwise_out_second),
        False,
    )
    new_attn = adam_pair(
        "adam_attn",
        attn.result(),
        (attend, attend_first, attend_second),
        (heads_out, heads_out_first, heads_out_second),
        False,
    )
    new_shrink = adam_single("adam_shrink", early_out.result(), shrinks, True, 0, new_late[3:])
    red_in = tail.result()
    new_expand = adam_single("adam_expand", red_in, expands, False, 0, new_late[:3])
    red_small = red_in[4 * er :].reshape(-1)[:small_size].reshape(tiny_rows, dr).astype(f32)
    new_taps = adam_update(depthwise, depthwise_first, depthwise_second, red_small[:TAPS], decay_rate)
    red_norms = red_small[TAPS:]
    new_norms = moments_only(norm_table_first, norm_table_second, red_norms)
    return (
        layer_output,
        frames_grad,
        *new_expand,
        *new_shrink,
        *new_attn,
        *new_conv,
        *new_taps,
        red_norms,
        *new_norms,
    )


def solution(mesh):
    return jax.shard_map(
        per_device,
        mesh=mesh,
        in_specs=(
            P(("dp", "fsdp"), None),
            P(("dp", "fsdp"), None),
            P(("dp", "fsdp"), None),
            P(None, "fsdp", None),
            P(None, "fsdp", None),
            P(None, "fsdp", None),
            P(None, "fsdp", None),
            P(None, "fsdp", None),
            P(None, "fsdp", None),
            P("fsdp", None),
            P("fsdp", None),
            P("fsdp", None),
            P("fsdp", None),
            P("fsdp", None),
            P("fsdp", None),
            P("fsdp", None),
            P("fsdp", None),
            P("fsdp", None),
            P("fsdp", None),
            P("fsdp", None),
            P("fsdp", None),
            P(None, "fsdp"),
            P(None, "fsdp"),
            P(None, "fsdp"),
            P(None, "fsdp"),
            P(None, "fsdp"),
            P(None, "fsdp"),
        ),
        out_specs=(
            P(("dp", "fsdp"), None),
            P(("dp", "fsdp"), None),
            P(None, "fsdp", None),
            P(None, "fsdp", None),
            P(None, "fsdp", None),
            P(None, "fsdp", None),
            P(None, "fsdp", None),
            P(None, "fsdp", None),
            P("fsdp", None),
            P("fsdp", None),
            P("fsdp", None),
            P("fsdp", None),
            P("fsdp", None),
            P("fsdp", None),
            P("fsdp", None),
            P("fsdp", None),
            P("fsdp", None),
            P("fsdp", None),
            P("fsdp", None),
            P("fsdp", None),
            P(None, "fsdp"),
            P(None, "fsdp"),
            P(None, "fsdp"),
            P(None, "fsdp"),
            P(None, "fsdp"),
            P(None, "fsdp"),
        ),
        check_vma=False,
    )
```

```python
import functools
import math

import jax
import jax.numpy as jnp
from jax import lax
from jax.experimental import pallas as pl
from jax.experimental.pallas import tpu as pltpu
from jax.sharding import PartitionSpec as P

HEADS = 8
STEP = 10
TAPS = 32
GAP = 16
LIMIT = 48 * 1024 * 1024
TILE = 256
WINDOWS = (512, 768)
BIG_TILE = 512
BIG = ("ff_forward", "norm_feed_forward_and_back")

norm_epsilon = 1e-05
batch_epsilon = 1e-05
masked_score = -1000000000.0
learn_rate = 0.1
beta_first = 0.9
beta_second = 0.98
adam_epsilon = 1e-08
decay_rate = 0.01

f32, bf16 = jnp.float32, jnp.bfloat16


def mm(a, b):
    return jnp.dot(a, b, preferred_element_type=f32)


def mm_nt(a, b):
    return lax.dot_general(a, b, (((1,), (1,)), ((), ())), preferred_element_type=f32)


def mm_tn(a, b):
    return lax.dot_general(a, b, (((0,), (0,)), ((), ())), preferred_element_type=f32)


def normalize(value):
    center = value - jnp.mean(value, axis=-1, keepdims=True)
    scale = lax.rsqrt(jnp.mean(center * center, axis=-1, keepdims=True) + norm_epsilon)
    return center * scale, scale


def norm_back(grad_out, gain, normed, scale):
    grad_norm = grad_out * gain
    return scale * (
        grad_norm
        - jnp.mean(grad_norm, axis=-1, keepdims=True)
        - normed * jnp.mean(grad_norm * normed, axis=-1, keepdims=True)
    )


def col_sum(value):
    return jnp.sum(value, axis=0, keepdims=True)


def sigmoid(value):
    return 0.5 * jnp.tanh(0.5 * value) + 0.5


def slope_of(value, sigma):
    return sigma * (1.0 + value * (1.0 - sigma))


def seg_of(places, ends):
    s = (places >= ends[0]).astype(jnp.int32)
    for j in range(1, 4):
        s = s + (places >= ends[j]).astype(jnp.int32)
    return s


def pick_last(values, count):
    out = values[0]
    for j in range(1, len(values)):
        out = jnp.where(count >= j, values[j], out)
    return out


def key_range(first, last, ends, rows):
    starts = [jnp.int32(0)] + ends
    stops = ends + [jnp.int32(rows)]
    return pick_last(starts, seg_of(first, ends)), pick_last(stops, seg_of(last, ends))


def in_window(lo, hi, rows, body):
    begin = (lo // 128) * 128
    done = jnp.bool_(False)
    for w in sorted({w for w in WINDOWS if w < rows} | {rows}):
        start = jnp.minimum(begin, rows - w)
        fits = jnp.logical_and(hi <= start + w, jnp.logical_not(done))

        @pl.when(fits)
        def _(start=start, w=w):
            body(pl.multiple_of(start, 128), w)

        done = jnp.logical_or(done, fits)


def partner(x):
    lane = lax.broadcasted_iota(jnp.int32, (1, 128), 1)
    return jnp.where((lane & 32) == 0, pltpu.roll(x, 96, 1), pltpu.roll(x, 32, 1))


def load_once(t, copies, sems):
    made = [pltpu.make_async_copy(s, d, sems.at[k]) for k, (s, d) in enumerate(copies)]

    @pl.when(t == 0)
    def _():
        for copy in made:
            copy.start()

    def ready(first=0, last=None):
        @pl.when(t == 0)
        def _():
            for copy in made[first:last]:
                copy.wait()

    return ready


def column_blocks(piece, owner, dst, rows, base=0):
    return [
        (
            piece.at[base + rows * j : base + rows * (j + 1), :],
            dst.at[pl.ds(owner * rows, rows), 512 * j : 512 * (j + 1)],
        )
        for j in range(dst.shape[1] // 512)
    ]


def row_block(piece, owner, dst, rows, base=0):
    return [(piece.at[base : base + rows, :], dst.at[pl.ds(owner * rows, rows), :])]


def row_spec(width):
    return "row"


def whole(*shape):
    return "whole"


def anywhere(count):
    return ["any"] * count


def out_shape(*shape, dtype=f32):
    return jax.ShapeDtypeStruct(shape, dtype)


def view(ref, kind, t):
    if kind == "row":
        return ref.at[pl.ds(pl.multiple_of(t * TILE, TILE), TILE), :]
    if kind == "col":
        return ref.at[:, pl.ds(pl.multiple_of(t * TILE, TILE), TILE)]
    if isinstance(kind, tuple):
        width = kind[1]
        return ref.at[:, pl.ds(pl.multiple_of(t * width, width), width)]
    return ref


def block_of(kind, shape, tile):
    if kind == "any":
        return pl.BlockSpec(memory_space=pl.ANY)
    if kind == "row":
        return pl.BlockSpec((tile, shape[1]), lambda i, *_: (i, 0))
    if kind == "col":
        return pl.BlockSpec((shape[0], tile), lambda i, *_: (0, i))
    if isinstance(kind, tuple) and kind[0] == "lane":
        return pl.BlockSpec((shape[0], kind[1]), lambda i, *_: (0, i))
    if isinstance(kind, tuple) and kind[0] == "cut":
        _, dim, width, at = kind
        block = (shape[0], width) if dim else (width, shape[1])
        return pl.BlockSpec(block, lambda i, *_: (0, at) if dim else (at, 0))
    if isinstance(kind, tuple):
        return pl.BlockSpec((None,) + shape[1:], lambda i, *_: (kind[1],) + (0,) * (len(shape) - 1))
    return pl.BlockSpec(shape, lambda i, *_: (0,) * len(shape))


def run(
    body, name, scalars, inputs, in_specs, out_specs, outs, scratch, grid, flops, count=0, piped=False
):
    tile = BIG_TILE if name in BIG else TILE
    size = sum(math.prod(o.shape) * o.dtype.itemsize for o in outs)
    size += sum(math.prod(o.shape) * o.dtype.itemsize for o in inputs)
    lead = len(scalars)
    cost = pl.CostEstimate(flops=int(flops), bytes_accessed=int(size), transcendentals=int(count))
    params = pltpu.CompilerParams(vmem_limit_bytes=LIMIT)
    if piped or grid[0] > 1:
        inputs = [pltpu.with_memory_space_constraint(v, pltpu.HBM) for v in inputs]
        outs = [pltpu.HBM(v.shape, v.dtype) for v in outs]
        return pl.pallas_call(
            lambda *refs: body(pl.program_id(0), *refs),
            grid_spec=pltpu.PrefetchScalarGridSpec(
                num_scalar_prefetch=lead,
                grid=grid,
                in_specs=[block_of(k, v.shape, tile) for k, v in zip(in_specs, inputs)],
                out_specs=[block_of(k, v.shape, tile) for k, v in zip(out_specs, outs)],
                scratch_shapes=scratch,
            ),
            out_shape=outs,
            cost_estimate=cost,
            compiler_params=params,
            name=name,
        )(*scalars, *inputs)
    kinds = list(in_specs) + list(out_specs)

    def kernel(*refs):
        held = refs[lead : lead + len(kinds)]
        rest = refs[lead + len(kinds) :]

        def step(t, carry):
            views = [view(ref, kind, t) for ref, kind in zip(held, kinds)]
            body(t, *refs[:lead], *views, *rest)
            return carry

        if grid[0] == 1:
            step(0, 0)
        else:
            lax.fori_loop(0, grid[0], step, 0)

    vmem = pl.BlockSpec(memory_space=pltpu.VMEM)
    place = lambda kind: pl.BlockSpec(memory_space=pl.ANY) if kind == "any" else vmem
    return pl.pallas_call(
        kernel,
        in_specs=[pl.BlockSpec(memory_space=pltpu.SMEM)] * lead + [place(k) for k in in_specs],
        out_specs=[vmem] * len(outs),
        out_shape=outs,
        scratch_shapes=scratch,
        cost_estimate=cost,
        compiler_params=params,
        name=name,
    )(*scalars, *inputs)


def ff_forward_body(t, me, x, norms, *refs, rel, er, sr):
    n = len(rel)
    parts = refs[:n]
    x1, hidden, before, active, w_in, w_out, sems = refs[n:]
    copies, later = [], []
    for k, r in enumerate(rel):
        copies += column_blocks(parts[k], me[0] ^ r, w_in, er)
        later += row_block(parts[k], me[0] ^ r, w_out, sr, 4 * er)
    split = len(copies)
    copies += later
    ready = load_once(t, copies, sems)
    value = x[...].astype(f32)
    normed, _ = normalize(value)
    h = (normed * norms[0:1, :] + norms[1:2, :]).astype(bf16)
    hidden[...] = h
    ready(0, split)
    total = None
    for j in range(w_in.shape[1] // 512):
        cols = slice(512 * j, 512 * (j + 1))
        a = mm(h, w_in[:, cols])
        s = (a * sigmoid(a)).astype(bf16)
        before[:, cols] = a.astype(bf16)
        active[:, cols] = s
        if j == 0:
            ready(split)
        part = mm(s, w_out[cols, :])
        total = part if total is None else total + part
    x1[...] = value + 0.5 * total


def ff_forward(me, x, norms, parts, rel):
    rows, d = x.shape
    er, sr = d // len(rel), 4 * d // len(rel)
    ff = sr * len(rel)
    return run(
        functools.partial(ff_forward_body, rel=rel, er=er, sr=sr),
        "ff_forward",
        (me,),
        (x, norms, *parts),
        [row_spec(d), whole(*norms.shape)] + anywhere(len(rel)),
        [row_spec(d), row_spec(d), row_spec(ff), row_spec(ff)],
        [
            out_shape(rows, d),
            out_shape(rows, d, dtype=bf16),
            out_shape(rows, ff, dtype=bf16),
            out_shape(rows, ff, dtype=bf16),
        ],
        [pltpu.VMEM((d, ff), bf16), pltpu.VMEM((ff, d), bf16), pltpu.SemaphoreType.DMA((5 * len(rel),))],
        (rows // BIG_TILE,),
        4 * rows * d * ff,
        rows * ff,
        True,
    )


def qkv_body(t, me, x1, norms, cs, sn, *refs, rel, ar):
    n = len(rel)
    parts = refs[:n]
    hidden, q, k, v, kt, w, sems = refs[n:]
    copies = []
    for j, r in enumerate(rel):
        copies += column_blocks(parts[j], me[0] ^ r, w, ar)
    ready = load_once(t, copies, sems)
    normed, _ = normalize(x1[...])
    h = (normed * norms[2:3, :] + norms[3:4, :]).astype(bf16)
    hidden[...] = h
    ready()
    c, s = cs[...], sn[...]
    for p in range(4):
        cols = slice(128 * p, 128 * (p + 1))
        a = mm(h, w[:, 128 * p : 128 * (p + 1)])
        q[:, cols] = ((a * c + partner(a) * s).astype(bf16) * 0.125).astype(bf16)
        a = mm(h, w[:, 512 + 128 * p : 512 + 128 * (p + 1)])
        turned = (a * c + partner(a) * s).astype(bf16)
        k[:, cols] = turned
        kt[cols, :] = turned.T
    v[...] = mm(h, w[:, 1024:1536]).astype(bf16)


def qkv(me, x1, norms, cs, sn, parts, rel):
    rows, d = x1.shape
    ar = parts[0].shape[0] // 4
    half = lambda: out_shape(rows, d, dtype=bf16)
    return run(
        functools.partial(qkv_body, rel=rel, ar=ar),
        "query_key_value",
        (me,),
        (x1, norms, cs, sn, *parts),
        [row_spec(d), whole(*norms.shape), row_spec(128), row_spec(128)] + anywhere(len(rel)),
        [row_spec(d)] * 4 + ["col"],
        [half(), half(), half(), half(), out_shape(d, rows, dtype=bf16)],
        [pltpu.VMEM((d, 3 * d), bf16), pltpu.SemaphoreType.DMA((3 * len(rel),))],
        (rows // TILE,),
        6 * rows * d * d,
    )


def attention_body(t, ends, me, q, k, v, x1, *refs, rel, ar, rows):
    n = len(rel)
    parts = refs[:n]
    x2, mixed, lse, w, sems = refs[n:]
    copies = []
    for j, r in enumerate(rel):
        copies += row_block(parts[j], me[0] ^ r, w, ar, 3 * ar)
    ready = load_once(t, copies, sems)
    e = [ends[j] for j in range(4)]
    first = t * TILE
    lo, hi = key_range(first, first + TILE - 1, e, rows)
    sq = seg_of(first + lax.broadcasted_iota(jnp.int32, (1, TILE), 1), e)
    low = lax.broadcasted_iota(jnp.int32, (1, 128), 1) < 64
    zero = jnp.zeros((), bf16)

    def body(start, w_keys):
        keys = pl.ds(start, w_keys)
        same = seg_of(start + lax.broadcasted_iota(jnp.int32, (w_keys, 1), 0), e) == sq

        def pair(p, carry):
            cols = pl.ds(pl.multiple_of(128 * p, 128), 128)
            qp, kp, vp = q[:, cols], k[keys, cols], v[keys, cols]
            both = None
            for h in range(2):
                head = 2 * p + h
                pick = low if h == 0 else jnp.logical_not(low)
                s = jnp.where(same, mm_nt(kp, jnp.where(pick, qp, zero)), masked_score)
                top = jnp.max(s, axis=0, keepdims=True)
                expo = jnp.exp(s - top)
                total = col_sum(expo)
                lse[pl.ds(head, 1), :] = top + jnp.log(total)
                prob = (expo * (1.0 / total)).astype(bf16)
                part = mm_tn(prob, jnp.where(pick, vp, zero))
                both = part if both is None else both + part
            mixed[:, cols] = both.astype(bf16)
            return carry

        lax.fori_loop(0, 4, pair, 0, unroll=2)

    in_window(lo, hi, rows, body)
    ready()
    x2[...] = x1[...] + mm(mixed[...], w[...])


def attention(ends, me, q, k, v, x1, parts, rel):
    rows, d = q.shape
    ar = parts[0].shape[0] // 4
    return run(
        functools.partial(attention_body, rel=rel, ar=ar, rows=rows),
        "attention_forward",
        (ends, me),
        (q, k, v, x1, *parts),
        [row_spec(d), whole(rows, d), whole(rows, d), row_spec(d)] + anywhere(len(rel)),
        [row_spec(d), row_spec(d), "col"],
        [out_shape(rows, d), out_shape(rows, d, dtype=bf16), out_shape(HEADS, rows)],
        [pltpu.VMEM((d, d), bf16), pltpu.SemaphoreType.DMA((len(rel),))],
        (rows // TILE,),
        16 * rows * rows * d // 4,
        HEADS * rows * rows,
    )


def attention_back_body(t, ends, q, k, kt, v, do, lse, delta, cs, sn, gp, dqt, *, rows, pairs, base):
    e = [ends[j] for j in range(4)]
    first = pl.multiple_of(t * TILE, TILE)
    lo, hi = key_range(first, first + TILE - 1, e, rows)
    sk = seg_of(first + lax.broadcasted_iota(jnp.int32, (TILE, 1), 0), e)
    low = lax.broadcasted_iota(jnp.int32, (1, 128), 1) < 64
    here = pl.ds(first, TILE)
    zero = jnp.zeros((), bf16)

    @pl.when(t == 0)
    def _():
        dqt[...] = jnp.zeros_like(dqt)

    def body(start, w):
        qs = pl.ds(start, w)
        same = sk == seg_of(start + lax.broadcasted_iota(jnp.int32, (1, w), 1), e)

        def pair(p, carry):
            held = pl.ds(pl.multiple_of(128 * p, 128), 128)
            qp, dop = q[qs, held], do[qs, held]
            kp, vp = k[here, held], v[here, held]
            gk, gv = None, None
            for h in range(2):
                head = 2 * p + h
                full = 2 * base + head
                pick = low if h == 0 else jnp.logical_not(low)
                qm, dom = jnp.where(pick, qp, zero), jnp.where(pick, dop, zero)
                hr = pl.ds(pl.multiple_of(64 * head, 64), 64)
                expo = jnp.exp(mm_nt(kp, qm) - lse[pl.ds(full, 1), qs])
                prob = jnp.where(same, expo, 0.0)
                ds = (prob * (mm_nt(vp, dom) - delta[pl.ds(full, 1), qs])).astype(bf16)
                v_part = mm(prob.astype(bf16), dom)
                k_part = mm(ds, qm)
                dqt[hr, qs] += mm(kt[hr, here], ds)
                gv = v_part if gv is None else gv + v_part
                gk = k_part if gk is None else gk + k_part
            c, s = cs[here, :], sn[here, :]
            gp[here, pl.ds(pl.multiple_of(128 * (2 * pairs + p), 128), 128)] = gv.astype(bf16)
            turned = gk * c - partner(gk) * s
            gp[here, pl.ds(pl.multiple_of(128 * (pairs + p), 128), 128)] = turned.astype(bf16)
            return carry

        lax.fori_loop(0, pairs, pair, 0, unroll=2)

    in_window(lo, hi, rows, body)

    @pl.when(t == rows // TILE - 1)
    def _():
        c, s = cs[...] * 0.125, sn[...] * 0.125
        for p in range(pairs):
            cols = slice(128 * p, 128 * (p + 1))
            g = dqt[cols, :].T
            gp[:, cols] = (g * c - partner(g) * s).astype(bf16)


def attention_back(ends, q, k, kt, v, do, lse, delta, cs, sn, base, pairs):
    rows, d = q.shape
    wide, at = 128 * pairs, base // pairs
    return run(
        functools.partial(attention_back_body, rows=rows, pairs=pairs, base=base),
        "attention_backward",
        (ends,),
        (q, k, kt, v, do, lse, delta, cs, sn),
        [("cut", 1, wide, at)] * 2
        + [("cut", 0, wide, at)]
        + [("cut", 1, wide, at)] * 2
        + [whole(HEADS, rows)] * 2
        + [whole(rows, 128)] * 2,
        [whole(rows, 3 * wide)],
        [out_shape(rows, 3 * wide, dtype=bf16)],
        [pltpu.VMEM((wide, rows), f32)],
        (rows // TILE,),
        10 * rows * rows * d * pairs // 4,
        HEADS * rows * rows * pairs // 4,
    )[0]


def spaced_rows(rows):
    return rows + 6 * GAP


def group_segments(row, ends):
    return seg_of(row + lax.broadcasted_iota(jnp.int32, (8, 128), 0), ends)


def spread_all(groups, first, spans, ends, read, buf):
    def put(s, row, seg, values):
        at = pl.ds(pl.multiple_of(GAP + GAP * s + row, 8), 8)
        keep = seg == s
        for c in range(4):
            buf[c, at, :] = jnp.where(keep, values[c], 0.0)

    def one(g, carry):
        row = 8 * (first + g)
        seg = group_segments(row, ends)
        values = read(g)
        put(spans[0, first + g], row, seg, values)
        put(spans[1, first + g], row, seg, values)
        return carry

    lax.fori_loop(0, groups, one, 0, unroll=4)

    @pl.when(spans[2, 0] > 1)
    def _():
        def rest(g, carry):
            row = 8 * (first + g)
            seg = group_segments(row, ends)
            values = read(g)

            def fix(s, inner):
                put(s, row, seg, values)
                return inner

            return lax.fori_loop(spans[0, first + g] + 1, spans[1, first + g], fix, carry)

        lax.fori_loop(0, groups, rest, 0)


def collect_all(groups, first, spans, ends, buf, out):
    def one(g, carry):
        row = 8 * (first + g)
        seg = group_segments(row, ends)
        lo, hi = spans[0, first + g], spans[1, first + g]
        keep = seg == lo
        a = pl.ds(pl.multiple_of(GAP + GAP * lo + row, 8), 8)
        b = pl.ds(pl.multiple_of(GAP + GAP * hi + row, 8), 8)
        to = pl.ds(pl.multiple_of(8 * g, 8), 8)
        for c in range(4):
            out[to, 128 * c : 128 * (c + 1)] = jnp.where(keep, buf[c, a, :], buf[c, b, :])
        return carry

    lax.fori_loop(0, groups, one, 0, unroll=4)

    @pl.when(spans[2, 0] > 1)
    def _():
        def rest(g, carry):
            row = 8 * (first + g)
            seg = group_segments(row, ends)
            to = pl.ds(pl.multiple_of(8 * g, 8), 8)

            def fix(s, inner):
                a = pl.ds(pl.multiple_of(GAP + GAP * s + row, 8), 8)
                for c in range(4):
                    cols = slice(128 * c, 128 * (c + 1))
                    out[to, cols] = jnp.where(seg == s, buf[c, a, :], out[to, cols])
                return inner

            return lax.fori_loop(spans[0, first + g] + 1, spans[1, first + g], fix, carry)

        lax.fori_loop(0, groups, rest, 0)


CHUNK = 8


def slide(src, taps, dst, rows, shift, reverse):
    span = 8 * CHUNK

    def step(i, carry):
        c = i // ((rows + 4 * GAP) // span)
        base = pl.multiple_of((i - c * ((rows + 4 * GAP) // span)) * span, 8)
        acc = [jnp.zeros((8, 128), f32) for _ in range(CHUNK)]
        for b in range(8):
            loads = [
                src[c, pl.ds(base + (shift + b + 8 * m), 8), :] for m in range(CHUNK + 3)
            ]
            for a in range(4):
                j = 8 * a + b
                j = TAPS - 1 - j if reverse else j
                w = jnp.broadcast_to(taps[c, j : j + 1, :], (8, 128))
                for m in range(CHUNK):
                    acc[m] = acc[m] + w * loads[m + a]
        for m in range(CHUNK):
            dst[c, pl.ds(base + GAP + 8 * m, 8), :] = acc[m]
        return carry

    lax.fori_loop(0, 4 * ((rows + 4 * GAP) // span), step, 0)


def tap_sums(grad, src, out, rows):
    span = 8 * CHUNK

    def lanes(c, carry):
        def step(i, acc):
            acc = list(acc)
            base = pl.multiple_of(i * span, 8)
            g = [grad[c, pl.ds(base + GAP + 8 * m, 8), :] for m in range(CHUNK)]
            for b in range(8):
                loads = [src[c, pl.ds(base + (b + 8 * m), 8), :] for m in range(CHUNK + 3)]
                for a in range(4):
                    j = 8 * a + b
                    for m in range(CHUNK):
                        acc[j] = acc[j] + g[m] * loads[m + a]
            return tuple(acc)

        zeros = tuple(jnp.zeros((8, 128), f32) for _ in range(TAPS))
        acc = lax.fori_loop(0, (rows + 4 * GAP) // span, step, zeros)
        for j in range(TAPS):
            out[c, j : j + 1, :] = col_sum(acc[j])
        return carry

    lax.fori_loop(0, 4, lanes, 0)


def conv_front_body(t, ends, me, spans, x2, norms, taps, *refs, rel, ar, rows):
    n = len(rel)
    parts = refs[:n]
    hidden, gates_out, conv, spaced, stats, glu, answer, w, sems = refs[n:]
    copies = []
    for j, r in enumerate(rel):
        copies += column_blocks(parts[j], me[0] ^ r, w, ar)
    ready = load_once(t, copies, sems)
    e = [ends[j] for j in range(4)]

    @pl.when(t == 0)
    def _():
        spaced[...] = jnp.zeros_like(spaced)

    normed, _ = normalize(x2[...])
    h = (normed * norms[4:5, :] + norms[5:6, :]).astype(bf16)
    hidden[...] = h
    ready()
    half = mm(h, w[:, :512])
    gate = mm(h, w[:, 512:])
    gates_out[:, :512] = half.astype(bf16)
    gates_out[:, 512:] = gate.astype(bf16)
    glu[...] = half * sigmoid(gate)

    def read(g):
        at = pl.ds(pl.multiple_of(8 * g, 8), 8)
        return [glu[at, 128 * c : 128 * (c + 1)] for c in range(4)]

    spread_all(TILE // 8, t * (TILE // 8), spans, e, read, spaced)

    @pl.when(t == rows // TILE - 1)
    def _():
        slide(spaced, taps, answer, rows, 0, False)
        collect_all(rows // 8, 0, spans, e, answer, conv)
        keep = lax.broadcasted_iota(jnp.int32, (rows, 1), 0) < e[3]
        kept = jnp.where(keep, conv[...], 0.0)
        stats[0:1, :] = col_sum(kept)
        stats[1:2, :] = col_sum(kept * kept)
        stats[2:3, :] = jnp.full((1, 512), e[3], jnp.int32).astype(f32)


def conv_front(ends, me, spans, x2, norms, taps, parts, rel):
    rows, d = x2.shape
    ar = parts[0].shape[0] // 3
    far = spaced_rows(rows)
    return run(
        functools.partial(conv_front_body, rel=rel, ar=ar, rows=rows),
        "gated_convolution",
        (ends, me, spans),
        (x2, norms, taps, *parts),
        [row_spec(d), whole(*norms.shape), whole(4, TAPS, 128)] + anywhere(len(rel)),
        [row_spec(d), row_spec(2 * d), whole(rows, d), whole(4, far, 128), whole(3, d)],
        [
            out_shape(rows, d, dtype=bf16),
            out_shape(rows, 2 * d, dtype=bf16),
            out_shape(rows, d),
            out_shape(4, far, 128),
            out_shape(3, d),
        ],
        [
            pltpu.VMEM((TILE, d), f32),
            pltpu.VMEM((4, far, 128), f32),
            pltpu.VMEM((d, 2 * d), bf16),
            pltpu.SemaphoreType.DMA((2 * len(rel),)),
        ],
        (rows // TILE,),
        8 * rows * d * d,
        rows * d,
    )


def conv_back_body(t, ends, spans, gz, conv, batch, totals, norms, taps, far, g_glu, tap_grad, grad, spaced, sem, *, rows):
    arriving = pltpu.make_async_copy(far, spaced, sem.at[0])
    arriving.start()
    e = [ends[j] for j in range(4)]
    grad[...] = jnp.zeros_like(grad)
    mean, scale, count = batch[0:1, :], batch[1:2, :], batch[2:3, :]
    bias_all = jnp.sum(totals[:, 0, :], axis=0, keepdims=True) / count
    gain_all = jnp.sum(totals[:, 1, :], axis=0, keepdims=True) / count
    factor = scale * norms[6:7, :]
    per = []
    for c in range(4):
        cols = slice(128 * c, 128 * (c + 1))
        per.append(
            [
                jnp.broadcast_to(v[:, cols], (8, 128))
                for v in (mean, scale, bias_all, gain_all, factor)
            ]
        )

    def read(g):
        row = pl.multiple_of(8 * g, 8)
        keep = row + lax.broadcasted_iota(jnp.int32, (8, 128), 0) < e[3]
        values = []
        for c in range(4):
            cols = slice(128 * c, 128 * (c + 1))
            m, s, b, k, f = per[c]
            zhat = (conv[pl.ds(row, 8), cols] - m) * s
            away = jnp.where(keep, b + zhat * k, 0.0)
            values.append(f * (gz[pl.ds(row, 8), cols] - away))
        return values

    spread_all(rows // 8, 0, spans, e, read, grad)
    slide(grad, taps, g_glu, rows, 1, True)
    arriving.wait()
    tap_sums(grad, spaced, tap_grad, rows)


def conv_back(ends, spans, gz, conv, batch, totals, norms, taps, spaced):
    rows, d = conv.shape
    far = spaced_rows(rows)
    return run(
        functools.partial(conv_back_body, rows=rows),
        "convolution_backward",
        (ends, spans),
        (gz, conv, batch, totals, norms, taps, spaced),
        [whole(rows, d), whole(rows, d), whole(3, d), whole(*totals.shape), whole(*norms.shape)]
        + [whole(4, TAPS, 128), "any"],
        [whole(4, far, 128), whole(4, TAPS, 128)],
        [out_shape(4, far, 128), out_shape(4, TAPS, 128)],
        [
            pltpu.VMEM((4, far, 128), f32),
            pltpu.VMEM((4, far, 128), f32),
            pltpu.SemaphoreType.DMA((1,)),
        ],
        (1,),
        12 * rows * d * TAPS * 40,
        rows * d,
    )


def gates_back_body(t, ends, me, spans, g_glu, norms, gates, x2, g3, mixed, *refs, rel, ar, rows):
    n = len(rel)
    parts, heads = refs[:n], refs[n : 2 * n]
    (g_gates, g2, g_attn, g_mixed, delta, sums) = refs[2 * n : 2 * n + 6]
    glu_rows, w, w_heads, sems = refs[2 * n + 6 :]
    copies = []
    for j, r in enumerate(rel):
        copies += column_blocks(parts[j], me[0] ^ r, w, ar)
        copies += row_block(heads[j], me[0] ^ r, w_heads, ar, 3 * ar)
    ready = load_once(t, copies, sems)
    e = [ends[j] for j in range(4)]

    @pl.when(t == 0)
    def _():
        sums[...] = jnp.zeros_like(sums)

    collect_all(TILE // 8, t * (TILE // 8), spans, e, g_glu, glu_rows)
    gg = glu_rows[...]
    sigma = sigmoid(gates[:, 512:].astype(f32))
    first = (gg * sigma).astype(bf16)
    second = (gg * gates[:, :512].astype(f32) * sigma * (1.0 - sigma)).astype(bf16)
    g_gates[:, :512] = first
    g_gates[:, 512:] = second
    ready()
    g_hidden = mm_nt(first, w[:, :512]) + mm_nt(second, w[:, 512:])
    normed, scale = normalize(x2[...])
    sums[0:1, :] += col_sum(g_hidden * normed)
    sums[1:2, :] += col_sum(g_hidden)
    out = g3[...] + norm_back(g_hidden, norms[4:5, :], normed, scale)
    g2[...] = out
    branch = out.astype(bf16)
    g_attn[...] = branch
    gm = mm_nt(branch, w_heads[...]).astype(bf16)
    g_mixed[...] = gm
    dots = gm.astype(f32) * mixed[...].astype(f32)
    upper = dots.astype(bf16)
    lower = (dots - upper.astype(f32)).astype(bf16)
    head = lax.broadcasted_iota(jnp.int32, (HEADS, 512), 0)
    ones = (lax.broadcasted_iota(jnp.int32, (HEADS, 512), 1) // 64 == head).astype(bf16)
    delta[...] = mm_nt(ones, upper) + mm_nt(ones, lower)


def gates_back(ends, me, spans, g_glu, norms, gates, x2, g3, mixed, parts, heads, rel):
    rows, d = x2.shape
    ar = parts[0].shape[0] // 3
    return run(
        functools.partial(gates_back_body, rel=rel, ar=ar, rows=rows),
        "gates_backward",
        (ends, me, spans),
        (g_glu, norms, gates, x2, g3, mixed, *parts, *heads),
        [whole(*g_glu.shape), whole(*norms.shape), row_spec(2 * d)]
        + [row_spec(d)] * 3
        + anywhere(2 * len(rel)),
        [row_spec(2 * d), row_spec(d), row_spec(d), row_spec(d)]
        + ["col", whole(2, d)],
        [
            out_shape(rows, 2 * d, dtype=bf16),
            out_shape(rows, d),
            out_shape(rows, d, dtype=bf16),
            out_shape(rows, d, dtype=bf16),
            out_shape(HEADS, rows),
            out_shape(2, d),
        ],
        [
            pltpu.VMEM((TILE, d), f32),
            pltpu.VMEM((d, 2 * d), bf16),
            pltpu.VMEM((d, d), bf16),
            pltpu.SemaphoreType.DMA((3 * len(rel),)),
        ],
        (rows // TILE,),
        6 * rows * d * d,
        rows * d,
    )


def rear_body(t, ends, me, conv, totals, x2, cot, norms, *refs, rel, ar, er, sr):
    n = len(rel)
    points, ffs = refs[:n], refs[n : 2 * n]
    (y, g_third, g_zed, wact, branch_out, hidden, active, g_before, g_out, sums, batch) = refs[2 * n : 2 * n + 11]
    w_point, w_in, w_out, slope, sems = refs[2 * n + 11 :]
    copies, later, last_ones = [], [], []
    for j, r in enumerate(rel):
        copies += row_block(points[j], me[0] ^ r, w_point, ar, 2 * ar)
        later += column_blocks(ffs[j], me[0] ^ r, w_in, er)
        last_ones += row_block(ffs[j], me[0] ^ r, w_out, sr, 4 * er)
    one, two = len(copies), len(copies) + len(later)
    copies += later + last_ones
    ready = load_once(t, copies, sems)

    @pl.when(t == 0)
    def _():
        sums[...] = jnp.zeros_like(sums)
        total = jnp.sum(totals[...], axis=0)
        count = total[2:3, :]
        mean = total[0:1, :] / count
        batch[0:1, :] = mean
        batch[1:2, :] = lax.rsqrt(total[1:2, :] / count - mean * mean + batch_epsilon)
        batch[2:3, :] = count

    zhat = (conv[...] - batch[0:1, :]) * batch[1:2, :]
    zed = zhat * norms[6:7, :] + norms[7:8, :]
    sigma = sigmoid(zed)
    wa = (zed * sigma).astype(bf16)
    wact[...] = wa
    zed_slope = slope_of(zed, sigma)
    ready(0, one)
    third = x2[...] + mm(wa, w_point[...])
    normed, scale = normalize(third)
    h = (normed * norms[8:9, :] + norms[9:10, :]).astype(bf16)
    hidden[...] = h
    ready(one, two)
    total = None
    for j in range(w_in.shape[1] // 512):
        cols = slice(512 * j, 512 * (j + 1))
        a = mm(h, w_in[:, cols])
        sg = sigmoid(a)
        s = (a * sg).astype(bf16)
        active[:, cols] = s
        slope[:, cols] = slope_of(a, sg)
        if j == 0:
            ready(two)
        part = mm(s, w_out[cols, :])
        total = part if total is None else total + part
    fourth = third + 0.5 * total
    last, last_scale = normalize(fourth)
    keep = t * BIG_TILE + lax.broadcasted_iota(jnp.int32, (BIG_TILE, 1), 0) < ends[3]
    y[...] = jnp.where(keep, last * norms[10:11, :] + norms[11:12, :], 0.0).astype(bf16)
    g_y = jnp.where(keep, cot[...].astype(f32), 0.0)
    sums[0:1, :] += col_sum(g_y * last)
    sums[1:2, :] += col_sum(g_y)
    g_fourth = norm_back(g_y, norms[10:11, :], last, last_scale)
    go = (0.5 * g_fourth).astype(bf16)
    g_out[...] = go
    g_hidden = None
    for j in range(w_in.shape[1] // 512):
        cols = slice(512 * j, 512 * (j + 1))
        gb = (mm_nt(go, w_out[cols, :]) * slope[:, cols]).astype(bf16)
        g_before[:, cols] = gb
        part = mm_nt(gb, w_in[:, cols])
        g_hidden = part if g_hidden is None else g_hidden + part
    sums[2:3, :] += col_sum(g_hidden * normed)
    sums[3:4, :] += col_sum(g_hidden)
    g3 = g_fourth + norm_back(g_hidden, norms[8:9, :], normed, scale)
    g_third[...] = g3
    branch = g3.astype(bf16)
    branch_out[...] = branch
    gz = mm_nt(branch, w_point[...]) * zed_slope
    g_zed[...] = gz
    sums[4:5, :] += col_sum(gz)
    sums[5:6, :] += col_sum(gz * zhat)


def rear(ends, me, conv, totals, x2, cot, norms, points, ffs, rel):
    rows, d = x2.shape
    ar = points[0].shape[0] // 3
    ff = 4 * d
    er, sr = d // len(rel), ff // len(rel)
    return run(
        functools.partial(rear_body, rel=rel, ar=ar, er=er, sr=sr),
        "norm_feed_forward_and_back",
        (ends, me),
        (conv, totals, x2, cot, norms, *points, *ffs),
        [row_spec(d), whole(*totals.shape), row_spec(d), row_spec(d), whole(*norms.shape)]
        + anywhere(2 * len(rel)),
        [row_spec(d)] * 6 + [row_spec(ff), row_spec(ff), row_spec(d), whole(6, d), whole(3, d)],
        [
            out_shape(rows, d, dtype=bf16),
            out_shape(rows, d),
            out_shape(rows, d),
            out_shape(rows, d, dtype=bf16),
            out_shape(rows, d, dtype=bf16),
            out_shape(rows, d, dtype=bf16),
            out_shape(rows, ff, dtype=bf16),
            out_shape(rows, ff, dtype=bf16),
            out_shape(rows, d, dtype=bf16),
            out_shape(6, d),
            out_shape(3, d),
        ],
        [
            pltpu.VMEM((d, d), bf16),
            pltpu.VMEM((d, ff), bf16),
            pltpu.VMEM((ff, d), bf16),
            pltpu.VMEM((BIG_TILE, ff), f32),
            pltpu.SemaphoreType.DMA((6 * len(rel),)),
        ],
        (rows // BIG_TILE,),
        rows * d * (8 * ff + 4 * d),
        rows * ff,
        True,
    )


def qkv_back_body(t, me, ga, gb, x1, g2, norms, *refs, rel, ar):
    n = len(rel)
    attn = refs[:n]
    g1, g_out, sums, w, sems = refs[n:]
    copies = []
    for j, r in enumerate(rel):
        copies += column_blocks(attn[j], me[0] ^ r, w, ar)
    ready = load_once(t, copies, sems)

    @pl.when(t == 0)
    def _():
        sums[...] = jnp.zeros_like(sums)

    normed, scale = normalize(x1[...])
    ready()
    g_hidden = None
    for z in range(3):
        for half, g in enumerate((ga, gb)):
            cols = slice(512 * z + 256 * half, 512 * z + 256 * (half + 1))
            part = mm_nt(g[:, 256 * z : 256 * (z + 1)], w[:, cols])
            g_hidden = part if g_hidden is None else g_hidden + part
    sums[0:1, :] += col_sum(g_hidden * normed)
    sums[1:2, :] += col_sum(g_hidden)
    out = g2[...] + norm_back(g_hidden, norms[2:3, :], normed, scale)
    g1[...] = out
    g_out[...] = (0.5 * out).astype(bf16)


def qkv_back(me, ga, gb, x1, g2, norms, attn, rel):
    rows, d = x1.shape
    ar = d // len(rel)
    return run(
        functools.partial(qkv_back_body, rel=rel, ar=ar),
        "query_key_value_backward",
        (me,),
        (ga, gb, x1, g2, norms, *attn),
        [row_spec(3 * d // 2)] * 2 + [row_spec(d)] * 2 + [whole(*norms.shape)] + anywhere(len(rel)),
        [row_spec(d), row_spec(d), whole(2, d)],
        [out_shape(rows, d), out_shape(rows, d, dtype=bf16), out_shape(2, d)],
        [pltpu.VMEM((d, 3 * d), bf16), pltpu.SemaphoreType.DMA((3 * len(rel),))],
        (rows // TILE,),
        6 * rows * d * d,
    )


def ff_back_body(t, me, g1, go, x, before, norms, qkv_sums, conv_sums, rear_sums, tap_grad, *refs, rel, er, sr, steps):
    n = len(rel)
    parts = refs[:n]
    g_frames, g_before, small, sums, w_in, w_out, sems = refs[n:]
    copies, later = [], []
    for j, r in enumerate(rel):
        copies += row_block(parts[j], me[0] ^ r, w_out, sr, 4 * er)
        later += column_blocks(parts[j], me[0] ^ r, w_in, er)
    split = len(copies)
    copies += later
    ready = load_once(t, copies, sems)

    @pl.when(t == 0)
    def _():
        sums[...] = jnp.zeros_like(sums)

    out = go[...]
    ready(0, split)
    g_hidden = None
    for j in range(w_in.shape[1] // 512):
        cols = slice(512 * j, 512 * (j + 1))
        a = before[:, cols].astype(f32)
        gb = (mm_nt(out, w_out[cols, :]) * slope_of(a, sigmoid(a))).astype(bf16)
        g_before[:, cols] = gb
        if j == 0:
            ready(split)
        part = mm_nt(gb, w_in[:, cols])
        g_hidden = part if g_hidden is None else g_hidden + part
    normed, scale = normalize(x[...].astype(f32))
    sums[0:1, :] += col_sum(g_hidden * normed)
    sums[1:2, :] += col_sum(g_hidden)
    g_frames[...] = g1[...] + norm_back(g_hidden, norms[0:1, :], normed, scale)

    @pl.when(t == steps - 1)
    def _():
        for c in range(tap_grad.shape[0]):
            small[:TAPS, 128 * c : 128 * (c + 1)] = tap_grad[c, :, :]
        rows = [sums[0:1, :], sums[1:2, :], qkv_sums[...], conv_sums[...], rear_sums[5:6, :]]
        rows += [rear_sums[4:5, :], rear_sums[2:4, :], rear_sums[0:2, :]]
        at = TAPS
        for row in rows:
            small[at : at + row.shape[0], :] = row
            at += row.shape[0]


def ff_back(me, g1, go, x, before, norms, sums, parts, rel):
    rows, d = x.shape
    ff = 4 * d
    er, sr = d // len(rel), ff // len(rel)
    return run(
        functools.partial(ff_back_body, rel=rel, er=er, sr=sr, steps=rows // TILE),
        "feed_forward_backward",
        (me,),
        (g1, go, x, before, norms, *sums, *parts),
        [row_spec(d), row_spec(d), row_spec(d), row_spec(ff), whole(*norms.shape)]
        + ["whole"] * len(sums)
        + anywhere(len(rel)),
        [row_spec(d), row_spec(ff), whole(TAPS + 12, d)],
        [out_shape(rows, d), out_shape(rows, ff, dtype=bf16), out_shape(TAPS + 12, d)],
        [
            pltpu.VMEM((2, d), f32),
            pltpu.VMEM((d, ff), bf16),
            pltpu.VMEM((ff, d), bf16),
            pltpu.SemaphoreType.DMA((5 * len(rel),)),
        ],
        (rows // TILE,),
        4 * rows * d * ff,
        rows * ff,
        True,
    )


def place_owners(me, tile, keep, send, base, height, owners, first):
    for k in range(owners):
        owner = first + k
        rows = tile[k * height : (k + 1) * height, :]
        mine = ((owner ^ me[0]) & 1) == 0

        @pl.when(mine)
        def _(rows=rows, owner=owner):
            keep[owner >> 1, pl.ds(base, height), :] = rows

        @pl.when(jnp.logical_not(mine))
        def _(rows=rows, owner=owner):
            send[owner >> 1, pl.ds(base, height), :] = rows


def weight_grad_body(t, me, *refs, fs, parts, n1, n2, extra):
    refs = list(refs)
    first = [refs.pop(0) for _ in range(1 + parts)] if n1 else None
    second = [refs.pop(0) for _ in range(2)] if n2 else None
    more = refs.pop(0) if extra else None
    keep, send = refs.pop(0), refs.pop(0)
    er = 512 // fs
    if n1:
        base = pl.multiple_of(t * er, er)
        tiles = [mm_tn(first[0][...], ref[...]).astype(bf16) for ref in first[1:]]
        tile = tiles[0] if parts == 1 else jnp.concatenate(tiles, axis=1)
        place_owners(me, tile, keep, send, base, er, fs, 0)
    if n2:
        sr = 512 * n2 // fs
        per = max(1, 512 // sr)

        def one(block):
            tile = mm_tn(second[0][...], second[1][...]).astype(bf16)
            place_owners(me, tile, keep, send, n1 * er, sr, per, block * per)

        if n1 in (0, n2):
            one(t)
        else:
            pl.when(t == 0)(lambda: one(0))
    if extra:

        @pl.when(t == 0)
        def _():
            tile = more[...].reshape(fs * extra, 512)
            place_owners(me, tile, keep, send, (n1 + n2) * er, extra, fs, 0)


def weight_grad(name, me, fs, first=None, second=None, more=None):
    inputs, specs = [], []
    n1 = n2 = parts = 0
    if first:
        h, gs = first
        rows, parts = h.shape[0], len(gs)
        wide = 512 // parts
        n1 = gs[0].shape[1] // wide
        inputs += [h, *gs]
        specs += [whole(rows, 512)] + [("lane", wide)] * parts
    if second:
        s, o = second
        rows = s.shape[0]
        n2 = s.shape[1] // 512
        inputs += [s, o]
        stepped = n1 in (0, n2)
        specs += [("lane", 512) if stepped else "whole", whole(rows, 512)]
    extra = 0
    if more is not None:
        extra = more.shape[1]
        inputs.append(more)
        specs.append("whole")
    height = (n1 + n2) * 512 // fs + extra
    return run(
        functools.partial(weight_grad_body, fs=fs, parts=parts, n1=n1, n2=n2, extra=extra),
        name,
        (me,),
        inputs,
        specs,
        [whole(fs // 2, height, 512)] * 2,
        [out_shape(fs // 2, height, 512, dtype=bf16)] * 2,
        [],
        (n1 or n2,),
        2 * rows * 512 * 512 * (n1 + n2),
        0,
        n1 == n2,
    )


def join(*pairs):
    return tuple(jnp.concatenate(list(side), axis=1) for side in zip(*pairs))


def bits_of(size):
    return int(size).bit_length() - 1


def swap(value, axis, size, mask):
    return lax.ppermute(value, axis, [(k, k ^ mask) for k in range(size)])


def relative(fs):
    rel = [0]
    for bit in reversed(range(bits_of(fs))):
        rel = rel + [r ^ (1 << bit) for r in rel]
    return tuple(rel)


def first_part(own, fs):
    parts = [own]
    for bit in reversed(range(1, bits_of(fs))):
        parts = parts + [swap(part, "fsdp", fs, 1 << bit) for part in parts]
    return parts


def second_part(parts, fs):
    return parts + [swap(part, "fsdp", fs, 1) for part in parts]


def sum_of(parts):
    total = parts[0].astype(f32)
    for part in parts[1:]:
        total = total + part.astype(f32)
    return total.astype(bf16)


class Chain:
    def __init__(self, pair, fs, dp):
        keep, send = pair
        self.fs, self.dp = fs, dp
        self.me, self.pack = lax.axis_index("fsdp"), lax.axis_index("dp")
        zero = jnp.int32(0)
        self.at, self.size = [zero, zero], list(keep.shape[:2])
        self.parts = [(keep, zero, zero)]
        self.stages = [("fsdp", bit, "halve") for bit in reversed(range(1, bits_of(fs)))]
        last = bits_of(dp) - 1
        self.stages += [("dp", bit, "halve") for bit in range(last)] + [("dp", last, "add")]
        self.stages += [("dp", bit, "join") for bit in reversed(range(last))]
        self.flight = swap(send, "fsdp", fs, 1)
        self.joining = None

    def take(self, y, r):
        shape = (self.size[0], self.size[1], 512)
        return sum_of(
            [lax.dynamic_slice(part, (y - y0, r - r0, 0), shape) for part, y0, r0 in self.parts]
        )

    def hold(self, *tokens):
        self.flight = after(self.flight, *tokens)

    def advance(self):
        if not self.stages:
            return None
        self.settle()
        axis, bit, kind = self.stages.pop(0)
        size, index = (self.fs, self.me) if axis == "fsdp" else (self.dp, self.pack)
        side = (index >> bit) & 1
        if kind == "halve":
            dim = 0 if axis == "fsdp" else 1
            base = self.at[dim]
            self.size[dim] //= 2
            self.at[dim] = base + (1 - side) * self.size[dim]
            send = self.take(*self.at)
            self.at[dim] = base + side * self.size[dim]
        else:
            if self.joining is None:
                send = self.take(*self.at)
            else:
                send = self.whole
            if kind == "join":
                send = send.reshape(-1, 512)
                self.whole, self.joining = send, side
            else:
                self.parts = [(send, *self.at)]
        self.flight = swap(send, axis, size, 1 << bit)
        return send

    def settle(self):
        if self.joining is None:
            self.parts.append((self.flight, *self.at))
        else:
            pair = [self.whole, self.flight]
            self.whole = jnp.where(
                self.joining == 0, jnp.concatenate(pair, axis=0), jnp.concatenate(pair[::-1], axis=0)
            )

    def result(self):
        while self.stages:
            self.advance()
        self.settle()
        return self.whole


def after(value, *tokens):
    tokens = [token for token in tokens if token is not None]
    return lax.optimization_barrier((value, *tokens))[0]


def from_everyone(rows):
    axes = ("dp", "fsdp")
    count = lax.axis_size(axes)
    spread = jnp.broadcast_to(rows[None], (count,) + rows.shape)
    return lax.all_to_all(spread, axes, 0, 0, tiled=True)


def to_rows(block):
    r, c = block.shape
    k = c // 512
    return block.reshape(r, k, 512).swapaxes(0, 1).reshape(k * r, 512)


def from_rows(rows, r, c):
    k = c // 512
    return rows.reshape(k, r, 512).swapaxes(0, 1).reshape(r, c)


def pack_body(t, a, b, out, *, n, er):
    for j in range(n):
        out[er * j : er * (j + 1), :] = a[:, 512 * j : 512 * (j + 1)].astype(bf16)
    out[er * n :, :] = b[...].astype(bf16)


def pack(name, a, b, index=None):
    er, n = a.shape[-2], a.shape[-1] // 512
    sr = b.shape[-2]
    return run(
        functools.partial(pack_body, n=n, er=er),
        name,
        (),
        (a, b),
        ["whole" if index is None else ("stack", index)] * 2,
        ["whole"],
        [out_shape(n * er + sr, 512, dtype=bf16)],
        [],
        (1,),
        er * n * 1024,
        0,
        True,
    )[0]


def adam_body(*refs):
    ga, gb = refs[0][...], refs[1][...]
    outs = refs[-6:]
    for ref, grad, to in ((refs[2:5], ga, outs[:3]), (refs[5:8], gb, outs[3:])):
        new = adam_update(ref[0][...], ref[1][...], ref[2][...], grad.astype(f32), decay_rate)
        for place, value in zip(to, new):
            place[...] = value


def adam_single_body(*refs):
    outs = refs[-3:]
    new = adam_update(refs[1][...], refs[2][...], refs[3][...], refs[0][...].astype(f32), decay_rate)
    for place, value in zip(outs, new):
        place[...] = value


def adam_single(name, grad, state, by_row, index, into):
    height, width = state[0].shape[-2:]
    n = 4
    block = (height // n, width) if by_row else (height, width // n)
    spec = pl.BlockSpec((None,) + block, lambda i: (index, i, 0) if by_row else (index, 0, i))
    return pl.pallas_call(
        adam_single_body,
        grid=(n,),
        in_specs=[pl.BlockSpec(block, lambda i: (i, 0))] + [spec] * 3 + [pl.BlockSpec(memory_space=pl.ANY)] * 3,
        out_specs=[spec] * 3,
        out_shape=[out_shape(*v.shape) for v in state],
        input_output_aliases={4 + j: j for j in range(3)},
        cost_estimate=pl.CostEstimate(
            flops=20 * height * width, bytes_accessed=26 * height * width, transcendentals=height * width
        ),
        compiler_params=pltpu.CompilerParams(vmem_limit_bytes=(8 if by_row else 48) * 1024 * 1024),
        name=name,
    )(grad, *state, *into)


def adam_pair(name, grad, first, second, steps, index=None, into=None):
    er, n = first[0].shape[-2], first[0].shape[-1] // 512
    sr = second[0].shape[-2]
    part = sr // n if steps else sr
    lead = () if index is None else (None,)
    at = () if index is None else (index,)
    spec_a = pl.BlockSpec(lead + (er, 512), lambda i: at + (0, i))
    spec_b = pl.BlockSpec(lead + (part, 512), lambda i: at + ((i, 0) if steps else (0, 0)))
    grad_a = pl.BlockSpec((er, 512), lambda i: (i, 0))
    grad_b = pl.BlockSpec((part, 512), lambda i: (n * er // part + (i if steps else 0), 0))
    inputs = [grad, grad, *first, *second]
    specs = [grad_a, grad_b] + [spec_a] * 3 + [spec_b] * 3
    alias = {}
    if into is not None:
        alias = {len(inputs) + j: j for j in range(6)}
        inputs += list(into)
        specs += [pl.BlockSpec(memory_space=pl.ANY)] * 6
    return pl.pallas_call(
        adam_body,
        grid=(n,),
        in_specs=specs,
        out_specs=[spec_a] * 3 + [spec_b] * 3,
        out_shape=[out_shape(*v.shape) for v in (*first, *second)],
        input_output_aliases=alias,
        cost_estimate=pl.CostEstimate(
            flops=20 * er * 512 * n, bytes_accessed=26 * (er * n + sr) * 512, transcendentals=er * 512 * n
        ),
        compiler_params=pltpu.CompilerParams(vmem_limit_bytes=8 * 1024 * 1024),
        name=name,
    )(*inputs)


def adam_update(master, first, second_block, grad, decay):
    first_new = beta_first * first + (1.0 - beta_first) * grad
    second_new = beta_second * second_block + (1.0 - beta_second) * grad * grad
    first_hat = first_new / (1.0 - beta_first**STEP)
    second_hat = second_new / (1.0 - beta_second**STEP)
    master_new = master - learn_rate * (
        first_hat / (jnp.sqrt(second_hat) + adam_epsilon) + decay * master
    )
    return (master_new, first_new, second_new)


def moments_only(first, second_block, grad):
    first_new = beta_first * first + (1.0 - beta_first) * grad
    second_new = beta_second * second_block + (1.0 - beta_second) * grad * grad
    return (first_new, second_new)


def rotary_tables(position, half):
    freq = jnp.exp(jnp.arange(half, dtype=f32) * (-math.log(10000.0) / half))
    angle = position.astype(f32)[:, None] * freq[None, :]
    cosine, sine = jnp.cos(angle), jnp.sin(angle)
    return (
        jnp.concatenate([cosine] * 4, axis=1),
        jnp.concatenate([-sine, sine, -sine, sine], axis=1),
    )


def per_device(
    frames,
    cotangent,
    lengths,
    expand,
    expand_first,
    expand_second,
    shrink,
    shrink_first,
    shrink_second,
    attend,
    attend_first,
    attend_second,
    heads_out,
    heads_out_first,
    heads_out_second,
    pointwise,
    pointwise_first,
    pointwise_second,
    pointwise_out,
    pointwise_out_first,
    pointwise_out_second,
    depthwise,
    depthwise_first,
    depthwise_second,
    norm_table,
    norm_table_first,
    norm_table_second,
):
    fs, dp = (lax.axis_size("fsdp"), lax.axis_size("dp"))
    rel = relative(fs)
    er, sr, ar = expand.shape[1], shrink.shape[1], attend.shape[0]
    dr = depthwise.shape[1]
    device = lax.axis_index("fsdp")
    me = device.astype(jnp.int32).reshape(1)
    ends = jnp.cumsum(lengths[0, :4]).astype(jnp.int32)
    rows, width = frames.shape

    early_own = pack("pack_early", expand, shrink, 0)
    ff_zero = first_part(early_own, fs)
    small = jnp.concatenate([after(depthwise, early_own), norm_table], axis=0).astype(bf16)
    tiny_rows = small.shape[0]
    small_parts = second_part(first_part(small, fs), fs)
    places = jnp.arange(rows, dtype=jnp.int32)
    segment = jnp.sum((places[:, None] >= ends[None, :]).astype(jnp.int32), axis=1)
    starts = jnp.concatenate([jnp.zeros((1,), jnp.int32), ends])
    pick = (segment[:, None] == jnp.arange(5, dtype=jnp.int32)[None, :]).astype(jnp.int32)
    position = places - jnp.sum(pick * starts[None, :], axis=1)
    lo, hi = segment[::8], segment[7::8]
    spans = jnp.stack([lo, hi, jnp.broadcast_to(jnp.max(hi - lo), lo.shape)])
    cs, sn = rotary_tables(position, width // HEADS // 2)

    attn_own = pack("pack_attn", attend, heads_out)
    conv_own = pack("pack_conv", pointwise, pointwise_out)
    late_own = pack("pack_late", expand, shrink, 1)
    small_full = jnp.zeros((fs, tiny_rows, dr), bf16)
    for k, r in enumerate(rel):
        small_full = lax.dynamic_update_slice_in_dim(small_full, small_parts[k][None], device ^ r, 0)
    small_full = small_full.swapaxes(0, 1).reshape(tiny_rows, fs * dr).astype(f32)
    norms = small_full[TAPS:]
    taps = small_full[:TAPS].reshape(TAPS, width // 128, 128).swapaxes(0, 1)
    ff_zero = [ff_zero[0]] + [after(part, attn_own, conv_own, late_own, cs, sn, norms, taps) for part in ff_zero[1:]]
    attn_parts = first_part(after(attn_own, *ff_zero), fs)
    ff_zero = second_part(ff_zero, fs)


    x1, hidden_zero, before_zero, active_zero = ff_forward(
        me, frames, norms, ff_zero, rel
    )
    attn_parts = [after(part, x1) for part in attn_parts]
    conv_parts = first_part(after(conv_own, *attn_parts), fs)
    attn_parts = second_part(attn_parts, fs)
    hidden_attn, q, k, v, kt = qkv(me, x1, norms, cs, sn, attn_parts, rel)
    conv_parts = [after(part, q) for part in conv_parts]
    ff_one = first_part(after(late_own, *conv_parts), fs)
    conv_parts = second_part(conv_parts, fs)
    x2, mixed, lse = attention(ends, me, after(q, *conv_parts), k, v, x1, attn_parts, rel)
    hidden_conv, gates, conv, spaced, stats = conv_front(ends, me, spans, x2, norms, taps, conv_parts, rel)
    ff_one = second_part([after(part, stats) for part in ff_one], fs)
    totals = from_everyone(stats)
    (
        layer_output,
        g_third,
        g_zed,
        wact,
        g_branch,
        hidden_one,
        active_one,
        g_before_one,
        g_out_one,
        rear_sums,
        batch,
    ) = rear(ends, me, conv, totals, x2, cotangent, norms, conv_parts, ff_one, rel)
    back_totals = from_everyone(rear_sums[4:6])
    late_pair = weight_grad(
        "weight_grad_late", me, fs, (hidden_one, (g_before_one,)), (active_one, g_out_one)
    )
    late = Chain((late_pair[0], after(late_pair[1], back_totals)), fs, dp)
    g_glu, tap_grad = conv_back(ends, spans, after(g_zed, late_pair[1]), conv, batch, back_totals, norms, taps, spaced)
    g_glu = after(g_glu, late.advance())
    g_gates, g_second, g_attn, g_mixed, delta, conv_sums = gates_back(
        ends, me, spans, g_glu, norms, gates, x2, g_third, mixed, conv_parts, attn_parts, rel
    )
    conv_pair = weight_grad("weight_grad_conv", me, fs, (hidden_conv, (g_gates,)), (wact, g_branch))
    middle = Chain(conv_pair, fs, dp)
    first_half = attention_back(
        ends, q, k, kt, v, after(g_mixed, conv_pair[1]), lse, delta, cs, sn, 0, 2
    )
    late.hold(first_half)
    middle.hold(first_half)
    tokens = (late.advance(), middle.advance(), first_half)
    second_half = attention_back(ends, q, k, kt, v, after(g_mixed, *tokens), lse, delta, cs, sn, 2, 2)
    late.hold(second_half)
    middle.hold(second_half)
    first_half = after(first_half, late.advance(), middle.advance())
    attn_pair = weight_grad(
        "weight_grad_attn", me, fs, (hidden_attn, (first_half, second_half)), (mixed, g_attn)
    )
    attn = Chain(attn_pair, fs, dp)
    g_first, g_out_zero, qkv_sums = qkv_back(
        me, after(first_half, attn_pair[1]), second_half, x1, g_second, norms, attn_parts, rel
    )
    for chain in (late, middle, attn):
        chain.hold(g_first)
    tokens = (late.advance(), middle.advance(), attn.advance())
    out_pair = weight_grad(
        "weight_grad_shrink", me, fs, None, (active_zero, after(g_out_zero, *tokens))
    )
    early_out = Chain(out_pair, fs, dp)
    middle.hold(out_pair[1])
    sums = (qkv_sums, conv_sums, rear_sums, tap_grad)
    frames_grad, g_before_zero, small_grad = ff_back(
        me,
        g_first,
        after(g_out_zero, out_pair[1], early_out.advance()),
        frames,
        before_zero,
        norms,
        sums,
        ff_zero,
        rel,
    )
    for chain in (late, middle, attn, early_out):
        chain.hold(g_before_zero)
    tokens = (attn.flight, early_out.flight, late.flight, middle.flight)
    small_grad = small_grad.astype(bf16).reshape(tiny_rows, fs, dr).swapaxes(0, 1)
    small_size = tiny_rows * dr
    small_pad = -small_size % (512 * 16)
    small_grad = jnp.pad(small_grad.reshape(fs, small_size), ((0, 0), (0, small_pad)))
    small_grad = small_grad.reshape(fs, -1, 512)
    tail_pair = weight_grad(
        "weight_grad_expand",
        me,
        fs,
        (hidden_zero, (after(g_before_zero, *tokens),)),
        None,
        small_grad,
    )
    tail = Chain(tail_pair, fs, dp)
    attn.hold(tail_pair[1])
    early_out.hold(tail_pair[1])
    tail_sent = tail.advance()
    expands = (expand, expand_first, expand_second)
    shrinks = (shrink, shrink_first, shrink_second)

    def hold(*chains):
        for chain in chains:
            chain.hold(tail_sent)

    hold(late, middle, attn, early_out)
    red_late, red_conv = late.result(), middle.result()
    new_late = adam_pair("adam_late", red_late, expands, shrinks, True, 1)
    new_conv = adam_pair(
        "adam_conv",
        red_conv,
        (pointwise, pointwise_first, pointwise_second),
        (pointwise_out, pointwise_out_first, pointwise_out_second),
        False,
    )
    new_attn = adam_pair(
        "adam_attn",
        attn.result(),
        (attend, attend_first, attend_second),
        (heads_out, heads_out_first, heads_out_second),
        False,
    )
    new_shrink = adam_single("adam_shrink", early_out.result(), shrinks, True, 0, new_late[3:])
    red_in = tail.result()
    new_expand = adam_single("adam_expand", red_in, expands, False, 0, new_late[:3])
    red_small = red_in[4 * er :].reshape(-1)[:small_size].reshape(tiny_rows, dr).astype(f32)
    new_taps = adam_update(depthwise, depthwise_first, depthwise_second, red_small[:TAPS], decay_rate)
    red_norms = red_small[TAPS:]
    new_norms = moments_only(norm_table_first, norm_table_second, red_norms)
    return (
        layer_output,
        frames_grad,
        *new_expand,
        *new_shrink,
        *new_attn,
        *new_conv,
        *new_taps,
        red_norms,
        *new_norms,
    )


def solution(mesh):
    return jax.shard_map(
        per_device,
        mesh=mesh,
        in_specs=(
            P(("dp", "fsdp"), None),
            P(("dp", "fsdp"), None),
            P(("dp", "fsdp"), None),
            P(None, "fsdp", None),
            P(None, "fsdp", None),
            P(None, "fsdp", None),
            P(None, "fsdp", None),
            P(None, "fsdp", None),
            P(None, "fsdp", None),
            P("fsdp", None),
            P("fsdp", None),
            P("fsdp", None),
            P("fsdp", None),
            P("fsdp", None),
            P("fsdp", None),
            P("fsdp", None),
            P("fsdp", None),
            P("fsdp", None),
            P("fsdp", None),
            P("fsdp", None),
            P("fsdp", None),
            P(None, "fsdp"),
            P(None, "fsdp"),
            P(None, "fsdp"),
            P(None, "fsdp"),
            P(None, "fsdp"),
            P(None, "fsdp"),
        ),
        out_specs=(
            P(("dp", "fsdp"), None),
            P(("dp", "fsdp"), None),
            P(None, "fsdp", None),
            P(None, "fsdp", None),
            P(None, "fsdp", None),
            P(None, "fsdp", None),
            P(None, "fsdp", None),
            P(None, "fsdp", None),
            P("fsdp", None),
            P("fsdp", None),
            P("fsdp", None),
            P("fsdp", None),
            P("fsdp", None),
            P("fsdp", None),
            P("fsdp", None),
            P("fsdp", None),
            P("fsdp", None),
            P("fsdp", None),
            P("fsdp", None),
            P("fsdp", None),
            P(None, "fsdp"),
            P(None, "fsdp"),
            P(None, "fsdp"),
            P(None, "fsdp"),
            P(None, "fsdp"),
            P(None, "fsdp"),
        ),
        check_vma=False,
    )
```

```python
import functools
import math

import jax
import jax.numpy as jnp
from jax import lax
from jax.experimental import pallas as pl
from jax.experimental.pallas import tpu as pltpu
from jax.sharding import PartitionSpec as P

HEADS = 8
STEP = 10
TAPS = 32
GAP = 16
LIMIT = 48 * 1024 * 1024
TILE = 256
WINDOWS = (512, 768)
BIG_TILE = 512
BIG = ("ff_forward", "norm_feed_forward_and_back")

norm_epsilon = 1e-05
batch_epsilon = 1e-05
masked_score = -1000000000.0
learn_rate = 0.1
beta_first = 0.9
beta_second = 0.98
adam_epsilon = 1e-08
decay_rate = 0.01

f32, bf16 = jnp.float32, jnp.bfloat16


def mm(a, b):
    return jnp.dot(a, b, preferred_element_type=f32)


def mm_nt(a, b):
    return lax.dot_general(a, b, (((1,), (1,)), ((), ())), preferred_element_type=f32)


def mm_tn(a, b):
    return lax.dot_general(a, b, (((0,), (0,)), ((), ())), preferred_element_type=f32)


def normalize(value):
    center = value - jnp.mean(value, axis=-1, keepdims=True)
    scale = lax.rsqrt(jnp.mean(center * center, axis=-1, keepdims=True) + norm_epsilon)
    return center * scale, scale


def norm_back(grad_out, gain, normed, scale):
    grad_norm = grad_out * gain
    return scale * (
        grad_norm
        - jnp.mean(grad_norm, axis=-1, keepdims=True)
        - normed * jnp.mean(grad_norm * normed, axis=-1, keepdims=True)
    )


def col_sum(value):
    return jnp.sum(value, axis=0, keepdims=True)


def sigmoid(value):
    return 0.5 * jnp.tanh(0.5 * value) + 0.5


def slope_of(value, sigma):
    return sigma * (1.0 + value * (1.0 - sigma))


def seg_of(places, ends):
    s = (places >= ends[0]).astype(jnp.int32)
    for j in range(1, 4):
        s = s + (places >= ends[j]).astype(jnp.int32)
    return s


def pick_last(values, count):
    out = values[0]
    for j in range(1, len(values)):
        out = jnp.where(count >= j, values[j], out)
    return out


def key_range(first, last, ends, rows):
    starts = [jnp.int32(0)] + ends
    stops = ends + [jnp.int32(rows)]
    return pick_last(starts, seg_of(first, ends)), pick_last(stops, seg_of(last, ends))


def in_window(lo, hi, rows, body):
    begin = (lo // 128) * 128
    done = jnp.bool_(False)
    for w in sorted({w for w in WINDOWS if w < rows} | {rows}):
        start = jnp.minimum(begin, rows - w)
        fits = jnp.logical_and(hi <= start + w, jnp.logical_not(done))

        @pl.when(fits)
        def _(start=start, w=w):
            body(pl.multiple_of(start, 128), w)

        done = jnp.logical_or(done, fits)


def partner(x):
    lane = lax.broadcasted_iota(jnp.int32, (1, 128), 1)
    return jnp.where((lane & 32) == 0, pltpu.roll(x, 96, 1), pltpu.roll(x, 32, 1))


def load_once(t, copies, sems):
    made = [pltpu.make_async_copy(s, d, sems.at[k]) for k, (s, d) in enumerate(copies)]

    @pl.when(t == 0)
    def _():
        for copy in made:
            copy.start()

    def ready(first=0, last=None):
        @pl.when(t == 0)
        def _():
            for copy in made[first:last]:
                copy.wait()

    return ready


def column_blocks(piece, owner, dst, rows, base=0):
    return [
        (
            piece.at[base + rows * j : base + rows * (j + 1), :],
            dst.at[pl.ds(owner * rows, rows), 512 * j : 512 * (j + 1)],
        )
        for j in range(dst.shape[1] // 512)
    ]


def row_block(piece, owner, dst, rows, base=0):
    return [(piece.at[base : base + rows, :], dst.at[pl.ds(owner * rows, rows), :])]


def row_spec(width):
    return "row"


def whole(*shape):
    return "whole"


def anywhere(count):
    return ["any"] * count


def out_shape(*shape, dtype=f32):
    return jax.ShapeDtypeStruct(shape, dtype)


def view(ref, kind, t):
    if kind == "row":
        return ref.at[pl.ds(pl.multiple_of(t * TILE, TILE), TILE), :]
    if kind == "col":
        return ref.at[:, pl.ds(pl.multiple_of(t * TILE, TILE), TILE)]
    if isinstance(kind, tuple):
        width = kind[1]
        return ref.at[:, pl.ds(pl.multiple_of(t * width, width), width)]
    return ref


def block_of(kind, shape, tile):
    if kind == "any":
        return pl.BlockSpec(memory_space=pl.ANY)
    if kind == "row":
        return pl.BlockSpec((tile, shape[1]), lambda i, *_: (i, 0))
    if kind == "col":
        return pl.BlockSpec((shape[0], tile), lambda i, *_: (0, i))
    if isinstance(kind, tuple) and kind[0] == "lane":
        return pl.BlockSpec((shape[0], kind[1]), lambda i, *_: (0, i))
    if isinstance(kind, tuple) and kind[0] == "cut":
        _, dim, width, at = kind
        block = (shape[0], width) if dim else (width, shape[1])
        return pl.BlockSpec(block, lambda i, *_: (0, at) if dim else (at, 0))
    if isinstance(kind, tuple):
        return pl.BlockSpec((None,) + shape[1:], lambda i, *_: (kind[1],) + (0,) * (len(shape) - 1))
    return pl.BlockSpec(shape, lambda i, *_: (0,) * len(shape))


def run(
    body, name, scalars, inputs, in_specs, out_specs, outs, scratch, grid, flops, count=0, piped=False
):
    tile = BIG_TILE if name in BIG else TILE
    size = sum(math.prod(o.shape) * o.dtype.itemsize for o in outs)
    size += sum(math.prod(o.shape) * o.dtype.itemsize for o in inputs)
    lead = len(scalars)
    cost = pl.CostEstimate(flops=int(flops), bytes_accessed=int(size), transcendentals=int(count))
    params = pltpu.CompilerParams(vmem_limit_bytes=LIMIT)
    if piped or (grid[0] > 1 and not name.startswith("weight_grad")):
        inputs = [pltpu.with_memory_space_constraint(v, pltpu.HBM) for v in inputs]
        outs = [pltpu.HBM(v.shape, v.dtype) for v in outs]
        return pl.pallas_call(
            lambda *refs: body(pl.program_id(0), *refs),
            grid_spec=pltpu.PrefetchScalarGridSpec(
                num_scalar_prefetch=lead,
                grid=grid,
                in_specs=[block_of(k, v.shape, tile) for k, v in zip(in_specs, inputs)],
                out_specs=[block_of(k, v.shape, tile) for k, v in zip(out_specs, outs)],
                scratch_shapes=scratch,
            ),
            out_shape=outs,
            cost_estimate=cost,
            compiler_params=params,
            name=name,
        )(*scalars, *inputs)
    kinds = list(in_specs) + list(out_specs)

    def kernel(*refs):
        held = refs[lead : lead + len(kinds)]
        rest = refs[lead + len(kinds) :]

        def step(t, carry):
            views = [view(ref, kind, t) for ref, kind in zip(held, kinds)]
            body(t, *refs[:lead], *views, *rest)
            return carry

        if grid[0] == 1:
            step(0, 0)
        else:
            lax.fori_loop(0, grid[0], step, 0)

    vmem = pl.BlockSpec(memory_space=pltpu.VMEM)
    place = lambda kind: pl.BlockSpec(memory_space=pl.ANY) if kind == "any" else vmem
    return pl.pallas_call(
        kernel,
        in_specs=[pl.BlockSpec(memory_space=pltpu.SMEM)] * lead + [place(k) for k in in_specs],
        out_specs=[vmem] * len(outs),
        out_shape=outs,
        scratch_shapes=scratch,
        cost_estimate=cost,
        compiler_params=params,
        name=name,
    )(*scalars, *inputs)


def ff_forward_body(t, me, x, norms, *refs, rel, er, sr):
    n = len(rel)
    parts = refs[:n]
    x1, hidden, before, active, w_in, w_out, sems = refs[n:]
    copies, later = [], []
    for k, r in enumerate(rel):
        copies += column_blocks(parts[k], me[0] ^ r, w_in, er)
        later += row_block(parts[k], me[0] ^ r, w_out, sr, 4 * er)
    split = len(copies)
    copies += later
    ready = load_once(t, copies, sems)
    value = x[...].astype(f32)
    normed, _ = normalize(value)
    h = (normed * norms[0:1, :] + norms[1:2, :]).astype(bf16)
    hidden[...] = h
    ready(0, split)
    total = None
    for j in range(w_in.shape[1] // 512):
        cols = slice(512 * j, 512 * (j + 1))
        a = mm(h, w_in[:, cols])
        s = (a * sigmoid(a)).astype(bf16)
        before[:, cols] = a.astype(bf16)
        active[:, cols] = s
        if j == 0:
            ready(split)
        part = mm(s, w_out[cols, :])
        total = part if total is None else total + part
    x1[...] = value + 0.5 * total


def ff_forward(me, x, norms, parts, rel):
    rows, d = x.shape
    er, sr = d // len(rel), 4 * d // len(rel)
    ff = sr * len(rel)
    return run(
        functools.partial(ff_forward_body, rel=rel, er=er, sr=sr),
        "ff_forward",
        (me,),
        (x, norms, *parts),
        [row_spec(d), whole(*norms.shape)] + anywhere(len(rel)),
        [row_spec(d), row_spec(d), row_spec(ff), row_spec(ff)],
        [
            out_shape(rows, d),
            out_shape(rows, d, dtype=bf16),
            out_shape(rows, ff, dtype=bf16),
            out_shape(rows, ff, dtype=bf16),
        ],
        [pltpu.VMEM((d, ff), bf16), pltpu.VMEM((ff, d), bf16), pltpu.SemaphoreType.DMA((5 * len(rel),))],
        (rows // BIG_TILE,),
        4 * rows * d * ff,
        rows * ff,
        True,
    )


def qkv_body(t, me, x1, norms, cs, sn, *refs, rel, ar):
    n = len(rel)
    parts = refs[:n]
    hidden, q, k, v, kt, w, sems = refs[n:]
    copies = []
    for j, r in enumerate(rel):
        copies += column_blocks(parts[j], me[0] ^ r, w, ar)
    ready = load_once(t, copies, sems)
    normed, _ = normalize(x1[...])
    h = (normed * norms[2:3, :] + norms[3:4, :]).astype(bf16)
    hidden[...] = h
    ready()
    c, s = cs[...], sn[...]
    for p in range(4):
        cols = slice(128 * p, 128 * (p + 1))
        a = mm(h, w[:, 128 * p : 128 * (p + 1)])
        q[:, cols] = ((a * c + partner(a) * s).astype(bf16) * 0.125).astype(bf16)
        a = mm(h, w[:, 512 + 128 * p : 512 + 128 * (p + 1)])
        turned = (a * c + partner(a) * s).astype(bf16)
        k[:, cols] = turned
        kt[cols, :] = turned.T
    v[...] = mm(h, w[:, 1024:1536]).astype(bf16)


def qkv(me, x1, norms, cs, sn, parts, rel):
    rows, d = x1.shape
    ar = parts[0].shape[0] // 4
    half = lambda: out_shape(rows, d, dtype=bf16)
    return run(
        functools.partial(qkv_body, rel=rel, ar=ar),
        "query_key_value",
        (me,),
        (x1, norms, cs, sn, *parts),
        [row_spec(d), whole(*norms.shape), row_spec(128), row_spec(128)] + anywhere(len(rel)),
        [row_spec(d)] * 4 + ["col"],
        [half(), half(), half(), half(), out_shape(d, rows, dtype=bf16)],
        [pltpu.VMEM((d, 3 * d), bf16), pltpu.SemaphoreType.DMA((3 * len(rel),))],
        (rows // TILE,),
        6 * rows * d * d,
    )


def attention_body(t, ends, me, q, k, v, x1, *refs, rel, ar, rows):
    n = len(rel)
    parts = refs[:n]
    x2, mixed, lse, w, sems = refs[n:]
    copies = []
    for j, r in enumerate(rel):
        copies += row_block(parts[j], me[0] ^ r, w, ar, 3 * ar)
    ready = load_once(t, copies, sems)
    e = [ends[j] for j in range(4)]
    first = t * TILE
    lo, hi = key_range(first, first + TILE - 1, e, rows)
    sq = seg_of(first + lax.broadcasted_iota(jnp.int32, (1, TILE), 1), e)
    low = lax.broadcasted_iota(jnp.int32, (1, 128), 1) < 64
    zero = jnp.zeros((), bf16)

    def body(start, w_keys):
        keys = pl.ds(start, w_keys)
        same = seg_of(start + lax.broadcasted_iota(jnp.int32, (w_keys, 1), 0), e) == sq

        def pair(p, carry):
            cols = pl.ds(pl.multiple_of(128 * p, 128), 128)
            qp, kp, vp = q[:, cols], k[keys, cols], v[keys, cols]
            both = None
            for h in range(2):
                head = 2 * p + h
                pick = low if h == 0 else jnp.logical_not(low)
                s = jnp.where(same, mm_nt(kp, jnp.where(pick, qp, zero)), masked_score)
                top = jnp.max(s, axis=0, keepdims=True)
                expo = jnp.exp(s - top)
                total = col_sum(expo)
                lse[pl.ds(head, 1), :] = top + jnp.log(total)
                prob = (expo * (1.0 / total)).astype(bf16)
                part = mm_tn(prob, jnp.where(pick, vp, zero))
                both = part if both is None else both + part
            mixed[:, cols] = both.astype(bf16)
            return carry

        lax.fori_loop(0, 4, pair, 0, unroll=2)

    in_window(lo, hi, rows, body)
    ready()
    x2[...] = x1[...] + mm(mixed[...], w[...])


def attention(ends, me, q, k, v, x1, parts, rel):
    rows, d = q.shape
    ar = parts[0].shape[0] // 4
    return run(
        functools.partial(attention_body, rel=rel, ar=ar, rows=rows),
        "attention_forward",
        (ends, me),
        (q, k, v, x1, *parts),
        [row_spec(d), whole(rows, d), whole(rows, d), row_spec(d)] + anywhere(len(rel)),
        [row_spec(d), row_spec(d), "col"],
        [out_shape(rows, d), out_shape(rows, d, dtype=bf16), out_shape(HEADS, rows)],
        [pltpu.VMEM((d, d), bf16), pltpu.SemaphoreType.DMA((len(rel),))],
        (rows // TILE,),
        16 * rows * rows * d // 4,
        HEADS * rows * rows,
    )


def attention_back_body(t, ends, q, k, kt, v, do, lse, delta, cs, sn, gp, dqt, *, rows, pairs, base):
    e = [ends[j] for j in range(4)]
    first = pl.multiple_of(t * TILE, TILE)
    lo, hi = key_range(first, first + TILE - 1, e, rows)
    sk = seg_of(first + lax.broadcasted_iota(jnp.int32, (TILE, 1), 0), e)
    low = lax.broadcasted_iota(jnp.int32, (1, 128), 1) < 64
    here = pl.ds(first, TILE)
    zero = jnp.zeros((), bf16)

    @pl.when(t == 0)
    def _():
        dqt[...] = jnp.zeros_like(dqt)

    def body(start, w):
        qs = pl.ds(start, w)
        same = sk == seg_of(start + lax.broadcasted_iota(jnp.int32, (1, w), 1), e)

        def pair(p, carry):
            held = pl.ds(pl.multiple_of(128 * p, 128), 128)
            qp, dop = q[qs, held], do[qs, held]
            kp, vp = k[here, held], v[here, held]
            gk, gv = None, None
            for h in range(2):
                head = 2 * p + h
                full = 2 * base + head
                pick = low if h == 0 else jnp.logical_not(low)
                qm, dom = jnp.where(pick, qp, zero), jnp.where(pick, dop, zero)
                hr = pl.ds(pl.multiple_of(64 * head, 64), 64)
                expo = jnp.exp(mm_nt(kp, qm) - lse[pl.ds(full, 1), qs])
                prob = jnp.where(same, expo, 0.0)
                ds = (prob * (mm_nt(vp, dom) - delta[pl.ds(full, 1), qs])).astype(bf16)
                v_part = mm(prob.astype(bf16), dom)
                k_part = mm(ds, qm)
                dqt[hr, qs] += mm(kt[hr, here], ds)
                gv = v_part if gv is None else gv + v_part
                gk = k_part if gk is None else gk + k_part
            c, s = cs[here, :], sn[here, :]
            gp[here, pl.ds(pl.multiple_of(128 * (2 * pairs + p), 128), 128)] = gv.astype(bf16)
            turned = gk * c - partner(gk) * s
            gp[here, pl.ds(pl.multiple_of(128 * (pairs + p), 128), 128)] = turned.astype(bf16)
            return carry

        lax.fori_loop(0, pairs, pair, 0, unroll=2)

    in_window(lo, hi, rows, body)

    @pl.when(t == rows // TILE - 1)
    def _():
        c, s = cs[...] * 0.125, sn[...] * 0.125
        for p in range(pairs):
            cols = slice(128 * p, 128 * (p + 1))
            g = dqt[cols, :].T
            gp[:, cols] = (g * c - partner(g) * s).astype(bf16)


def attention_back(ends, q, k, kt, v, do, lse, delta, cs, sn, base, pairs):
    rows, d = q.shape
    wide, at = 128 * pairs, base // pairs
    return run(
        functools.partial(attention_back_body, rows=rows, pairs=pairs, base=base),
        "attention_backward",
        (ends,),
        (q, k, kt, v, do, lse, delta, cs, sn),
        [("cut", 1, wide, at)] * 2
        + [("cut", 0, wide, at)]
        + [("cut", 1, wide, at)] * 2
        + [whole(HEADS, rows)] * 2
        + [whole(rows, 128)] * 2,
        [whole(rows, 3 * wide)],
        [out_shape(rows, 3 * wide, dtype=bf16)],
        [pltpu.VMEM((wide, rows), f32)],
        (rows // TILE,),
        10 * rows * rows * d * pairs // 4,
        HEADS * rows * rows * pairs // 4,
    )[0]


def spaced_rows(rows):
    return rows + 6 * GAP


def group_segments(row, ends):
    return seg_of(row + lax.broadcasted_iota(jnp.int32, (8, 128), 0), ends)


def spread_all(groups, first, spans, ends, read, buf):
    def put(s, row, seg, values):
        at = pl.ds(pl.multiple_of(GAP + GAP * s + row, 8), 8)
        keep = seg == s
        for c in range(4):
            buf[c, at, :] = jnp.where(keep, values[c], 0.0)

    def one(g, carry):
        row = 8 * (first + g)
        seg = group_segments(row, ends)
        values = read(g)
        put(spans[0, first + g], row, seg, values)
        put(spans[1, first + g], row, seg, values)
        return carry

    lax.fori_loop(0, groups, one, 0, unroll=4)

    @pl.when(spans[2, 0] > 1)
    def _():
        def rest(g, carry):
            row = 8 * (first + g)
            seg = group_segments(row, ends)
            values = read(g)

            def fix(s, inner):
                put(s, row, seg, values)
                return inner

            return lax.fori_loop(spans[0, first + g] + 1, spans[1, first + g], fix, carry)

        lax.fori_loop(0, groups, rest, 0)


def collect_all(groups, first, spans, ends, buf, out):
    def one(g, carry):
        row = 8 * (first + g)
        seg = group_segments(row, ends)
        lo, hi = spans[0, first + g], spans[1, first + g]
        keep = seg == lo
        a = pl.ds(pl.multiple_of(GAP + GAP * lo + row, 8), 8)
        b = pl.ds(pl.multiple_of(GAP + GAP * hi + row, 8), 8)
        to = pl.ds(pl.multiple_of(8 * g, 8), 8)
        for c in range(4):
            out[to, 128 * c : 128 * (c + 1)] = jnp.where(keep, buf[c, a, :], buf[c, b, :])
        return carry

    lax.fori_loop(0, groups, one, 0, unroll=4)

    @pl.when(spans[2, 0] > 1)
    def _():
        def rest(g, carry):
            row = 8 * (first + g)
            seg = group_segments(row, ends)
            to = pl.ds(pl.multiple_of(8 * g, 8), 8)

            def fix(s, inner):
                a = pl.ds(pl.multiple_of(GAP + GAP * s + row, 8), 8)
                for c in range(4):
                    cols = slice(128 * c, 128 * (c + 1))
                    out[to, cols] = jnp.where(seg == s, buf[c, a, :], out[to, cols])
                return inner

            return lax.fori_loop(spans[0, first + g] + 1, spans[1, first + g], fix, carry)

        lax.fori_loop(0, groups, rest, 0)


CHUNK = 8


def slide(src, taps, dst, rows, shift, reverse):
    span = 8 * CHUNK

    def step(i, carry):
        c = i // ((rows + 4 * GAP) // span)
        base = pl.multiple_of((i - c * ((rows + 4 * GAP) // span)) * span, 8)
        acc = [jnp.zeros((8, 128), f32) for _ in range(CHUNK)]
        for b in range(8):
            loads = [
                src[c, pl.ds(base + (shift + b + 8 * m), 8), :] for m in range(CHUNK + 3)
            ]
            for a in range(4):
                j = 8 * a + b
                j = TAPS - 1 - j if reverse else j
                w = jnp.broadcast_to(taps[c, j : j + 1, :], (8, 128))
                for m in range(CHUNK):
                    acc[m] = acc[m] + w * loads[m + a]
        for m in range(CHUNK):
            dst[c, pl.ds(base + GAP + 8 * m, 8), :] = acc[m]
        return carry

    lax.fori_loop(0, 4 * ((rows + 4 * GAP) // span), step, 0)


def tap_sums(grad, src, out, rows):
    span = 8 * CHUNK

    def lanes(c, carry):
        def step(i, acc):
            acc = list(acc)
            base = pl.multiple_of(i * span, 8)
            g = [grad[c, pl.ds(base + GAP + 8 * m, 8), :] for m in range(CHUNK)]
            for b in range(8):
                loads = [src[c, pl.ds(base + (b + 8 * m), 8), :] for m in range(CHUNK + 3)]
                for a in range(4):
                    j = 8 * a + b
                    for m in range(CHUNK):
                        acc[j] = acc[j] + g[m] * loads[m + a]
            return tuple(acc)

        zeros = tuple(jnp.zeros((8, 128), f32) for _ in range(TAPS))
        acc = lax.fori_loop(0, (rows + 4 * GAP) // span, step, zeros)
        for j in range(TAPS):
            out[c, j : j + 1, :] = col_sum(acc[j])
        return carry

    lax.fori_loop(0, 4, lanes, 0)


def conv_front_body(t, ends, me, spans, x2, norms, taps, *refs, rel, ar, rows):
    n = len(rel)
    parts = refs[:n]
    hidden, gates_out, conv, spaced, stats, glu, answer, w, sems = refs[n:]
    copies = []
    for j, r in enumerate(rel):
        copies += column_blocks(parts[j], me[0] ^ r, w, ar)
    ready = load_once(t, copies, sems)
    e = [ends[j] for j in range(4)]

    @pl.when(t == 0)
    def _():
        spaced[...] = jnp.zeros_like(spaced)

    normed, _ = normalize(x2[...])
    h = (normed * norms[4:5, :] + norms[5:6, :]).astype(bf16)
    hidden[...] = h
    ready()
    half = mm(h, w[:, :512])
    gate = mm(h, w[:, 512:])
    gates_out[:, :512] = half.astype(bf16)
    gates_out[:, 512:] = gate.astype(bf16)
    glu[...] = half * sigmoid(gate)

    def read(g):
        at = pl.ds(pl.multiple_of(8 * g, 8), 8)
        return [glu[at, 128 * c : 128 * (c + 1)] for c in range(4)]

    spread_all(TILE // 8, t * (TILE // 8), spans, e, read, spaced)

    @pl.when(t == rows // TILE - 1)
    def _():
        slide(spaced, taps, answer, rows, 0, False)
        collect_all(rows // 8, 0, spans, e, answer, conv)
        keep = lax.broadcasted_iota(jnp.int32, (rows, 1), 0) < e[3]
        kept = jnp.where(keep, conv[...], 0.0)
        stats[0:1, :] = col_sum(kept)
        stats[1:2, :] = col_sum(kept * kept)
        stats[2:3, :] = jnp.full((1, 512), e[3], jnp.int32).astype(f32)


def conv_front(ends, me, spans, x2, norms, taps, parts, rel):
    rows, d = x2.shape
    ar = parts[0].shape[0] // 3
    far = spaced_rows(rows)
    return run(
        functools.partial(conv_front_body, rel=rel, ar=ar, rows=rows),
        "gated_convolution",
        (ends, me, spans),
        (x2, norms, taps, *parts),
        [row_spec(d), whole(*norms.shape), whole(4, TAPS, 128)] + anywhere(len(rel)),
        [row_spec(d), row_spec(2 * d), whole(rows, d), whole(4, far, 128), whole(3, d)],
        [
            out_shape(rows, d, dtype=bf16),
            out_shape(rows, 2 * d, dtype=bf16),
            out_shape(rows, d),
            out_shape(4, far, 128),
            out_shape(3, d),
        ],
        [
            pltpu.VMEM((TILE, d), f32),
            pltpu.VMEM((4, far, 128), f32),
            pltpu.VMEM((d, 2 * d), bf16),
            pltpu.SemaphoreType.DMA((2 * len(rel),)),
        ],
        (rows // TILE,),
        8 * rows * d * d,
        rows * d,
    )


def conv_back_body(t, ends, spans, gz, conv, batch, totals, norms, taps, far, g_glu, tap_grad, grad, spaced, sem, *, rows):
    arriving = pltpu.make_async_copy(far, spaced, sem.at[0])
    arriving.start()
    e = [ends[j] for j in range(4)]
    grad[...] = jnp.zeros_like(grad)
    mean, scale, count = batch[0:1, :], batch[1:2, :], batch[2:3, :]
    bias_all = jnp.sum(totals[:, 0, :], axis=0, keepdims=True) / count
    gain_all = jnp.sum(totals[:, 1, :], axis=0, keepdims=True) / count
    factor = scale * norms[6:7, :]
    per = []
    for c in range(4):
        cols = slice(128 * c, 128 * (c + 1))
        per.append(
            [
                jnp.broadcast_to(v[:, cols], (8, 128))
                for v in (mean, scale, bias_all, gain_all, factor)
            ]
        )

    def read(g):
        row = pl.multiple_of(8 * g, 8)
        keep = row + lax.broadcasted_iota(jnp.int32, (8, 128), 0) < e[3]
        values = []
        for c in range(4):
            cols = slice(128 * c, 128 * (c + 1))
            m, s, b, k, f = per[c]
            zhat = (conv[pl.ds(row, 8), cols] - m) * s
            away = jnp.where(keep, b + zhat * k, 0.0)
            values.append(f * (gz[pl.ds(row, 8), cols] - away))
        return values

    spread_all(rows // 8, 0, spans, e, read, grad)
    slide(grad, taps, g_glu, rows, 1, True)
    arriving.wait()
    tap_sums(grad, spaced, tap_grad, rows)


def conv_back(ends, spans, gz, conv, batch, totals, norms, taps, spaced):
    rows, d = conv.shape
    far = spaced_rows(rows)
    return run(
        functools.partial(conv_back_body, rows=rows),
        "convolution_backward",
        (ends, spans),
        (gz, conv, batch, totals, norms, taps, spaced),
        [whole(rows, d), whole(rows, d), whole(3, d), whole(*totals.shape), whole(*norms.shape)]
        + [whole(4, TAPS, 128), "any"],
        [whole(4, far, 128), whole(4, TAPS, 128)],
        [out_shape(4, far, 128), out_shape(4, TAPS, 128)],
        [
            pltpu.VMEM((4, far, 128), f32),
            pltpu.VMEM((4, far, 128), f32),
            pltpu.SemaphoreType.DMA((1,)),
        ],
        (1,),
        12 * rows * d * TAPS * 40,
        rows * d,
    )


def gates_back_body(t, ends, me, spans, g_glu, norms, gates, x2, g3, mixed, *refs, rel, ar, rows):
    n = len(rel)
    parts, heads = refs[:n], refs[n : 2 * n]
    (g_gates, g2, g_attn, g_mixed, delta, sums) = refs[2 * n : 2 * n + 6]
    glu_rows, w, w_heads, sems = refs[2 * n + 6 :]
    copies = []
    for j, r in enumerate(rel):
        copies += column_blocks(parts[j], me[0] ^ r, w, ar)
        copies += row_block(heads[j], me[0] ^ r, w_heads, ar, 3 * ar)
    ready = load_once(t, copies, sems)
    e = [ends[j] for j in range(4)]

    @pl.when(t == 0)
    def _():
        sums[...] = jnp.zeros_like(sums)

    collect_all(TILE // 8, t * (TILE // 8), spans, e, g_glu, glu_rows)
    gg = glu_rows[...]
    sigma = sigmoid(gates[:, 512:].astype(f32))
    first = (gg * sigma).astype(bf16)
    second = (gg * gates[:, :512].astype(f32) * sigma * (1.0 - sigma)).astype(bf16)
    g_gates[:, :512] = first
    g_gates[:, 512:] = second
    ready()
    g_hidden = mm_nt(first, w[:, :512]) + mm_nt(second, w[:, 512:])
    normed, scale = normalize(x2[...])
    sums[0:1, :] += col_sum(g_hidden * normed)
    sums[1:2, :] += col_sum(g_hidden)
    out = g3[...] + norm_back(g_hidden, norms[4:5, :], normed, scale)
    g2[...] = out
    branch = out.astype(bf16)
    g_attn[...] = branch
    gm = mm_nt(branch, w_heads[...]).astype(bf16)
    g_mixed[...] = gm
    dots = gm.astype(f32) * mixed[...].astype(f32)
    upper = dots.astype(bf16)
    lower = (dots - upper.astype(f32)).astype(bf16)
    head = lax.broadcasted_iota(jnp.int32, (HEADS, 512), 0)
    ones = (lax.broadcasted_iota(jnp.int32, (HEADS, 512), 1) // 64 == head).astype(bf16)
    delta[...] = mm_nt(ones, upper) + mm_nt(ones, lower)


def gates_back(ends, me, spans, g_glu, norms, gates, x2, g3, mixed, parts, heads, rel):
    rows, d = x2.shape
    ar = parts[0].shape[0] // 3
    return run(
        functools.partial(gates_back_body, rel=rel, ar=ar, rows=rows),
        "gates_backward",
        (ends, me, spans),
        (g_glu, norms, gates, x2, g3, mixed, *parts, *heads),
        [whole(*g_glu.shape), whole(*norms.shape), row_spec(2 * d)]
        + [row_spec(d)] * 3
        + anywhere(2 * len(rel)),
        [row_spec(2 * d), row_spec(d), row_spec(d), row_spec(d)]
        + ["col", whole(2, d)],
        [
            out_shape(rows, 2 * d, dtype=bf16),
            out_shape(rows, d),
            out_shape(rows, d, dtype=bf16),
            out_shape(rows, d, dtype=bf16),
            out_shape(HEADS, rows),
            out_shape(2, d),
        ],
        [
            pltpu.VMEM((TILE, d), f32),
            pltpu.VMEM((d, 2 * d), bf16),
            pltpu.VMEM((d, d), bf16),
            pltpu.SemaphoreType.DMA((3 * len(rel),)),
        ],
        (rows // TILE,),
        6 * rows * d * d,
        rows * d,
    )


def rear_body(t, ends, me, conv, totals, x2, cot, norms, *refs, rel, ar, er, sr):
    n = len(rel)
    points, ffs = refs[:n], refs[n : 2 * n]
    (y, g_third, g_zed, wact, branch_out, hidden, active, g_before, g_out, sums, batch) = refs[2 * n : 2 * n + 11]
    w_point, w_in, w_out, slope, sems = refs[2 * n + 11 :]
    copies, later, last_ones = [], [], []
    for j, r in enumerate(rel):
        copies += row_block(points[j], me[0] ^ r, w_point, ar, 2 * ar)
        later += column_blocks(ffs[j], me[0] ^ r, w_in, er)
        last_ones += row_block(ffs[j], me[0] ^ r, w_out, sr, 4 * er)
    one, two = len(copies), len(copies) + len(later)
    copies += later + last_ones
    ready = load_once(t, copies, sems)

    @pl.when(t == 0)
    def _():
        sums[...] = jnp.zeros_like(sums)
        total = jnp.sum(totals[...], axis=0)
        count = total[2:3, :]
        mean = total[0:1, :] / count
        batch[0:1, :] = mean
        batch[1:2, :] = lax.rsqrt(total[1:2, :] / count - mean * mean + batch_epsilon)
        batch[2:3, :] = count

    zhat = (conv[...] - batch[0:1, :]) * batch[1:2, :]
    zed = zhat * norms[6:7, :] + norms[7:8, :]
    sigma = sigmoid(zed)
    wa = (zed * sigma).astype(bf16)
    wact[...] = wa
    zed_slope = slope_of(zed, sigma)
    ready(0, one)
    third = x2[...] + mm(wa, w_point[...])
    normed, scale = normalize(third)
    h = (normed * norms[8:9, :] + norms[9:10, :]).astype(bf16)
    hidden[...] = h
    ready(one, two)
    total = None
    for j in range(w_in.shape[1] // 512):
        cols = slice(512 * j, 512 * (j + 1))
        a = mm(h, w_in[:, cols])
        sg = sigmoid(a)
        s = (a * sg).astype(bf16)
        active[:, cols] = s
        slope[:, cols] = slope_of(a, sg)
        if j == 0:
            ready(two)
        part = mm(s, w_out[cols, :])
        total = part if total is None else total + part
    fourth = third + 0.5 * total
    last, last_scale = normalize(fourth)
    keep = t * BIG_TILE + lax.broadcasted_iota(jnp.int32, (BIG_TILE, 1), 0) < ends[3]
    y[...] = jnp.where(keep, last * norms[10:11, :] + norms[11:12, :], 0.0).astype(bf16)
    g_y = jnp.where(keep, cot[...].astype(f32), 0.0)
    sums[0:1, :] += col_sum(g_y * last)
    sums[1:2, :] += col_sum(g_y)
    g_fourth = norm_back(g_y, norms[10:11, :], last, last_scale)
    go = (0.5 * g_fourth).astype(bf16)
    g_out[...] = go
    g_hidden = None
    for j in range(w_in.shape[1] // 512):
        cols = slice(512 * j, 512 * (j + 1))
        gb = (mm_nt(go, w_out[cols, :]) * slope[:, cols]).astype(bf16)
        g_before[:, cols] = gb
        part = mm_nt(gb, w_in[:, cols])
        g_hidden = part if g_hidden is None else g_hidden + part
    sums[2:3, :] += col_sum(g_hidden * normed)
    sums[3:4, :] += col_sum(g_hidden)
    g3 = g_fourth + norm_back(g_hidden, norms[8:9, :], normed, scale)
    g_third[...] = g3
    branch = g3.astype(bf16)
    branch_out[...] = branch
    gz = mm_nt(branch, w_point[...]) * zed_slope
    g_zed[...] = gz
    sums[4:5, :] += col_sum(gz)
    sums[5:6, :] += col_sum(gz * zhat)


def rear(ends, me, conv, totals, x2, cot, norms, points, ffs, rel):
    rows, d = x2.shape
    ar = points[0].shape[0] // 3
    ff = 4 * d
    er, sr = d // len(rel), ff // len(rel)
    return run(
        functools.partial(rear_body, rel=rel, ar=ar, er=er, sr=sr),
        "norm_feed_forward_and_back",
        (ends, me),
        (conv, totals, x2, cot, norms, *points, *ffs),
        [row_spec(d), whole(*totals.shape), row_spec(d), row_spec(d), whole(*norms.shape)]
        + anywhere(2 * len(rel)),
        [row_spec(d)] * 6 + [row_spec(ff), row_spec(ff), row_spec(d), whole(6, d), whole(3, d)],
        [
            out_shape(rows, d, dtype=bf16),
            out_shape(rows, d),
            out_shape(rows, d),
            out_shape(rows, d, dtype=bf16),
            out_shape(rows, d, dtype=bf16),
            out_shape(rows, d, dtype=bf16),
            out_shape(rows, ff, dtype=bf16),
            out_shape(rows, ff, dtype=bf16),
            out_shape(rows, d, dtype=bf16),
            out_shape(6, d),
            out_shape(3, d),
        ],
        [
            pltpu.VMEM((d, d), bf16),
            pltpu.VMEM((d, ff), bf16),
            pltpu.VMEM((ff, d), bf16),
            pltpu.VMEM((BIG_TILE, ff), f32),
            pltpu.SemaphoreType.DMA((6 * len(rel),)),
        ],
        (rows // BIG_TILE,),
        rows * d * (8 * ff + 4 * d),
        rows * ff,
        True,
    )


def qkv_back_body(t, me, ga, gb, x1, g2, norms, *refs, rel, ar):
    n = len(rel)
    attn = refs[:n]
    g1, g_out, sums, w, sems = refs[n:]
    copies = []
    for j, r in enumerate(rel):
        copies += column_blocks(attn[j], me[0] ^ r, w, ar)
    ready = load_once(t, copies, sems)

    @pl.when(t == 0)
    def _():
        sums[...] = jnp.zeros_like(sums)

    normed, scale = normalize(x1[...])
    ready()
    g_hidden = None
    for z in range(3):
        for half, g in enumerate((ga, gb)):
            cols = slice(512 * z + 256 * half, 512 * z + 256 * (half + 1))
            part = mm_nt(g[:, 256 * z : 256 * (z + 1)], w[:, cols])
            g_hidden = part if g_hidden is None else g_hidden + part
    sums[0:1, :] += col_sum(g_hidden * normed)
    sums[1:2, :] += col_sum(g_hidden)
    out = g2[...] + norm_back(g_hidden, norms[2:3, :], normed, scale)
    g1[...] = out
    g_out[...] = (0.5 * out).astype(bf16)


def qkv_back(me, ga, gb, x1, g2, norms, attn, rel):
    rows, d = x1.shape
    ar = d // len(rel)
    return run(
        functools.partial(qkv_back_body, rel=rel, ar=ar),
        "query_key_value_backward",
        (me,),
        (ga, gb, x1, g2, norms, *attn),
        [row_spec(3 * d // 2)] * 2 + [row_spec(d)] * 2 + [whole(*norms.shape)] + anywhere(len(rel)),
        [row_spec(d), row_spec(d), whole(2, d)],
        [out_shape(rows, d), out_shape(rows, d, dtype=bf16), out_shape(2, d)],
        [pltpu.VMEM((d, 3 * d), bf16), pltpu.SemaphoreType.DMA((3 * len(rel),))],
        (rows // TILE,),
        6 * rows * d * d,
    )


def ff_back_body(t, me, g1, go, x, before, norms, qkv_sums, conv_sums, rear_sums, tap_grad, *refs, rel, er, sr, steps):
    n = len(rel)
    parts = refs[:n]
    g_frames, g_before, small, sums, w_in, w_out, sems = refs[n:]
    copies, later = [], []
    for j, r in enumerate(rel):
        copies += row_block(parts[j], me[0] ^ r, w_out, sr, 4 * er)
        later += column_blocks(parts[j], me[0] ^ r, w_in, er)
    split = len(copies)
    copies += later
    ready = load_once(t, copies, sems)

    @pl.when(t == 0)
    def _():
        sums[...] = jnp.zeros_like(sums)

    out = go[...]
    ready(0, split)
    g_hidden = None
    for j in range(w_in.shape[1] // 512):
        cols = slice(512 * j, 512 * (j + 1))
        a = before[:, cols].astype(f32)
        gb = (mm_nt(out, w_out[cols, :]) * slope_of(a, sigmoid(a))).astype(bf16)
        g_before[:, cols] = gb
        if j == 0:
            ready(split)
        part = mm_nt(gb, w_in[:, cols])
        g_hidden = part if g_hidden is None else g_hidden + part
    normed, scale = normalize(x[...].astype(f32))
    sums[0:1, :] += col_sum(g_hidden * normed)
    sums[1:2, :] += col_sum(g_hidden)
    g_frames[...] = g1[...] + norm_back(g_hidden, norms[0:1, :], normed, scale)

    @pl.when(t == steps - 1)
    def _():
        for c in range(tap_grad.shape[0]):
            small[:TAPS, 128 * c : 128 * (c + 1)] = tap_grad[c, :, :]
        rows = [sums[0:1, :], sums[1:2, :], qkv_sums[...], conv_sums[...], rear_sums[5:6, :]]
        rows += [rear_sums[4:5, :], rear_sums[2:4, :], rear_sums[0:2, :]]
        at = TAPS
        for row in rows:
            small[at : at + row.shape[0], :] = row
            at += row.shape[0]


def ff_back(me, g1, go, x, before, norms, sums, parts, rel):
    rows, d = x.shape
    ff = 4 * d
    er, sr = d // len(rel), ff // len(rel)
    return run(
        functools.partial(ff_back_body, rel=rel, er=er, sr=sr, steps=rows // TILE),
        "feed_forward_backward",
        (me,),
        (g1, go, x, before, norms, *sums, *parts),
        [row_spec(d), row_spec(d), row_spec(d), row_spec(ff), whole(*norms.shape)]
        + ["whole"] * len(sums)
        + anywhere(len(rel)),
        [row_spec(d), row_spec(ff), whole(TAPS + 12, d)],
        [out_shape(rows, d), out_shape(rows, ff, dtype=bf16), out_shape(TAPS + 12, d)],
        [
            pltpu.VMEM((2, d), f32),
            pltpu.VMEM((d, ff), bf16),
            pltpu.VMEM((ff, d), bf16),
            pltpu.SemaphoreType.DMA((5 * len(rel),)),
        ],
        (rows // TILE,),
        4 * rows * d * ff,
        rows * ff,
        True,
    )


def place_owners(me, tile, keep, send, base, height, owners, first):
    for k in range(owners):
        owner = first + k
        rows = tile[k * height : (k + 1) * height, :]
        mine = ((owner ^ me[0]) & 1) == 0

        @pl.when(mine)
        def _(rows=rows, owner=owner):
            keep[owner >> 1, pl.ds(base, height), :] = rows

        @pl.when(jnp.logical_not(mine))
        def _(rows=rows, owner=owner):
            send[owner >> 1, pl.ds(base, height), :] = rows


def weight_grad_body(t, me, *refs, fs, parts, n1, n2, extra):
    refs = list(refs)
    first = [refs.pop(0) for _ in range(1 + parts)] if n1 else None
    second = [refs.pop(0) for _ in range(2)] if n2 else None
    more = refs.pop(0) if extra else None
    keep, send = refs.pop(0), refs.pop(0)
    er = 512 // fs
    if n1:
        base = pl.multiple_of(t * er, er)
        tiles = [mm_tn(first[0][...], ref[...]).astype(bf16) for ref in first[1:]]
        tile = tiles[0] if parts == 1 else jnp.concatenate(tiles, axis=1)
        place_owners(me, tile, keep, send, base, er, fs, 0)
    if n2:
        sr = 512 * n2 // fs
        per = max(1, 512 // sr)

        def one(block):
            tile = mm_tn(second[0][...], second[1][...]).astype(bf16)
            place_owners(me, tile, keep, send, n1 * er, sr, per, block * per)

        if n1 in (0, n2):
            one(t)
        else:
            pl.when(t == 0)(lambda: one(0))
    if extra:

        @pl.when(t == 0)
        def _():
            tile = more[...].reshape(fs * extra, 512)
            place_owners(me, tile, keep, send, (n1 + n2) * er, extra, fs, 0)


def weight_grad(name, me, fs, first=None, second=None, more=None):
    inputs, specs = [], []
    n1 = n2 = parts = 0
    if first:
        h, gs = first
        rows, parts = h.shape[0], len(gs)
        wide = 512 // parts
        n1 = gs[0].shape[1] // wide
        inputs += [h, *gs]
        specs += [whole(rows, 512)] + [("lane", wide)] * parts
    if second:
        s, o = second
        rows = s.shape[0]
        n2 = s.shape[1] // 512
        inputs += [s, o]
        stepped = n1 in (0, n2)
        specs += [("lane", 512) if stepped else "whole", whole(rows, 512)]
    extra = 0
    if more is not None:
        extra = more.shape[1]
        inputs.append(more)
        specs.append("whole")
    height = (n1 + n2) * 512 // fs + extra
    return run(
        functools.partial(weight_grad_body, fs=fs, parts=parts, n1=n1, n2=n2, extra=extra),
        name,
        (me,),
        inputs,
        specs,
        [whole(fs // 2, height, 512)] * 2,
        [out_shape(fs // 2, height, 512, dtype=bf16)] * 2,
        [],
        (n1 or n2,),
        2 * rows * 512 * 512 * (n1 + n2),
        0,
        n1 == n2,
    )


def join(*pairs):
    return tuple(jnp.concatenate(list(side), axis=1) for side in zip(*pairs))


def bits_of(size):
    return int(size).bit_length() - 1


def swap(value, axis, size, mask):
    return lax.ppermute(value, axis, [(k, k ^ mask) for k in range(size)])


def relative(fs):
    rel = [0]
    for bit in reversed(range(bits_of(fs))):
        rel = rel + [r ^ (1 << bit) for r in rel]
    return tuple(rel)


def first_part(own, fs):
    parts = [own]
    for bit in reversed(range(1, bits_of(fs))):
        parts = parts + [swap(part, "fsdp", fs, 1 << bit) for part in parts]
    return parts


def second_part(parts, fs):
    return parts + [swap(part, "fsdp", fs, 1) for part in parts]


def sum_of(parts):
    total = parts[0].astype(f32)
    for part in parts[1:]:
        total = total + part.astype(f32)
    return total.astype(bf16)


class Chain:
    def __init__(self, pair, fs, dp):
        keep, send = pair
        self.fs, self.dp = fs, dp
        self.me, self.pack = lax.axis_index("fsdp"), lax.axis_index("dp")
        zero = jnp.int32(0)
        self.at, self.size = [zero, zero], list(keep.shape[:2])
        self.parts = [(keep, zero, zero)]
        self.stages = [("fsdp", bit, "halve") for bit in reversed(range(1, bits_of(fs)))]
        last = bits_of(dp) - 1
        self.stages += [("dp", bit, "halve") for bit in range(last)] + [("dp", last, "add")]
        self.stages += [("dp", bit, "join") for bit in reversed(range(last))]
        self.flight = swap(send, "fsdp", fs, 1)
        self.joining = None

    def take(self, y, r):
        shape = (self.size[0], self.size[1], 512)
        return sum_of(
            [lax.dynamic_slice(part, (y - y0, r - r0, 0), shape) for part, y0, r0 in self.parts]
        )

    def hold(self, *tokens):
        self.flight = after(self.flight, *tokens)

    def advance(self):
        if not self.stages:
            return None
        self.settle()
        axis, bit, kind = self.stages.pop(0)
        size, index = (self.fs, self.me) if axis == "fsdp" else (self.dp, self.pack)
        side = (index >> bit) & 1
        if kind == "halve":
            dim = 0 if axis == "fsdp" else 1
            base = self.at[dim]
            self.size[dim] //= 2
            self.at[dim] = base + (1 - side) * self.size[dim]
            send = self.take(*self.at)
            self.at[dim] = base + side * self.size[dim]
        else:
            if self.joining is None:
                send = self.take(*self.at)
            else:
                send = self.whole
            if kind == "join":
                send = send.reshape(-1, 512)
                self.whole, self.joining = send, side
            else:
                self.parts = [(send, *self.at)]
        self.flight = swap(send, axis, size, 1 << bit)
        return send

    def settle(self):
        if self.joining is None:
            self.parts.append((self.flight, *self.at))
        else:
            pair = [self.whole, self.flight]
            self.whole = jnp.where(
                self.joining == 0, jnp.concatenate(pair, axis=0), jnp.concatenate(pair[::-1], axis=0)
            )

    def result(self):
        while self.stages:
            self.advance()
        self.settle()
        return self.whole


def after(value, *tokens):
    tokens = [token for token in tokens if token is not None]
    return lax.optimization_barrier((value, *tokens))[0]


def from_everyone(rows):
    axes = ("dp", "fsdp")
    count = lax.axis_size(axes)
    spread = jnp.broadcast_to(rows[None], (count,) + rows.shape)
    return lax.all_to_all(spread, axes, 0, 0, tiled=True)


def to_rows(block):
    r, c = block.shape
    k = c // 512
    return block.reshape(r, k, 512).swapaxes(0, 1).reshape(k * r, 512)


def from_rows(rows, r, c):
    k = c // 512
    return rows.reshape(k, r, 512).swapaxes(0, 1).reshape(r, c)


def pack_body(t, a, b, out, *, n, er):
    for j in range(n):
        out[er * j : er * (j + 1), :] = a[:, 512 * j : 512 * (j + 1)].astype(bf16)
    out[er * n :, :] = b[...].astype(bf16)


def pack(name, a, b, index=None):
    er, n = a.shape[-2], a.shape[-1] // 512
    sr = b.shape[-2]
    return run(
        functools.partial(pack_body, n=n, er=er),
        name,
        (),
        (a, b),
        ["whole" if index is None else ("stack", index)] * 2,
        ["whole"],
        [out_shape(n * er + sr, 512, dtype=bf16)],
        [],
        (1,),
        er * n * 1024,
        0,
        True,
    )[0]


def adam_body(*refs):
    ga, gb = refs[0][...], refs[1][...]
    outs = refs[-6:]
    for ref, grad, to in ((refs[2:5], ga, outs[:3]), (refs[5:8], gb, outs[3:])):
        new = adam_update(ref[0][...], ref[1][...], ref[2][...], grad.astype(f32), decay_rate)
        for place, value in zip(to, new):
            place[...] = value


def adam_single_body(*refs):
    outs = refs[-3:]
    new = adam_update(refs[1][...], refs[2][...], refs[3][...], refs[0][...].astype(f32), decay_rate)
    for place, value in zip(outs, new):
        place[...] = value


def adam_single(name, grad, state, by_row, index, into):
    height, width = state[0].shape[-2:]
    n = 4
    block = (height // n, width) if by_row else (height, width // n)
    spec = pl.BlockSpec((None,) + block, lambda i: (index, i, 0) if by_row else (index, 0, i))
    return pl.pallas_call(
        adam_single_body,
        grid=(n,),
        in_specs=[pl.BlockSpec(block, lambda i: (i, 0))] + [spec] * 3 + [pl.BlockSpec(memory_space=pl.ANY)] * 3,
        out_specs=[spec] * 3,
        out_shape=[out_shape(*v.shape) for v in state],
        input_output_aliases={4 + j: j for j in range(3)},
        cost_estimate=pl.CostEstimate(
            flops=20 * height * width, bytes_accessed=26 * height * width, transcendentals=height * width
        ),
        compiler_params=pltpu.CompilerParams(vmem_limit_bytes=(8 if by_row else 48) * 1024 * 1024),
        name=name,
    )(grad, *state, *into)


def adam_pair(name, grad, first, second, steps, index=None, into=None):
    er, n = first[0].shape[-2], first[0].shape[-1] // 512
    sr = second[0].shape[-2]
    part = sr // n if steps else sr
    lead = () if index is None else (None,)
    at = () if index is None else (index,)
    spec_a = pl.BlockSpec(lead + (er, 512), lambda i: at + (0, i))
    spec_b = pl.BlockSpec(lead + (part, 512), lambda i: at + ((i, 0) if steps else (0, 0)))
    grad_a = pl.BlockSpec((er, 512), lambda i: (i, 0))
    grad_b = pl.BlockSpec((part, 512), lambda i: (n * er // part + (i if steps else 0), 0))
    inputs = [grad, grad, *first, *second]
    specs = [grad_a, grad_b] + [spec_a] * 3 + [spec_b] * 3
    alias = {}
    if into is not None:
        alias = {len(inputs) + j: j for j in range(6)}
        inputs += list(into)
        specs += [pl.BlockSpec(memory_space=pl.ANY)] * 6
    return pl.pallas_call(
        adam_body,
        grid=(n,),
        in_specs=specs,
        out_specs=[spec_a] * 3 + [spec_b] * 3,
        out_shape=[out_shape(*v.shape) for v in (*first, *second)],
        input_output_aliases=alias,
        cost_estimate=pl.CostEstimate(
            flops=20 * er * 512 * n, bytes_accessed=26 * (er * n + sr) * 512, transcendentals=er * 512 * n
        ),
        compiler_params=pltpu.CompilerParams(vmem_limit_bytes=8 * 1024 * 1024),
        name=name,
    )(*inputs)


def adam_update(master, first, second_block, grad, decay):
    first_new = beta_first * first + (1.0 - beta_first) * grad
    second_new = beta_second * second_block + (1.0 - beta_second) * grad * grad
    first_hat = first_new / (1.0 - beta_first**STEP)
    second_hat = second_new / (1.0 - beta_second**STEP)
    master_new = master - learn_rate * (
        first_hat / (jnp.sqrt(second_hat) + adam_epsilon) + decay * master
    )
    return (master_new, first_new, second_new)


def moments_only(first, second_block, grad):
    first_new = beta_first * first + (1.0 - beta_first) * grad
    second_new = beta_second * second_block + (1.0 - beta_second) * grad * grad
    return (first_new, second_new)


def rotary_tables(position, half):
    freq = jnp.exp(jnp.arange(half, dtype=f32) * (-math.log(10000.0) / half))
    angle = position.astype(f32)[:, None] * freq[None, :]
    cosine, sine = jnp.cos(angle), jnp.sin(angle)
    return (
        jnp.concatenate([cosine] * 4, axis=1),
        jnp.concatenate([-sine, sine, -sine, sine], axis=1),
    )


def per_device(
    frames,
    cotangent,
    lengths,
    expand,
    expand_first,
    expand_second,
    shrink,
    shrink_first,
    shrink_second,
    attend,
    attend_first,
    attend_second,
    heads_out,
    heads_out_first,
    heads_out_second,
    pointwise,
    pointwise_first,
    pointwise_second,
    pointwise_out,
    pointwise_out_first,
    pointwise_out_second,
    depthwise,
    depthwise_first,
    depthwise_second,
    norm_table,
    norm_table_first,
    norm_table_second,
):
    fs, dp = (lax.axis_size("fsdp"), lax.axis_size("dp"))
    rel = relative(fs)
    er, sr, ar = expand.shape[1], shrink.shape[1], attend.shape[0]
    dr = depthwise.shape[1]
    device = lax.axis_index("fsdp")
    me = device.astype(jnp.int32).reshape(1)
    ends = jnp.cumsum(lengths[0, :4]).astype(jnp.int32)
    rows, width = frames.shape

    early_own = pack("pack_early", expand, shrink, 0)
    ff_zero = first_part(early_own, fs)
    small = jnp.concatenate([after(depthwise, early_own), norm_table], axis=0).astype(bf16)
    tiny_rows = small.shape[0]
    small_parts = second_part(first_part(small, fs), fs)
    places = jnp.arange(rows, dtype=jnp.int32)
    segment = jnp.sum((places[:, None] >= ends[None, :]).astype(jnp.int32), axis=1)
    starts = jnp.concatenate([jnp.zeros((1,), jnp.int32), ends])
    pick = (segment[:, None] == jnp.arange(5, dtype=jnp.int32)[None, :]).astype(jnp.int32)
    position = places - jnp.sum(pick * starts[None, :], axis=1)
    lo, hi = segment[::8], segment[7::8]
    spans = jnp.stack([lo, hi, jnp.broadcast_to(jnp.max(hi - lo), lo.shape)])
    cs, sn = rotary_tables(position, width // HEADS // 2)

    attn_own = pack("pack_attn", attend, heads_out)
    conv_own = pack("pack_conv", pointwise, pointwise_out)
    late_own = pack("pack_late", expand, shrink, 1)
    small_full = jnp.zeros((fs, tiny_rows, dr), bf16)
    for k, r in enumerate(rel):
        small_full = lax.dynamic_update_slice_in_dim(small_full, small_parts[k][None], device ^ r, 0)
    small_full = small_full.swapaxes(0, 1).reshape(tiny_rows, fs * dr).astype(f32)
    norms = small_full[TAPS:]
    taps = small_full[:TAPS].reshape(TAPS, width // 128, 128).swapaxes(0, 1)
    ff_zero = [ff_zero[0]] + [after(part, attn_own, conv_own, late_own, cs, sn, norms, taps) for part in ff_zero[1:]]
    attn_parts = first_part(after(attn_own, *ff_zero), fs)
    ff_zero = second_part(ff_zero, fs)


    x1, hidden_zero, before_zero, active_zero = ff_forward(
        me, frames, norms, ff_zero, rel
    )
    attn_parts = [after(part, x1) for part in attn_parts]
    conv_parts = first_part(after(conv_own, *attn_parts), fs)
    attn_parts = second_part(attn_parts, fs)
    hidden_attn, q, k, v, kt = qkv(me, x1, norms, cs, sn, attn_parts, rel)
    conv_parts = [after(part, q) for part in conv_parts]
    ff_one = first_part(after(late_own, *conv_parts), fs)
    conv_parts = second_part(conv_parts, fs)
    x2, mixed, lse = attention(ends, me, after(q, *conv_parts), k, v, x1, attn_parts, rel)
    hidden_conv, gates, conv, spaced, stats = conv_front(ends, me, spans, x2, norms, taps, conv_parts, rel)
    ff_one = second_part([after(part, stats) for part in ff_one], fs)
    totals = from_everyone(stats)
    (
        layer_output,
        g_third,
        g_zed,
        wact,
        g_branch,
        hidden_one,
        active_one,
        g_before_one,
        g_out_one,
        rear_sums,
        batch,
    ) = rear(ends, me, conv, totals, x2, cotangent, norms, conv_parts, ff_one, rel)
    back_totals = from_everyone(rear_sums[4:6])
    late_pair = weight_grad(
        "weight_grad_late", me, fs, (hidden_one, (g_before_one,)), (active_one, g_out_one)
    )
    late = Chain((late_pair[0], after(late_pair[1], back_totals)), fs, dp)
    g_glu, tap_grad = conv_back(ends, spans, after(g_zed, late_pair[1]), conv, batch, back_totals, norms, taps, spaced)
    g_glu = after(g_glu, late.advance())
    g_gates, g_second, g_attn, g_mixed, delta, conv_sums = gates_back(
        ends, me, spans, g_glu, norms, gates, x2, g_third, mixed, conv_parts, attn_parts, rel
    )
    conv_pair = weight_grad("weight_grad_conv", me, fs, (hidden_conv, (g_gates,)), (wact, g_branch))
    middle = Chain(conv_pair, fs, dp)
    first_half = attention_back(
        ends, q, k, kt, v, after(g_mixed, conv_pair[1]), lse, delta, cs, sn, 0, 2
    )
    late.hold(first_half)
    middle.hold(first_half)
    tokens = (late.advance(), middle.advance(), first_half)
    second_half = attention_back(ends, q, k, kt, v, after(g_mixed, *tokens), lse, delta, cs, sn, 2, 2)
    late.hold(second_half)
    middle.hold(second_half)
    first_half = after(first_half, late.advance(), middle.advance())
    attn_pair = weight_grad(
        "weight_grad_attn", me, fs, (hidden_attn, (first_half, second_half)), (mixed, g_attn)
    )
    attn = Chain(attn_pair, fs, dp)
    g_first, g_out_zero, qkv_sums = qkv_back(
        me, after(first_half, attn_pair[1]), second_half, x1, g_second, norms, attn_parts, rel
    )
    for chain in (late, middle, attn):
        chain.hold(g_first)
    tokens = (late.advance(), middle.advance(), attn.advance())
    out_pair = weight_grad(
        "weight_grad_shrink", me, fs, None, (active_zero, after(g_out_zero, *tokens))
    )
    early_out = Chain(out_pair, fs, dp)
    middle.hold(out_pair[1])
    sums = (qkv_sums, conv_sums, rear_sums, tap_grad)
    frames_grad, g_before_zero, small_grad = ff_back(
        me,
        g_first,
        after(g_out_zero, out_pair[1], early_out.advance()),
        frames,
        before_zero,
        norms,
        sums,
        ff_zero,
        rel,
    )
    for chain in (late, middle, attn, early_out):
        chain.hold(g_before_zero)
    tokens = (attn.flight, early_out.flight, late.flight, middle.flight)
    small_grad = small_grad.astype(bf16).reshape(tiny_rows, fs, dr).swapaxes(0, 1)
    small_size = tiny_rows * dr
    small_pad = -small_size % (512 * 16)
    small_grad = jnp.pad(small_grad.reshape(fs, small_size), ((0, 0), (0, small_pad)))
    small_grad = small_grad.reshape(fs, -1, 512)
    tail_pair = weight_grad(
        "weight_grad_expand",
        me,
        fs,
        (hidden_zero, (after(g_before_zero, *tokens),)),
        None,
        small_grad,
    )
    tail = Chain(tail_pair, fs, dp)
    attn.hold(tail_pair[1])
    early_out.hold(tail_pair[1])
    tail_sent = tail.advance()
    expands = (expand, expand_first, expand_second)
    shrinks = (shrink, shrink_first, shrink_second)

    def hold(*chains):
        for chain in chains:
            chain.hold(tail_sent)

    hold(late, middle, attn, early_out)
    red_late, red_conv = late.result(), middle.result()
    new_late = adam_pair("adam_late", red_late, expands, shrinks, True, 1)
    new_conv = adam_pair(
        "adam_conv",
        red_conv,
        (pointwise, pointwise_first, pointwise_second),
        (pointwise_out, pointwise_out_first, pointwise_out_second),
        False,
    )
    new_attn = adam_pair(
        "adam_attn",
        attn.result(),
        (attend, attend_first, attend_second),
        (heads_out, heads_out_first, heads_out_second),
        False,
    )
    new_shrink = adam_single("adam_shrink", early_out.result(), shrinks, True, 0, new_late[3:])
    red_in = tail.result()
    new_expand = adam_single("adam_expand", red_in, expands, False, 0, new_late[:3])
    red_small = red_in[4 * er :].reshape(-1)[:small_size].reshape(tiny_rows, dr).astype(f32)
    new_taps = adam_update(depthwise, depthwise_first, depthwise_second, red_small[:TAPS], decay_rate)
    red_norms = red_small[TAPS:]
    new_norms = moments_only(norm_table_first, norm_table_second, red_norms)
    return (
        layer_output,
        frames_grad,
        *new_expand,
        *new_shrink,
        *new_attn,
        *new_conv,
        *new_taps,
        red_norms,
        *new_norms,
    )


def solution(mesh):
    return jax.shard_map(
        per_device,
        mesh=mesh,
        in_specs=(
            P(("dp", "fsdp"), None),
            P(("dp", "fsdp"), None),
            P(("dp", "fsdp"), None),
            P(None, "fsdp", None),
            P(None, "fsdp", None),
            P(None, "fsdp", None),
            P(None, "fsdp", None),
            P(None, "fsdp", None),
            P(None, "fsdp", None),
            P("fsdp", None),
            P("fsdp", None),
            P("fsdp", None),
            P("fsdp", None),
            P("fsdp", None),
            P("fsdp", None),
            P("fsdp", None),
            P("fsdp", None),
            P("fsdp", None),
            P("fsdp", None),
            P("fsdp", None),
            P("fsdp", None),
            P(None, "fsdp"),
            P(None, "fsdp"),
            P(None, "fsdp"),
            P(None, "fsdp"),
            P(None, "fsdp"),
            P(None, "fsdp"),
        ),
        out_specs=(
            P(("dp", "fsdp"), None),
            P(("dp", "fsdp"), None),
            P(None, "fsdp", None),
            P(None, "fsdp", None),
            P(None, "fsdp", None),
            P(None, "fsdp", None),
            P(None, "fsdp", None),
            P(None, "fsdp", None),
            P("fsdp", None),
            P("fsdp", None),
            P("fsdp", None),
            P("fsdp", None),
            P("fsdp", None),
            P("fsdp", None),
            P("fsdp", None),
            P("fsdp", None),
            P("fsdp", None),
            P("fsdp", None),
            P("fsdp", None),
            P("fsdp", None),
            P(None, "fsdp"),
            P(None, "fsdp"),
            P(None, "fsdp"),
            P(None, "fsdp"),
            P(None, "fsdp"),
            P(None, "fsdp"),
        ),
        check_vma=False,
    )
```
